32 devices in a mesh: row: 4 (over y, core), col: 8 (over z, x).
Axes of the slice: x: 2, y: 2, z: 4, core: 2. Of those that a mesh axis runs over, the one named last changes fastest.
Arguments:
- start_block: float32 [64, 65536], P(None, ('row', 'col')), may hold values from -6 to 6
- struct_blocks: bfloat16 [3, 512, 4, 128, 128], P(None, ('row', 'col'))
- block_ids: int32 [512, 4], P(('row', 'col')), may hold values from 0 to 17, as said below
- rim_rows: int32 [4096], P(('row', 'col')), may hold values from 0 to 2047, as said below
- wet_slots: int32 [32768], P(('row', 'col')), may hold values from 0 to 2047, as said below
- wet_counts: int32 [32], P(('row', 'col')), may hold values from 341 to 1024
- added_mass: bfloat16 [1024, 32768], P('col', 'row'), may hold values from -0.03125 to 0.03125
- coupling_rates: float32 [2], replicated, may hold values from 0.5 to 1.5
Outputs:
- lanczos_block: float32 [64, 65536], P(None, ('row', 'col'))
- coefficients: float32 [6, 3, 64, 64], replicated
The draws below stay inside these ranges and needn't reach their ends.
Inputs may be any that keep to these rules, and one draw needn't show every extreme that they name: `block_ids`: each block row's first entry is its own local block row; the first local block row names 2048//128 (rim of the shard before) as its second entry and the last names 17; entries may repeat. `rim_rows`: local indices into a shard's 2048 degrees of freedom, distinct within one shard. `wet_slots`: local indices into a shard's 2048 degrees of freedom, distinct within one shard.
All inputs are finite; a program needn't handle non-finite values.
Results may differ from the reference program's by a relative error of at most 0.023.
Values may be sent and summed in bfloat16 or wider, within the bound.
No kernel may reach another device: no remote copies, remote signals or barrier semaphores. Data moves between devices by JAX's collectives and lax.ppermute only.
A program may use at most 128 MiB of HBM per device.

```python
import jax
import jax.numpy as jnp
from jax import lax

VEC = 64
BS = 128
NNZ = 4
STEPS = 6
NS_DEV = 2048
WCAP = 1024
WR = 32
NST = 65536
NB = 32768
NBR = 1024
N_ROW = 4
N_COL = 8
DEVICES = 32


def draw_struct_blocks(key, part):
    array_shape = (3, NST // BS, NNZ, BS, BS)
    values = jax.random.normal(key, array_shape, jnp.float32)
    values = values * (NNZ * BS) ** (-0.5)
    diagonal_mask = (jnp.arange(3) == 0)[:, None, None, None, None] & (jnp.arange(NNZ) == 0)[None, None, :, None, None] & jnp.eye(BS, dtype=bool)[None, None, None, :, :]
    return (values + 2.0 * diagonal_mask.astype(jnp.float32)).astype(jnp.bfloat16)


def draw_block_ids(key, part):
    row_count = NST // BS
    local_blocks = NS_DEV // BS
    own_block = jnp.arange(row_count, dtype=jnp.int32) % local_blocks
    random_ids = jax.random.randint(key, (row_count, NNZ - 1), 0, local_blocks + 2).astype(jnp.int32)
    second = jnp.where(own_block == 0, local_blocks, jnp.where(own_block == local_blocks - 1, local_blocks + 1, random_ids[:, 0]))
    return jnp.concatenate([own_block[:, None], second[:, None].astype(jnp.int32), random_ids[:, 1:]], 1).astype(jnp.int32)


def shard_lists(key, taken):
    shard_keys = jax.random.split(key, DEVICES)
    chosen = jax.vmap(lambda single: jax.random.permutation(single, NS_DEV)[:taken])(shard_keys)
    return chosen.reshape(-1).astype(jnp.int32)


def draw_rim_rows(key, part):
    return shard_lists(jax.random.fold_in(key, 11), BS)


def draw_wet_slots(key, part):
    return shard_lists(jax.random.fold_in(key, 23), WCAP)


def draw_wet_counts(key, part):
    counts = jax.random.randint(key, (DEVICES,), WCAP // 3, WCAP + 1).astype(jnp.int32)
    busiest = jax.random.randint(jax.random.fold_in(key, 1), (), 0, DEVICES)
    counts = counts.at[busiest].set(WCAP)
    counts = counts.at[(busiest + 1) % DEVICES].set(WCAP // 3)
    return counts.astype(jnp.int32)


def level_of(rng, dims, cuts, least, top_value):
    def one(dim, blocks):
        draws = jax.random.uniform(jax.random.fold_in(jax.random.fold_in(rng, 6), dim), (blocks,), jnp.float32, least / len(cuts), top_value / len(cuts))
        return jnp.repeat(jnp.exp(draws), dims[dim] // blocks).reshape((-1,) + (1,) * (len(dims) - dim - 1))

    loudness = one(*cuts[0])
    for cut in cuts[1:]:
        loudness = loudness * one(*cut)
    return loudness


def normal_values(key, shape, scale, most, cuts=(), kind=jnp.bfloat16):
    gain = level_of(key, shape, cuts, -0.22, 0.18) if cuts else 1.0
    values = jax.random.normal(key, shape, jnp.float32) * scale * gain
    return jnp.minimum(jnp.maximum(values, -most), most).astype(kind)


def setup_inputs(seed: int = 0) -> dict:
    keys = jax.random.split(jax.random.key(seed), 9)
    start_block = normal_values(keys[0], (VEC, NST), 1.0, 6.0, ((1, 32),), jnp.float32)
    struct_blocks = draw_struct_blocks(jax.random.fold_in(keys[8], 71), 0)
    block_ids = draw_block_ids(jax.random.fold_in(keys[8], 71), 0)
    rim_rows = draw_rim_rows(jax.random.fold_in(keys[8], 71), 0)
    wet_slots = draw_wet_slots(jax.random.fold_in(keys[8], 71), 0)
    wet_counts = draw_wet_counts(jax.random.fold_in(keys[8], 71), 0)
    added_mass = normal_values(keys[6], (NBR, NB), NB ** -0.5, 0.03125, ((0, 8), (1, 4)))
    coupling_rates = jnp.clip(jax.random.uniform(keys[7], (2,), jnp.float32, 0.5, 1.5), 0.5, 1.5)
    return dict(start_block=start_block, struct_blocks=struct_blocks, block_ids=block_ids, rim_rows=rim_rows, wet_slots=wet_slots, wet_counts=wet_counts, added_mass=added_mass, coupling_rates=coupling_rates)


def contract_rows(left, right):
    return lax.dot_general(left, right, (((1,), (1,)), ((), ())), precision=lax.Precision.HIGHEST)

def reference(start_block, struct_blocks, block_ids, rim_rows, wet_slots, wet_counts, added_mass, coupling_rates):
    shards = N_ROW * N_COL
    block_count = NS_DEV // BS
    total_rows = NS_DEV * shards
    blocks = struct_blocks.reshape(3, shards, block_count, NNZ, BS, BS)
    shard_ids = block_ids.reshape(shards, block_count, NNZ)
    rim_index = rim_rows.reshape(shards, BS)
    wet_index = wet_slots.reshape(shards, WCAP)
    live_slots = jnp.arange(WCAP)[None, :] < wet_counts[:, None]

    def operate(block_bf):
        by_shard = jnp.transpose(block_bf.reshape(VEC, shards, NS_DEV), (1, 0, 2))
        rim_values = jax.vmap(lambda values, index: values[:, index])(by_shard, rim_index)
        zero_rim = jnp.zeros((1, VEC, BS), block_bf.dtype)
        below_rim = jnp.concatenate([zero_rim, rim_values[:-1]], 0)
        above_rim = jnp.concatenate([rim_values[1:], zero_rim], 0)
        extended = jnp.concatenate([by_shard, below_rim, above_rim], 2).reshape(shards, VEC, block_count + 2, BS)
        slot_values = jax.vmap(lambda values, index: values[:, index])(by_shard, wet_index)
        slot_values = jnp.where(live_slots[:, None, :], slot_values, jnp.zeros((), block_bf.dtype))
        columns = jnp.transpose(slot_values, (1, 0, 2)).reshape(VEC, shards * WCAP)
        row_blocks = added_mass.reshape(N_COL, N_ROW * WR, shards * WCAP)
        pressure = lax.map(lambda matrix_rows: lax.dot_general(columns.astype(jnp.float32), matrix_rows.astype(jnp.float32), (((1,), (1,)), ((), ())), preferred_element_type=jnp.float32), row_blocks)
        pressure = jnp.transpose(pressure.reshape(N_COL, VEC, N_ROW, WR), (2, 0, 1, 3)).reshape(shards, VEC, WR)

        def shard_term(shard):
            picked = extended[shard][:, shard_ids[shard]].astype(jnp.float32)
            own_blocks = lax.dynamic_index_in_dim(blocks, shard, 1, keepdims=False).astype(jnp.float32)
            products = jnp.einsum('vikb,mikab->mvia', picked, own_blocks).reshape(3, VEC, NS_DEV)
            wet_force = jnp.zeros((VEC, NS_DEV), jnp.float32).at[:, wet_index[shard][:WR]].add(pressure[shard])
            return products[0] + coupling_rates[0] * products[1] - coupling_rates[1] * (products[2] + wet_force)
        results = lax.map(shard_term, jnp.arange(shards))
        return jnp.transpose(results, (1, 0, 2)).reshape(VEC, total_rows)
    current = start_block
    previous = jnp.zeros_like(start_block)
    coefficients = []
    for number in range(STEPS):
        applied = operate(current.astype(jnp.bfloat16))
        coef_self = contract_rows(applied, current) / total_rows
        coef_prev = contract_rows(applied, previous) / total_rows
        residual = applied - jnp.dot(coef_self, current, precision=lax.Precision.HIGHEST) - jnp.dot(coef_prev, previous, precision=lax.Precision.HIGHEST)
        gram_matrix = contract_rows(residual, residual) / total_rows
        factor = jnp.linalg.cholesky(gram_matrix)
        following = lax.linalg.triangular_solve(factor, residual, left_side=True, lower=True)
        coefficients.append(jnp.stack([coef_self, coef_prev, factor]))
        previous = current
        current = following
    return (current, jnp.stack(coefficients))
```

```python
import functools

import jax
import jax.numpy as jnp
from jax import lax
from jax.experimental import pallas as pl
from jax.experimental.pallas import tpu as pltpu
from jax.sharding import PartitionSpec as P

STEPS = 6
AXES = ("row", "col")
VMEM = pl.BlockSpec(memory_space=pltpu.VMEM)
SMEM = pl.BlockSpec(memory_space=pltpu.SMEM)
F32 = jnp.float32
BF16 = jnp.bfloat16
LIMIT = 40 * 1024 * 1024


def exact(left, right):
    return lax.dot_general(
        left, right, (((1,), (0,)), ((), ())), precision=lax.Precision.HIGHEST, preferred_element_type=F32
    )


def exact_rows(left, right):
    return lax.dot_general(
        left, right, (((1,), (1,)), ((), ())), precision=lax.Precision.HIGHEST, preferred_element_type=F32
    )


def rows(left, right):
    return lax.dot_general(left, right, (((1,), (1,)), ((), ())), preferred_element_type=F32)


def combine_kernel(rates, rim, wet, start, blocks, mixed, pick, place, halo):
    size = blocks.shape[-1]
    for k in range(blocks.shape[2]):
        whole = (
            blocks[0, 0, k].astype(F32)
            + rates[0] * blocks[1, 0, k].astype(F32)
            - rates[1] * blocks[2, 0, k].astype(F32)
        ).T
        high = whole.astype(BF16)
        mixed[0, k * size : (k + 1) * size, :size] = high
        mixed[0, k * size : (k + 1) * size, size:] = (whole - high.astype(F32)).astype(BF16)

    @pl.when(pl.program_id(0) == 0)
    def _():
        index = lax.broadcasted_iota(jnp.int32, pick.shape, 0)
        pick[...] = jnp.where(index == rim[...], 1.0, 0.0).astype(BF16)
        index = lax.broadcasted_iota(jnp.int32, place.shape, 1)
        place[...] = jnp.where(index == wet[...], 1.0, 0.0).astype(F32)
        halo[...] = jnp.dot(start[...].astype(BF16), pick[...], preferred_element_type=F32)


def combine(rates, rim, wet, start, blocks):
    _, count, nnz, size, _ = blocks.shape
    vectors, width = start.shape
    whole = lambda shape: pl.BlockSpec(shape, lambda i: (0,) * len(shape))
    return pl.pallas_call(
        combine_kernel,
        grid=(count,),
        in_specs=[
            SMEM,
            whole(rim.shape),
            whole(wet.shape),
            whole(start.shape),
            pl.BlockSpec((3, 1, nnz, size, size), lambda i: (0, i, 0, 0, 0)),
        ],
        out_specs=[
            pl.BlockSpec((1, nnz * size, 2 * size), lambda i: (i, 0, 0)),
            whole((width, rim.shape[1])),
            whole((wet.shape[0], width)),
            whole((vectors, rim.shape[1])),
        ],
        out_shape=[
            jax.ShapeDtypeStruct((count, nnz * size, 2 * size), BF16),
            jax.ShapeDtypeStruct((width, rim.shape[1]), BF16),
            jax.ShapeDtypeStruct((wet.shape[0], width), F32),
            jax.ShapeDtypeStruct((vectors, rim.shape[1]), F32),
        ],
        compiler_params=pltpu.CompilerParams(vmem_limit_bytes=LIMIT),
        name="combine",
    )(rates, rim, wet, start, blocks)


def spread_kernel(count, slots, start, mass, spread, part, onehot, values):
    @pl.when(pl.program_id(0) == 0)
    def _():
        slot = lax.broadcasted_iota(jnp.int32, slots.shape, 1)
        live = jnp.where(slot < count[0], slots[...], -1)
        index = lax.broadcasted_iota(jnp.int32, onehot.shape, 0)
        onehot[...] = jnp.where(index == live, 1.0, 0.0).astype(BF16)
        values[...] = start[...].astype(BF16)

    width, vectors = onehot.shape[0], values.shape[0]
    halves = []
    for h in range(2):
        own = mass[:, 0, h].reshape(-1, mass.shape[-1])
        spread[h] = rows(own, onehot[...]).astype(BF16)
        halves.append(rows(spread[h], values[...]))
    part[:, :vectors] = halves[0]
    part[:, vectors:] = halves[1]


def spread_mass(count, slots, start, mass):
    n_col, n_row, _, half, wcap = mass.shape
    vectors, width = start.shape
    size = n_col * half
    return pl.pallas_call(
        spread_kernel,
        grid=(n_row,),
        in_specs=[
            SMEM,
            pl.BlockSpec(slots.shape, lambda r: (0, 0)),
            pl.BlockSpec(start.shape, lambda r: (0, 0)),
            pl.BlockSpec((n_col, 1, 2, half, wcap), lambda r: (0, r, 0, 0, 0)),
        ],
        out_specs=[
            pl.BlockSpec((2, size, width), lambda r: (0, r, 0)),
            pl.BlockSpec((size, 2 * vectors), lambda r: (r, 0)),
        ],
        out_shape=[
            jax.ShapeDtypeStruct((2, n_row * size, width), BF16),
            jax.ShapeDtypeStruct((n_row * size, 2 * vectors), F32),
        ],
        scratch_shapes=[pltpu.VMEM((width, wcap), BF16), pltpu.VMEM((vectors, width), BF16)],
        compiler_params=pltpu.CompilerParams(vmem_limit_bytes=LIMIT),
        name="spread",
    )(count, slots, start, mass)


def small_matrices(total, gram, inner, factor_t, mix, coef):
    n = gram.shape[0] // 2
    scale = 1.0 / total
    aa = gram[:n, :n] * scale
    self_ = gram[:n, n:] * scale
    prev = gram[n:, :n] * scale
    cc = gram[n:, n:] * scale
    cp = inner[:, :n]
    pp = inner[:, n:]
    t_c = self_ - exact(self_, cc) - exact_rows(prev, cp)
    t_p = prev - exact(self_, cp) - exact(prev, pp)
    t_a = aa - exact_rows(self_, self_) - exact_rows(prev, prev)
    matrix = t_a - exact_rows(t_c, self_) - exact_rows(t_p, prev)
    matrix = 0.5 * (matrix + matrix.T)
    row_id = lax.broadcasted_iota(jnp.int32, (n, 2 * n), 0)
    lane_id = lax.broadcasted_iota(jnp.int32, (n, 2 * n), 1)
    factor_t[:, :n] = matrix
    factor_t[:, n:] = jnp.where(row_id == lane_id, 1.0, 0.0).astype(F32)[:, :n]
    work = [factor_t[g * 8 : (g + 1) * 8, :] for g in range(n // 8)]
    sub = lax.broadcasted_iota(jnp.int32, (8, 1), 0)
    for j in range(n):
        g, s = divmod(j, 8)
        pivot_row = work[g][s : s + 1, :]
        scaled = pivot_row / pivot_row[:, j : j + 1]
        for i in range(g, n // 8):
            column = work[i][:, j : j + 1]
            if i == g:
                column = jnp.where(sub > s, column, 0.0)
            work[i] = work[i] - column * scaled
    reduced = jnp.concatenate(work, 0)
    diagonal = jnp.sum(jnp.where(row_id == lane_id, reduced, 0.0), 1, keepdims=True)
    reduced = reduced * lax.rsqrt(diagonal)
    factor_t[...] = reduced
    inverse = factor_t[:, n:]
    mix[:, :n] = inverse
    mix[:, n : 2 * n] = -exact(inverse, self_)
    mix[:, 2 * n :] = -exact(inverse, prev)
    coef[0] = self_
    coef[1] = prev
    upper = jnp.where(row_id <= lane_id, reduced, 0.0)
    coef[2] = upper.T[:n, :]
    return exact(inverse, t_c), cc


def advance_kernel(first, total, *refs):
    it = iter(refs)
    ids, rates = next(it), next(it)
    if first:
        start = next(it)
    else:
        gram_in, inner, stack, edges, wet_held = (next(it) for _ in range(5))
    arrived, below, above, mixed, pick, place, spread = (next(it) for _ in range(7))
    stack_out, edges_out, wet_out, gram_out, halo_out, part_out = (next(it) for _ in range(6))
    if not first:
        inner_out, coef = next(it), next(it)
    extended, split = next(it), next(it)
    if not first:
        factor_t, mix, edge_all = (next(it) for _ in range(3))
    n = stack_out.shape[0] // 3
    width = stack_out.shape[1]
    size = below.shape[1]
    summed = jnp.sum(arrived[...].astype(F32), 0)
    half = summed.shape[0]
    if first:
        current = start[...]
        stack_out[n : 2 * n, :] = current
        stack_out[2 * n :, :] = jnp.zeros_like(current)
        edges_out[:n, :size] = below[...]
        edges_out[:n, size:] = above[...]
        edges_out[n:, :] = jnp.zeros_like(edges_out[n:, :])
        wet_out[:half, :n] = summed[:, :n]
        wet_out[half:, :n] = summed[:, n:]
        wet_out[:, n:] = jnp.zeros_like(wet_out[:, n:])
    else:
        cp, cc = small_matrices(total, gram_in, inner, factor_t, mix, coef)
        inner_out[:, :n] = cp
        inner_out[:, n:] = cc
        current = exact(mix[...], stack[...])
        stack_out[n : 2 * n, :] = current
        stack_out[2 * n :, :] = stack[n : 2 * n, :]
        edge_all[:n, :size] = below[...]
        edge_all[:n, size:] = above[...]
        edge_all[n:, :] = edges[...]
        edges_out[:n, :] = exact(mix[...], edge_all[...])
        edges_out[n:, :] = edges[:n, :]
        fresh = exact_rows(jnp.concatenate([summed[:, :n], summed[:, n:]], 0), mix[:, :n])
        fresh = fresh + exact_rows(wet_held[:, :n], mix[:, n : 2 * n])
        fresh = fresh + exact_rows(wet_held[:, n:], mix[:, 2 * n :])
        wet_out[:, :n] = fresh
        wet_out[:, n:] = wet_held[:, :n]
    count = width // size
    for i in range(count):
        extended[i] = stack_out[n : 2 * n, i * size : (i + 1) * size].astype(BF16)
    extended[count] = edges_out[:n, :size].astype(BF16)
    extended[count + 1] = edges_out[:n, size:].astype(BF16)
    force = wet_out[:, :n].T * rates[1]
    for i in range(count):
        picked = jnp.concatenate([extended[ids[i, k]] for k in range(ids.shape[1])], 1)
        both = jnp.dot(picked, mixed[i], preferred_element_type=F32)
        lanes = slice(i * size, (i + 1) * size)
        applied = both[:, :size] + both[:, size:] - exact(force, place[:, lanes])
        stack_out[:n, lanes] = applied
        high = applied.astype(BF16)
        split[:n, lanes] = high
        split[n:, lanes] = (applied - high.astype(F32)).astype(BF16)
    products = exact_rows(stack_out[:n, :], stack_out[...])
    gram_out[:n, :] = products[:, : 2 * n]
    gram_out[n:, :n] = products[:, 2 * n :]
    gram_out[n:, n:] = exact_rows(stack_out[n : 2 * n, :], stack_out[n : 2 * n, :])
    rim = jnp.dot(split[...], pick[...], preferred_element_type=F32)
    halo_out[...] = rim[:n] + rim[n:]
    tops = rows(spread[0], split[...])
    tops = tops + pltpu.roll(tops, n, 1)
    ends = rows(spread[1], split[...])
    ends = ends + pltpu.roll(ends, n, 1)
    lane = lax.broadcasted_iota(jnp.int32, tops.shape, 1)
    part_out[...] = jnp.where(lane < n, tops, ends).astype(part_out.dtype)


def advance(first, total, ids, rates, state, arrived, below, above, fixed):
    mixed, pick, place, spread = fixed
    vectors, size = below.shape
    width = pick.shape[0]
    wets = place.shape[0]
    shapes = [
        jax.ShapeDtypeStruct((3 * vectors, width), F32),
        jax.ShapeDtypeStruct((2 * vectors, 2 * size), F32),
        jax.ShapeDtypeStruct((wets, 2 * vectors), F32),
        jax.ShapeDtypeStruct((2 * vectors, 2 * vectors), F32),
        jax.ShapeDtypeStruct((vectors, size), F32),
        jax.ShapeDtypeStruct((spread.shape[1], 2 * vectors), F32),
    ]
    scratch = [
        pltpu.VMEM((width // size + 2, vectors, size), BF16),
        pltpu.VMEM((2 * vectors, width), BF16),
    ]
    if not first:
        shapes += [
            jax.ShapeDtypeStruct((vectors, 2 * vectors), F32),
            jax.ShapeDtypeStruct((3, vectors, vectors), F32),
        ]
        scratch += [
            pltpu.VMEM((vectors, 2 * vectors), F32),
            pltpu.VMEM((vectors, 3 * vectors), F32),
            pltpu.VMEM((3 * vectors, 2 * size), F32),
        ]
    return pl.pallas_call(
        functools.partial(advance_kernel, first, total),
        in_specs=[SMEM, SMEM] + [VMEM] * (len(state) + 7),
        out_specs=[VMEM] * len(shapes),
        out_shape=shapes,
        scratch_shapes=scratch,
        compiler_params=pltpu.CompilerParams(vmem_limit_bytes=LIMIT),
        name="advance",
    )(ids, rates, *state, arrived, below, above, mixed, pick, place, spread)


def finish_kernel(total, gram_in, inner, stack, out, coef, factor_t, mix):
    small_matrices(total, gram_in, inner, factor_t, mix, coef)
    out[...] = exact(mix[...], stack[...])


def finish(total, gram, inner, stack):
    vectors = gram.shape[0] // 2
    return pl.pallas_call(
        functools.partial(finish_kernel, total),
        in_specs=[VMEM] * 3,
        out_specs=[VMEM] * 2,
        out_shape=[
            jax.ShapeDtypeStruct((vectors, stack.shape[1]), F32),
            jax.ShapeDtypeStruct((3, vectors, vectors), F32),
        ],
        scratch_shapes=[
            pltpu.VMEM((vectors, 2 * vectors), F32),
            pltpu.VMEM((vectors, 3 * vectors), F32),
        ],
        compiler_params=pltpu.CompilerParams(vmem_limit_bytes=LIMIT),
        name="finish",
    )(gram, inner, stack)


def local(n_row, n_col, start_block, struct_blocks, block_ids, rim_rows, wet_slots, wet_counts, added_mass, rates):
    peers = n_row * n_col
    vectors, width = start_block.shape
    total = float(width * peers)
    wcap = wet_slots.shape[0]
    wets = added_mass.shape[0] // n_row

    def exchange(parts):
        return lax.all_to_all(parts, AXES, 0, 0, tiled=True)

    def neighbours(halo):
        up = [(i, i + 1) for i in range(peers - 1)]
        down = [(i + 1, i) for i in range(peers - 1)]
        return lax.ppermute(halo, AXES, up), lax.ppermute(halo, AXES, down)

    def summed(gram):
        lines = gram.shape[0] // peers
        mine = exchange(gram.reshape(peers, lines, -1)).sum(0)
        return exchange(jnp.broadcast_to(mine[None], (peers, *mine.shape))).reshape(gram.shape)

    def pressure(part):
        return exchange(part.reshape(peers, wets // 2, 2 * vectors))

    blocks = added_mass.reshape(-1, n_col, wcap).transpose(1, 0, 2)
    mass = lax.all_to_all(blocks, "col", 0, 0, tiled=True)
    mass = mass.reshape(n_col, n_row, 2, wets // 2, wcap)
    mixed, pick, place, halo = combine(
        rates, rim_rows[None, :], wet_slots[:wets, None], start_block, struct_blocks
    )
    spread, part = spread_mass(wet_counts, wet_slots[None, :], start_block, mass)
    fixed = (mixed, pick, place, spread)
    coefficients = []
    state = (start_block,)
    for number in range(STEPS):
        below, above = neighbours(halo)
        arrived = pressure(part)
        outs = advance(number == 0, total, block_ids, rates, state, arrived, below, above, fixed)
        stack, edges, wet_held, gram, halo, part = outs[:6]
        if number == 0:
            inner = jnp.zeros((vectors, 2 * vectors), F32)
        else:
            inner = outs[6]
            coefficients.append(outs[7])
        gram = summed(gram)
        state = (gram, inner, stack, edges, wet_held)
    final, coef = finish(total, gram, inner, stack)
    coefficients.append(coef)
    return final, jnp.stack(coefficients)


def solution(mesh):
    return jax.shard_map(
        functools.partial(local, mesh.shape["row"], mesh.shape["col"]),
        mesh=mesh,
        in_specs=(
            P(None, AXES),
            P(None, AXES, None, None, None),
            P(AXES, None),
            P(AXES),
            P(AXES),
            P(AXES),
            P("col", "row"),
            P(),
        ),
        out_specs=(P(None, AXES), P()),
        check_vma=False,
    )
```

```python
import functools

import jax
import jax.numpy as jnp
from jax import lax
from jax.experimental import pallas as pl
from jax.experimental.pallas import tpu as pltpu
from jax.sharding import PartitionSpec as P

STEPS = 6
AXES = ("row", "col")
VMEM = pl.BlockSpec(memory_space=pltpu.VMEM)
SMEM = pl.BlockSpec(memory_space=pltpu.SMEM)
HBM = pl.BlockSpec(memory_space=pltpu.HBM)
F32 = jnp.float32
BF16 = jnp.bfloat16
LIMIT = 40 * 1024 * 1024


def exact(left, right):
    return lax.dot_general(
        left, right, (((1,), (0,)), ((), ())), precision=lax.Precision.HIGHEST, preferred_element_type=F32
    )


def exact_rows(left, right):
    return lax.dot_general(
        left, right, (((1,), (1,)), ((), ())), precision=lax.Precision.HIGHEST, preferred_element_type=F32
    )


def rows(left, right):
    return lax.dot_general(left, right, (((1,), (1,)), ((), ())), preferred_element_type=F32)


def combine_kernel(rates, rim, wet, start, blocks, mixed, pick, place, halo):
    size = blocks.shape[-1]
    for k in range(blocks.shape[2]):
        whole = (
            blocks[0, 0, k].astype(F32)
            + rates[0] * blocks[1, 0, k].astype(F32)
            - rates[1] * blocks[2, 0, k].astype(F32)
        ).T
        high = whole.astype(BF16)
        mixed[0, k * size : (k + 1) * size, :size] = high
        mixed[0, k * size : (k + 1) * size, size:] = (whole - high.astype(F32)).astype(BF16)

    @pl.when(pl.program_id(0) == 0)
    def _():
        index = lax.broadcasted_iota(jnp.int32, pick.shape, 0)
        pick[...] = jnp.where(index == rim[...], 1.0, 0.0).astype(BF16)
        index = lax.broadcasted_iota(jnp.int32, place.shape, 1)
        place[...] = jnp.where(index == wet[...], 1.0, 0.0).astype(BF16)
        halo[...] = jnp.dot(start[...].astype(BF16), pick[...], preferred_element_type=F32)


def combine(rates, rim, wet, start, blocks):
    _, count, nnz, size, _ = blocks.shape
    vectors, width = start.shape
    whole = lambda shape: pl.BlockSpec(shape, lambda i: (0,) * len(shape))
    return pl.pallas_call(
        combine_kernel,
        grid=(count,),
        in_specs=[
            SMEM,
            whole(rim.shape),
            whole(wet.shape),
            whole(start.shape),
            pl.BlockSpec((3, 1, nnz, size, size), lambda i: (0, i, 0, 0, 0)),
        ],
        out_specs=[
            pl.BlockSpec((1, nnz * size, 2 * size), lambda i: (i, 0, 0)),
            whole((width, rim.shape[1])),
            whole((wet.shape[0], width)),
            whole((vectors, rim.shape[1])),
        ],
        out_shape=[
            jax.ShapeDtypeStruct((count, nnz * size, 2 * size), BF16),
            jax.ShapeDtypeStruct((width, rim.shape[1]), BF16),
            jax.ShapeDtypeStruct((wet.shape[0], width), BF16),
            jax.ShapeDtypeStruct((vectors, rim.shape[1]), F32),
        ],
        compiler_params=pltpu.CompilerParams(vmem_limit_bytes=LIMIT),
        name="combine",
    )(rates, rim, wet, start, blocks)


def spread_kernel(count, slots, start, mass, spread, part, own, total):
    n_col, n_row, _, half, wcap = mass.shape
    size = n_col * half
    step = pl.program_id(0)

    @pl.when(step == 0)
    def _():
        for h in range(2):
            for r in range(n_row):
                first = (h * n_row + r) * size
                own[first : first + size] = mass[:, r, h].reshape(size, wcap)
        total[...] = jnp.zeros_like(total)

    slot = lax.broadcasted_iota(jnp.int32, slots.shape, 1)
    live = jnp.where(slot < count[0], slots[...], -1)
    columns, vectors = spread.shape[1], start.shape[0]
    index = lax.broadcasted_iota(jnp.int32, (columns, wcap), 0) + step * columns
    onehot = jnp.where(index == live, 1.0, 0.0).astype(BF16)
    block = rows(own[...], onehot).astype(BF16)
    spread[...] = block
    total[...] += rows(block, start[...].astype(BF16))

    @pl.when(step == pl.num_programs(0) - 1)
    def _():
        part[:, :vectors] = total[: n_row * size]
        part[:, vectors:] = total[n_row * size :]


def spread_mass(count, slots, start, mass):
    n_col, n_row, _, half, wcap = mass.shape
    vectors, width = start.shape
    size = n_col * n_row * half
    columns = min(width, 512)
    return pl.pallas_call(
        spread_kernel,
        grid=(width // columns,),
        in_specs=[
            SMEM,
            pl.BlockSpec(slots.shape, lambda i: (0, 0)),
            pl.BlockSpec((vectors, columns), lambda i: (0, i)),
            pl.BlockSpec(mass.shape, lambda i: (0,) * 5),
        ],
        out_specs=[
            pl.BlockSpec((2 * size, columns), lambda i: (0, i)),
            pl.BlockSpec((size, 2 * vectors), lambda i: (0, 0)),
        ],
        out_shape=[
            jax.ShapeDtypeStruct((2 * size, width), BF16),
            jax.ShapeDtypeStruct((size, 2 * vectors), F32),
        ],
        scratch_shapes=[pltpu.VMEM((2 * size, wcap), BF16), pltpu.VMEM((2 * size, vectors), F32)],
        compiler_params=pltpu.CompilerParams(vmem_limit_bytes=LIMIT),
        name="spread",
    )(count, slots, start, mass)


def coefficients_of(total, gram, inner, mix, coef):
    n = gram.shape[0] // 2
    scale = 1.0 / total
    aa = gram[:n, :n] * scale
    self_ = gram[:n, n:] * scale
    prev = gram[n:, :n] * scale
    cc = gram[n:, n:] * scale
    cp = inner[:, :n]
    pp = inner[:, n:]
    mix[:, :n] = -self_
    mix[:, n:] = -prev
    coef[0] = self_
    coef[1] = prev
    t_c = self_ - exact(self_, cc) - exact_rows(prev, cp)
    t_p = prev - exact(self_, cp) - exact(prev, pp)
    t_a = aa - exact_rows(self_, self_) - exact_rows(prev, prev)
    matrix = t_a - exact_rows(t_c, self_) - exact_rows(t_p, prev)
    return 0.5 * (matrix + matrix.T), t_c, cc


def eliminate(matrix, beside, coef, factor_t):
    n = matrix.shape[0]
    row_id = lax.broadcasted_iota(jnp.int32, (n, 2 * n), 0)
    lane_id = lax.broadcasted_iota(jnp.int32, (n, 2 * n), 1)
    factor_t[...] = jnp.where(row_id + n == lane_id, 1.0, 0.0)
    factor_t[:, :n] = matrix
    work = [factor_t[g * 8 : (g + 1) * 8, :] for g in range(n // 8)]
    sub = lax.broadcasted_iota(jnp.int32, (8, 1), 0)
    done = 0
    for j in range(0, n, 2):
        g, s = divmod(j, 8)
        top = work[g][s : s + 1, :]
        low = work[g][s + 1 : s + 2, :]
        a, b, c = top[:, j : j + 1], top[:, j + 1 : j + 2], low[:, j + 1 : j + 2]
        scale = 1.0 / (a * c - b * b)
        new_top = (c * top - b * low) * scale
        new_low = (a * low - b * top) * scale
        for i in range(g, n // 8):
            left, right = work[i][:, j : j + 1], work[i][:, j + 1 : j + 2]
            if i == g:
                left = jnp.where(sub > s + 1, left, 0.0)
                right = jnp.where(sub > s + 1, right, 0.0)
            work[i] = work[i] - (left * new_top + right * new_low)
        goal = len(beside) * (j + 2) // n
        while done < goal:
            beside[done]()
            done += 1
    reduced = jnp.concatenate(work, 0)
    above = pltpu.roll(reduced, 1, 0)
    odd = lax.broadcasted_iota(jnp.int32, (n, 1), 0) % 2 == 1
    pick = lambda values, where: jnp.sum(jnp.where(where, values, 0.0), 1, keepdims=True)
    under = pick(above, lane_id == row_id) / jnp.where(odd, pick(above, lane_id + 1 == row_id), 1.0)
    reduced = reduced - jnp.where(odd, under, 0.0) * above
    diagonal = pick(reduced, lane_id == row_id)
    scale = lax.rsqrt(diagonal)
    scale = scale * (1.5 - 0.5 * diagonal * scale * scale)
    reduced = reduced * scale
    factor_t[...] = reduced
    upper = jnp.where(row_id <= lane_id, reduced, 0.0)
    coef[2] = upper.T[:n, :]
    return factor_t[:, n:]


def thirds(values):
    high = values.astype(BF16)
    rest = values - high.astype(F32)
    middle = rest.astype(BF16)
    return jnp.concatenate([high, middle, (rest - middle.astype(F32)).astype(BF16)], 0)


def unpack(lines, received, target, lanes, offset):
    for s in range(received.shape[0]):
        if s * lines < target.shape[0]:
            target[s * lines : (s + 1) * lines, lanes] = received[s, offset : offset + lines]


def advance_kernel(mode, total, peers, *refs):
    it = iter(refs)
    take = lambda k: [next(it) for _ in range(k)]
    ids, rates = take(2)
    if mode == "first":
        arrived, below, above, held_in = take(4)
        held = [held_in]
    else:
        received, pressed, inner, edges, wet_held = take(5)
        held = take(3)
    pick, place, mixed_in, spread_in = take(4)
    (applied_out,) = take(1)
    edges_out, wet_out, send = take(3) if mode != "last" else (None, None, None)
    if mode == "last":
        (gram_s,) = take(1)
    if mode != "first":
        current_out, inner_out, coef = take(3)
    extended, split, stack, fresh, mixed, spread, sems = take(7)
    if mode != "last":
        (gram_s,) = take(1)
    if mode != "first":
        factor_t, mix, gram_in, edge_in = take(4)
    else:
        (edge_in,) = take(1)

    n = fresh.shape[0]
    width = fresh.shape[1] // 2
    size = edge_in.shape[1] // 2
    count = width // size
    glines = -(-2 * n // peers)
    hlines = -(-n // peers)
    loads = []
    for k, source in enumerate(held):
        place_at = stack.at[pl.ds(k * n, n)] if mode != "first" else fresh.at[:, pl.ds(width, width)]
        loads.append(pltpu.make_async_copy(source, place_at, sems.at[k]))
    load_mixed = pltpu.make_async_copy(mixed_in, mixed, sems.at[3])
    for copy in loads + [load_mixed]:
        copy.start()
    if mode != "last":
        load_spread = pltpu.make_async_copy(spread_in, spread, sems.at[4])
        load_spread.start()

    if mode == "first":
        edge_in[:n, :size] = below[...]
        edge_in[:n, size:] = above[...]
        summed = jnp.sum(arrived[...], 0)
    else:
        unpack(glines, received, gram_in, slice(None), 0)
        unpack(hlines, received, edge_in.at[pl.ds(0, n)], slice(0, size), glines)
        unpack(hlines, received, edge_in.at[pl.ds(0, n)], slice(size, 2 * size), glines + hlines)
        edge_in[n:, :] = edges[...]
        summed = pressed[...]
        matrix, t_c, cc = coefficients_of(total, gram_in, inner, mix, coef)
    wet = jnp.concatenate([summed[:, :n], summed[:, n:]], 0)
    edge = edge_in[:n, :]
    for copy in loads:
        copy.wait()
    if mode == "first":
        residual = fresh[:, width:]
    else:
        wet = wet + exact_rows(wet_held[...], mix[...])
        edge = edge + exact(mix[...], edge_in[n:, :])
        residual = stack[:n, :] + exact(mix[...], stack[n:, :])
        stack[:n, :] = residual
    for i in range(count):
        extended[i] = residual[:, i * size : (i + 1) * size].astype(BF16)
    extended[count] = edge[:, :size].astype(BF16)
    extended[count + 1] = edge[:, size:].astype(BF16)
    force = thirds(wet.T * rates[1])
    load_mixed.wait()

    def block(i):
        picked = jnp.concatenate([extended[ids[i, k]] for k in range(ids.shape[1])], 1)
        both = jnp.dot(picked, mixed[i], preferred_element_type=F32)
        lanes = slice(i * size, (i + 1) * size)
        added = jnp.dot(force, place[:, lanes], preferred_element_type=F32)
        fresh[:, lanes] = both[:, :size] + both[:, size:] - (added[:n] + added[n : 2 * n] + added[2 * n :])

    beside = [functools.partial(block, i) for i in range(count)]
    stores = []
    if mode == "first":
        for emit in beside:
            emit()
        edges_out[:n, :] = edge
        edges_out[n:, :] = jnp.zeros_like(edge)
        wet_out[:, :n] = wet
        wet_out[:, n:] = jnp.zeros_like(wet)
    else:
        inverse = eliminate(matrix, beside, coef, factor_t)
        fresh[:, width:] = exact(inverse, stack[:n, :])
        stores.append(pltpu.make_async_copy(fresh.at[:, pl.ds(width, width)], current_out, sems.at[5]))
        stores[-1].start()
        fresh[:, :width] = exact(inverse, fresh[:, :width])
        inner_out[:, :n] = exact(inverse, t_c)
        inner_out[:, n:] = cc
        if mode != "last":
            edges_out[:n, :] = exact(inverse, edge)
            edges_out[n:, :] = edges[:n, :]
            wet_out[:, :n] = exact_rows(wet, inverse)
            wet_out[:, n:] = wet_held[:, :n]
    stores.append(pltpu.make_async_copy(fresh.at[:, pl.ds(0, width)], applied_out, sems.at[6]))
    stores[-1].start()
    applied = fresh[:, :width]
    current = fresh[:, width:]
    gram_s[:n, :n] = exact_rows(applied, applied)
    gram_s[:n, n:] = exact_rows(applied, current)
    if mode == "first":
        gram_s[n:, :n] = jnp.zeros((n, n), F32)
    else:
        gram_s[n : 2 * n, :n] = exact_rows(applied, stack[n : 2 * n, :])
    gram_s[n : 2 * n, n:] = exact_rows(current, current)
    if mode != "last":
        high = applied.astype(BF16)
        split[:n, :] = high
        split[n:, :] = (applied - high.astype(F32)).astype(BF16)
        rim = jnp.dot(split[...], pick[...], preferred_element_type=F32)
        edge_in[:n, :size] = rim[:n] + rim[n:]
        load_spread.wait()
        wets = wet_out.shape[0] // 2
        middle = spread.shape[0] // 2
        tops = rows(spread[:middle], split[...])
        tops = tops + pltpu.roll(tops, n, 1)
        ends = rows(spread[middle:], split[...])
        ends = ends + pltpu.roll(ends, n, 1)
        lane = lax.broadcasted_iota(jnp.int32, tops.shape, 1)
        send[:, :wets, :] = jnp.where(lane < n, tops, ends).reshape(peers, wets, 2 * n)
        rest = send.shape[1] - wets
        send[:, wets:, :] = jnp.zeros((peers, rest, 2 * n), F32)
        for d in range(peers):
            if d * glines < 2 * n:
                send[d, wets : wets + glines] = gram_s[d * glines : (d + 1) * glines, :]
            if d * hlines < n:
                send[d, wets + glines : wets + glines + hlines] = edge_in[d * hlines : (d + 1) * hlines, :size]
    for copy in stores:
        copy.wait()


def advance(mode, total, peers, ids, rates, state, fixed):
    mixed, pick, place, spread = fixed
    vectors, size = mixed.shape[1] // ids.shape[1] // 2, mixed.shape[2] // 2
    width = pick.shape[0]
    wets = place.shape[0]
    vectors = state[-1].shape[0]
    lines = -(-(wets // 2 + -(-2 * vectors // peers) + -(-vectors // peers)) // 8) * 8
    sds = jax.ShapeDtypeStruct
    block = sds((vectors, width), F32)
    shapes, specs = [block], [HBM]
    if mode != "last":
        shapes += [
            sds((2 * vectors, 2 * size), F32),
            sds((wets, 2 * vectors), F32),
            sds((peers, lines, 2 * vectors), F32),
        ]
        specs += [VMEM] * 3
    else:
        shapes += [sds((2 * vectors, 2 * vectors), F32)]
        specs += [VMEM]
    if mode != "first":
        shapes += [block, sds((vectors, 2 * vectors), F32), sds((3, vectors, vectors), F32)]
        specs += [HBM, VMEM, VMEM]
    scratch = [
        pltpu.VMEM((width // size + 2, vectors, size), BF16),
        pltpu.VMEM((2 * vectors, width), BF16),
        pltpu.VMEM((3 * vectors, width), F32),
        pltpu.VMEM((vectors, 2 * width), F32),
        pltpu.VMEM(mixed.shape, BF16),
        pltpu.VMEM(spread.shape, BF16),
        pltpu.SemaphoreType.DMA((7,)),
    ]
    if mode != "last":
        scratch += [pltpu.VMEM((2 * vectors, 2 * vectors), F32)]
    if mode != "first":
        scratch += [
            pltpu.VMEM((vectors, 2 * vectors), F32),
            pltpu.VMEM((vectors, 2 * vectors), F32),
            pltpu.VMEM((2 * vectors, 2 * vectors), F32),
            pltpu.VMEM((3 * vectors, 2 * size), F32),
        ]
        held = 3
    else:
        scratch += [pltpu.VMEM((vectors, 2 * size), F32)]
        held = 1
    return pl.pallas_call(
        functools.partial(advance_kernel, mode, total, peers),
        in_specs=[SMEM, SMEM] + [VMEM] * (len(state) - held) + [HBM] * held + [VMEM, VMEM, HBM, HBM],
        out_specs=specs,
        out_shape=shapes,
        scratch_shapes=scratch,
        compiler_params=pltpu.CompilerParams(vmem_limit_bytes=LIMIT),
        name="advance_" + mode,
    )(ids, rates, *state, pick, place, mixed, spread)


def route_kernel(vectors, wets, received, pressed, send):
    peers = received.shape[0]
    glines = -(-2 * vectors // peers)
    hlines = -(-vectors // peers)
    pressed[...] = jnp.sum(received[:, :wets, :], 0)
    mine = jnp.sum(received[:, wets:, :], 0)[:glines]
    edge = wets + glines
    nothing = jnp.zeros((hlines, 2 * vectors), F32)
    for t in range(peers):
        send[t] = jnp.zeros(send.shape[1:], F32)
        send[t, :glines] = mine
        send[t, glines : glines + hlines] = received[t - 1, edge : edge + hlines] if t > 0 else nothing
        send[t, glines + hlines : glines + 2 * hlines] = (
            received[t + 1, edge : edge + hlines] if t < peers - 1 else nothing
        )


def route(vectors, wets, received):
    peers = received.shape[0]
    return pl.pallas_call(
        functools.partial(route_kernel, vectors, wets),
        in_specs=[VMEM],
        out_specs=[VMEM] * 2,
        out_shape=[
            jax.ShapeDtypeStruct((wets, 2 * vectors), F32),
            jax.ShapeDtypeStruct((peers, 8, 2 * vectors), F32),
        ],
        compiler_params=pltpu.CompilerParams(vmem_limit_bytes=LIMIT),
        name="route",
    )(received)


def finish_kernel(total, gram_in, inner, applied, current, previous, out, coef, factor_t, mix, stack, sems):
    n = inner.shape[0]
    loads = []
    for k, source in enumerate((applied, current, previous)):
        loads.append(pltpu.make_async_copy(source, stack.at[pl.ds(k * n, n)], sems.at[k]))
        loads[-1].start()
    matrix, _, _ = coefficients_of(total, gram_in, inner, mix, coef)
    for copy in loads:
        copy.wait()

    def residual():
        stack[:n, :] = stack[:n, :] + exact(mix[...], stack[n:, :])

    inverse = eliminate(matrix, [residual], coef, factor_t)
    out[...] = exact(inverse, stack[:n, :])


def finish(total, gram, inner, held):
    vectors, width = held[0].shape
    return pl.pallas_call(
        functools.partial(finish_kernel, total),
        in_specs=[VMEM] * 2 + [HBM] * 3,
        out_specs=[VMEM] * 2,
        out_shape=[
            jax.ShapeDtypeStruct((vectors, width), F32),
            jax.ShapeDtypeStruct((3, vectors, vectors), F32),
        ],
        scratch_shapes=[
            pltpu.VMEM((vectors, 2 * vectors), F32),
            pltpu.VMEM((vectors, 2 * vectors), F32),
            pltpu.VMEM((3 * vectors, width), F32),
            pltpu.SemaphoreType.DMA((3,)),
        ],
        compiler_params=pltpu.CompilerParams(vmem_limit_bytes=LIMIT),
        name="finish",
    )(gram, inner, *held)


def local(n_row, n_col, start_block, struct_blocks, block_ids, rim_rows, wet_slots, wet_counts, added_mass, rates):
    peers = n_row * n_col
    vectors, width = start_block.shape
    total = float(width * peers)
    wcap = wet_slots.shape[0]
    wets = added_mass.shape[0] // n_row

    def exchange(parts):
        return lax.all_to_all(parts, AXES, 0, 0, tiled=True)

    def neighbours(halo):
        up = [(i, i + 1) for i in range(peers - 1)]
        down = [(i + 1, i) for i in range(peers - 1)]
        return lax.ppermute(halo, AXES, up), lax.ppermute(halo, AXES, down)

    def summed(gram):
        lines = gram.shape[0] // peers
        mine = exchange(gram.reshape(peers, lines, -1)).sum(0)
        return exchange(jnp.broadcast_to(mine[None], (peers, *mine.shape))).reshape(gram.shape)

    blocks = added_mass.reshape(-1, n_col, wcap).transpose(1, 0, 2)
    mass = lax.all_to_all(blocks, "col", 0, 0, tiled=True)
    mass = mass.reshape(n_col, n_row, 2, wets // 2, wcap)
    mixed, pick, place, halo = combine(
        rates, rim_rows[None, :], wet_slots[:wets, None], start_block, struct_blocks
    )
    spread, part = spread_mass(wet_counts, wet_slots[None, :], start_block, mass)
    fixed = (mixed, pick, place, spread)
    below, above = neighbours(halo)
    arrived = exchange(part.reshape(peers, wets // 2, 2 * vectors))
    step = functools.partial(advance, total=total, peers=peers, ids=block_ids, rates=rates, fixed=fixed)
    applied, edges, wet_held, send = step("first", state=(arrived, below, above, start_block))
    inner = jnp.zeros((vectors, 2 * vectors), F32)
    current, previous = start_block, jnp.zeros_like(start_block)
    coefficients = []
    for number in range(1, STEPS):
        pressed, again = route(vectors, wets // 2, exchange(send))
        received = exchange(again)
        state = (received, pressed, inner, edges, wet_held, applied, current, previous)
        if number < STEPS - 1:
            applied, edges, wet_held, send, following, inner, coef = step("mid", state=state)
        else:
            applied, gram, following, inner, coef = step("last", state=state)
        coefficients.append(coef)
        previous, current = current, following
    final, coef = finish(total, summed(gram), inner, (applied, current, previous))
    coefficients.append(coef)
    return final, jnp.stack(coefficients)


def solution(mesh):
    return jax.shard_map(
        functools.partial(local, mesh.shape["row"], mesh.shape["col"]),
        mesh=mesh,
        in_specs=(
            P(None, AXES),
            P(None, AXES, None, None, None),
            P(AXES, None),
            P(AXES),
            P(AXES),
            P(AXES),
            P("col", "row"),
            P(),
        ),
        out_specs=(P(None, AXES), P()),
        check_vma=False,
    )
```

```python
import functools

import jax
import jax.numpy as jnp
from jax import lax
from jax.experimental import pallas as pl
from jax.experimental.pallas import tpu as pltpu
from jax.sharding import PartitionSpec as P

STEPS = 6
AXES = ("row", "col")
VMEM = pl.BlockSpec(memory_space=pltpu.VMEM)
SMEM = pl.BlockSpec(memory_space=pltpu.SMEM)
HBM = pl.BlockSpec(memory_space=pltpu.HBM)
ANY = pl.BlockSpec(memory_space=pl.ANY)
F32 = jnp.float32
BF16 = jnp.bfloat16
LIMIT = 40 * 1024 * 1024


def exact(left, right):
    return lax.dot_general(
        left, right, (((1,), (0,)), ((), ())), precision=lax.Precision.HIGHEST, preferred_element_type=F32
    )


def exact_rows(left, right):
    return lax.dot_general(
        left, right, (((1,), (1,)), ((), ())), precision=lax.Precision.HIGHEST, preferred_element_type=F32
    )


def rows(left, right):
    return lax.dot_general(left, right, (((1,), (1,)), ((), ())), preferred_element_type=F32)


def in_hbm(values):
    return pltpu.with_memory_space_constraint(values, pltpu.HBM)


def halves(values):
    high = values.astype(BF16)
    return high, (values - high.astype(F32)).astype(BF16)


def combine_kernel(rates, rim, wet, start, blocks, mixed, pick, place, halo):
    size = blocks.shape[-1]
    for k in range(blocks.shape[2]):
        whole = (
            blocks[0, 0, k].astype(F32)
            + rates[0] * blocks[1, 0, k].astype(F32)
            - rates[1] * blocks[2, 0, k].astype(F32)
        ).T
        high = whole.astype(BF16)
        mixed[0, k * size : (k + 1) * size, :size] = high
        mixed[0, k * size : (k + 1) * size, size:] = (whole - high.astype(F32)).astype(BF16)

    @pl.when(pl.program_id(0) == 0)
    def _():
        index = lax.broadcasted_iota(jnp.int32, pick.shape, 0)
        pick[...] = jnp.where(index == rim[...], 1.0, 0.0).astype(BF16)
        index = lax.broadcasted_iota(jnp.int32, place.shape, 1)
        place[...] = jnp.where(index == wet[...], 1.0, 0.0).astype(BF16)
        high, low = halves(start[...])
        halo[...] = jnp.dot(high, pick[...], preferred_element_type=F32) + jnp.dot(
            low, pick[...], preferred_element_type=F32
        )


def combine(rates, rim, wet, start, blocks):
    _, count, nnz, size, _ = blocks.shape
    vectors, width = start.shape
    whole = lambda shape: pl.BlockSpec(shape, lambda i: (0,) * len(shape))
    return pl.pallas_call(
        combine_kernel,
        grid=(count,),
        in_specs=[
            SMEM,
            whole(rim.shape),
            whole(wet.shape),
            whole(start.shape),
            pl.BlockSpec((3, 1, nnz, size, size), lambda i: (0, i, 0, 0, 0)),
        ],
        out_specs=[
            pl.BlockSpec((1, nnz * size, 2 * size), lambda i: (i, 0, 0)),
            whole((width, rim.shape[1])),
            whole((wet.shape[0], width)),
            whole((vectors, rim.shape[1])),
        ],
        out_shape=[
            pltpu.HBM((count, nnz * size, 2 * size), BF16),
            jax.ShapeDtypeStruct((width, rim.shape[1]), BF16),
            jax.ShapeDtypeStruct((wet.shape[0], width), BF16),
            jax.ShapeDtypeStruct((vectors, rim.shape[1]), F32),
        ],
        compiler_params=pltpu.CompilerParams(vmem_limit_bytes=LIMIT),
        name="combine",
    )(rates, rim, wet, start, blocks)


def spread_kernel(count, slots, start, mass, _below, _above, spread, part, own, total):
    n_col, n_row, _, half, wcap = mass.shape
    size = n_col * half
    step = pl.program_id(0)

    @pl.when(step == 0)
    def _():
        for h in range(2):
            for r in range(n_row):
                first = (h * n_row + r) * size
                own[first : first + size] = mass[:, r, h].reshape(size, wcap)
        total[...] = jnp.zeros_like(total)

    slot = lax.broadcasted_iota(jnp.int32, slots.shape, 1)
    live = jnp.where(slot < count[0], slots[...], -1)
    columns, vectors = spread.shape[1], start.shape[0]
    index = lax.broadcasted_iota(jnp.int32, (columns, wcap), 0) + step * columns
    onehot = jnp.where(index == live, 1.0, 0.0).astype(BF16)
    block = rows(own[...], onehot).astype(BF16)
    spread[...] = block
    total[...] += rows(block, start[...].astype(BF16))

    @pl.when(step == pl.num_programs(0) - 1)
    def _():
        part[:, :vectors] = total[: n_row * size].astype(BF16)
        part[:, vectors:] = total[n_row * size :].astype(BF16)


def spread_mass(count, slots, start, mass, *ready):
    n_col, n_row, _, half, wcap = mass.shape
    vectors, width = start.shape
    size = n_col * n_row * half
    columns = min(width, 512)
    return pl.pallas_call(
        spread_kernel,
        grid=(width // columns,),
        in_specs=[
            SMEM,
            pl.BlockSpec(slots.shape, lambda i: (0, 0)),
            pl.BlockSpec((vectors, columns), lambda i: (0, i)),
            pl.BlockSpec(mass.shape, lambda i: (0,) * 5),
            ANY,
            ANY,
        ],
        out_specs=[
            pl.BlockSpec((2 * size, columns), lambda i: (0, i)),
            pl.BlockSpec((size, 2 * vectors), lambda i: (0, 0)),
        ],
        out_shape=[
            pltpu.HBM((2 * size, width), BF16),
            jax.ShapeDtypeStruct((size, 2 * vectors), BF16),
        ],
        scratch_shapes=[pltpu.VMEM((2 * size, wcap), BF16), pltpu.VMEM((2 * size, vectors), F32)],
        compiler_params=pltpu.CompilerParams(vmem_limit_bytes=LIMIT),
        name="spread",
    )(count, slots, start, mass, *ready)


def eliminate(matrix, beside, coef, factor_t):
    n = matrix.shape[0]
    row_id = lax.broadcasted_iota(jnp.int32, (n, 2 * n), 0)
    lane_id = lax.broadcasted_iota(jnp.int32, (n, 2 * n), 1)
    factor_t[...] = jnp.where(row_id + n == lane_id, 1.0, 0.0)
    factor_t[:, :n] = matrix
    work = [factor_t[g * 8 : (g + 1) * 8, :] for g in range(n // 8)]
    sub = lax.broadcasted_iota(jnp.int32, (8, 1), 0)
    done = 0
    for j in range(0, n, 2):
        g, s = divmod(j, 8)
        top = work[g][s : s + 1, :]
        low = work[g][s + 1 : s + 2, :]
        a, b, c = top[:, j : j + 1], top[:, j + 1 : j + 2], low[:, j + 1 : j + 2]
        scale = 1.0 / (a * c - b * b)
        new_top = (c * top - b * low) * scale
        new_low = (a * low - b * top) * scale
        for i in range(g, n // 8):
            left, right = work[i][:, j : j + 1], work[i][:, j + 1 : j + 2]
            if i == g:
                left = jnp.where(sub > s + 1, left, 0.0)
                right = jnp.where(sub > s + 1, right, 0.0)
            work[i] = work[i] - (left * new_top + right * new_low)
        goal = len(beside) * (j + 2) // n
        while done < goal:
            beside[done]()
            done += 1
    reduced = jnp.concatenate(work, 0)
    above = pltpu.roll(reduced, 1, 0)
    odd = lax.broadcasted_iota(jnp.int32, (n, 1), 0) % 2 == 1
    pick = lambda values, where: jnp.sum(jnp.where(where, values, 0.0), 1, keepdims=True)
    under = pick(above, lane_id == row_id) / jnp.where(odd, pick(above, lane_id + 1 == row_id), 1.0)
    reduced = reduced - jnp.where(odd, under, 0.0) * above
    diagonal = pick(reduced, lane_id == row_id)
    scale = lax.rsqrt(diagonal)
    scale = scale * (1.5 - 0.5 * diagonal * scale * scale)
    reduced = reduced * scale
    factor_t[...] = reduced
    upper = jnp.where(row_id <= lane_id, reduced, 0.0)
    coef[2] = upper.T[:n, :]
    return factor_t[:, n:]


def thirds(values):
    high = values.astype(BF16)
    rest = values - high.astype(F32)
    middle = rest.astype(BF16)
    return jnp.concatenate([high, middle, (rest - middle.astype(F32)).astype(BF16)], 0)


def unpack(lines, received, target, lanes, offset):
    for s in range(received.shape[0]):
        if s * lines < target.shape[0]:
            target[s * lines : (s + 1) * lines, lanes] = received[s, offset : offset + lines]


def congruent(factor, matrix):
    return exact(factor, exact_rows(matrix, factor))


def settle(total, gram, inner, lag, both, beside, coef, factor_t):
    n = gram.shape[0] // 2
    scale = 1.0 / total
    pull = lag[:, :n]
    aa = congruent(pull, gram[:n, :n] * scale)
    cc = congruent(pull, gram[n:, n:] * scale)
    self_ = both[:, :n]
    prev = both[:, n:]
    cp = inner[:, :n]
    pp = inner[:, n:]
    coef[0] = self_
    coef[1] = prev
    t_c = self_ - exact(self_, cc) - exact_rows(prev, cp)
    t_p = prev - exact(self_, cp) - exact(prev, pp)
    t_a = aa - exact_rows(self_, self_) - exact_rows(prev, prev)
    matrix = t_a - exact_rows(t_c, self_) - exact_rows(t_p, prev)
    inverse = eliminate(0.5 * (matrix + matrix.T), beside, coef, factor_t)
    return inverse, t_c, cc


def blend(total, gram, lag, both, mix):
    n = gram.shape[0] // 2
    scale = 1.0 / total
    pull, square = lag[:, :n], lag[:, n:]
    crossed = gram[:n, n:] * scale
    prev = exact(pull, gram[n:, :n] * scale)
    mix[:, :n] = pull
    mix[:, n : 2 * n] = -exact(pull, exact(crossed, square))
    mix[:, 2 * n :] = -prev
    both[:, :n] = congruent(pull, crossed)
    both[:, n:] = prev


def factor_kernel(total, gram, inner, lag, both, lag_out, inner_out, coef, factor_t):
    n = gram.shape[0] // 2
    inverse, t_c, cc = settle(total, gram, inner, lag, both, [], coef, factor_t)
    lag_out[:, :n] = inverse
    lag_out[:, n:] = exact(inverse.T, inverse)
    inner_out[:, :n] = exact(inverse, t_c)
    inner_out[:, n:] = cc


def factor(total, gram, inner, lag, both):
    n = gram.shape[0] // 2
    sds = jax.ShapeDtypeStruct
    return pl.pallas_call(
        functools.partial(factor_kernel, total),
        in_specs=[VMEM] * 4,
        out_specs=[VMEM] * 3,
        out_shape=[sds((n, 2 * n), F32), sds((n, 2 * n), F32), sds((3, n, n), F32)],
        scratch_shapes=[pltpu.VMEM((n, 2 * n), F32)],
        compiler_params=pltpu.CompilerParams(vmem_limit_bytes=LIMIT),
        cost_estimate=pl.CostEstimate(flops=100_000_000, bytes_accessed=10_000_000, transcendentals=0),
        name="factor",
    )(gram, inner, lag, both)


def thirds(values):
    high = values.astype(BF16)
    rest = values - high.astype(F32)
    return jnp.concatenate([high, *halves(rest)], 0)


def unpack(lines, received, target, lanes, offset):
    for s in range(received.shape[0]):
        if s * lines < target.shape[0]:
            target[s * lines : (s + 1) * lines, lanes] = received[s, offset : offset + lines]


def advance_kernel(mode, total, peers, *refs):
    it = iter(refs)
    take = lambda k: [next(it) for _ in range(k)]
    ids, rates = take(2)
    if mode == "first":
        arrived, below, above, held_in = take(4)
        held = [held_in]
    else:
        received, pressed, lag, edges, wet_held = take(5)
        held = take(3)
    pick, place, mixed_in, spread_in = take(4)
    (applied_out,) = take(1)
    if mode == "last":
        (gram_s,) = take(1)
    else:
        edges_out, wet_out, send = take(3)
    if mode != "first":
        residual_out, previous_out, both, gram_in = take(4)
    extended, terms, stack, fresh, mixed, spread, edge_in, sems = take(8)
    if mode != "last":
        gram_s, rest = take(2)
    if mode != "first":
        (mix,) = take(1)

    n = fresh.shape[0]
    width = fresh.shape[1]
    size = edge_in.shape[1] // 2
    count = width // size
    glines = -(-2 * n // peers)
    hlines = -(-n // peers)
    loads = []
    for k, source in enumerate(held):
        first = k * n if mode != "first" else n
        loads.append(pltpu.make_async_copy(source, stack.at[pl.ds(first, n)], sems.at[k]))
    load_mixed = pltpu.make_async_copy(mixed_in, mixed, sems.at[3])
    for copy in loads + [load_mixed]:
        copy.start()
    if mode != "last":
        load_spread = pltpu.make_async_copy(spread_in, spread, sems.at[4])
        load_spread.start()

    stores = []
    if mode == "first":
        edge = jnp.concatenate([below[...], above[...]], 1)
        summed = jnp.sum(arrived[...].astype(F32), 0)
        wet = jnp.concatenate([summed[:, :n], summed[:, n:]], 0)
        edges_out[:n, :] = edge
        edges_out[n:, :] = jnp.zeros_like(edge)
        wet_out[:, :n] = wet
        wet_out[:, n:] = jnp.zeros_like(wet)
        for copy in loads:
            copy.wait()
        residual = stack[n : 2 * n, :]
    else:
        unpack(glines, received, gram_in, slice(None), 0)
        unpack(hlines, received, edge_in.at[pl.ds(0, n)], slice(0, size), glines)
        unpack(hlines, received, edge_in.at[pl.ds(0, n)], slice(size, 2 * size), glines + hlines)
        edge_in[n:, :] = edges[...]
        blend(total, gram_in, lag, both, mix)
        pull = lag[:, :n]
        edge = exact(mix[...], edge_in[...])
        summed = pressed[...]
        wet = exact_rows(jnp.concatenate([summed[:, :n], summed[:, n:]], 0), pull)
        wet = wet + exact_rows(wet_held[...], mix[:, n:])
        if mode != "last":
            edges_out[:n, :] = edge
            edges_out[n:, :] = exact(pull, edges[:n, :])
            wet_out[:, :n] = wet
            wet_out[:, n:] = exact_rows(wet_held[:, :n], pull)
        for copy in loads:
            copy.wait()
        residual = exact(mix[...], stack[...])
        previous = exact(pull, stack[n : 2 * n, :])
        stack[:n, :] = residual
        stack[n : 2 * n, :] = previous
        stores.append(pltpu.make_async_copy(stack.at[pl.ds(0, n)], residual_out, sems.at[0]))
        stores.append(pltpu.make_async_copy(stack.at[pl.ds(n, n)], previous_out, sems.at[1]))
        for copy in stores:
            copy.start()
        terms[4 * n : 5 * n, :], terms[5 * n :, :] = halves(previous)
    high, low = halves(residual)
    terms[2 * n : 3 * n, :] = high
    terms[3 * n : 4 * n, :] = low
    for i in range(count):
        extended[i] = high[:, i * size : (i + 1) * size]
    extended[count] = edge[:, :size].astype(BF16)
    extended[count + 1] = edge[:, size:].astype(BF16)
    force = thirds(wet.T * rates[1])
    load_mixed.wait()
    for i in range(count):
        picked = jnp.concatenate([extended[ids[i, k]] for k in range(ids.shape[1])], 1)
        pair = jnp.dot(picked, mixed[i], preferred_element_type=F32)
        lanes = slice(i * size, (i + 1) * size)
        added = jnp.dot(force, place[:, lanes], preferred_element_type=F32)
        applied = pair[:, :size] + pair[:, size:] - (added[:n] + added[n : 2 * n] + added[2 * n :])
        fresh[:, lanes] = applied
        terms[:n, lanes], terms[n : 2 * n, lanes] = halves(applied)
    stores.append(pltpu.make_async_copy(fresh, applied_out, sems.at[2]))
    stores[-1].start()

    known = 4 * n if mode == "first" else 6 * n
    products = rows(terms[: 2 * n, :], terms[:known, :])
    products = products[:n] + products[n:]
    gram_s[:n, :n] = products[:, :n] + products[:, n : 2 * n]
    gram_s[:n, n:] = products[:, 2 * n : 3 * n] + products[:, 3 * n : 4 * n]
    if mode == "first":
        gram_s[n:, :n] = jnp.zeros((n, n), F32)
    else:
        gram_s[n:, :n] = products[:, 4 * n : 5 * n] + products[:, 5 * n :]
    squares = rows(terms[2 * n : 4 * n, :], terms[2 * n : 4 * n, :])
    squares = squares[:n] + squares[n:]
    gram_s[n:, n:] = squares[:, :n] + squares[:, n:]
    if mode != "last":
        rim = jnp.dot(terms[: 2 * n, :], pick[...], preferred_element_type=F32)
        edge_in[:n, :size] = rim[:n] + rim[n:]
        load_spread.wait()
        wets = wet_out.shape[0] // 2
        middle = spread.shape[0] // 2
        tops = rows(spread[:middle], terms[: 2 * n, :])
        tops = tops + pltpu.roll(tops, n, 1)
        ends = rows(spread[middle:], terms[: 2 * n, :])
        ends = ends + pltpu.roll(ends, n, 1)
        lane = lax.broadcasted_iota(jnp.int32, tops.shape, 1)
        send[:, :wets, :] = jnp.where(lane < n, tops, ends).astype(BF16).reshape(peers, wets, 2 * n)
        left = gram_s[...]
        offset = 0
        for _ in range(3):
            term = left.astype(BF16).astype(F32)
            left = left - term
            gram_s[...] = term
            for d in range(peers):
                if d * glines < 2 * n:
                    rest[d, offset : offset + glines] = gram_s[d * glines : (d + 1) * glines, :]
            offset += glines
        left = edge_in[:n, :size]
        for _ in range(2):
            term = left.astype(BF16).astype(F32)
            left = left - term
            edge_in[:n, :size] = term
            for d in range(peers):
                if d * hlines < n:
                    rest[d, offset : offset + hlines] = edge_in[d * hlines : (d + 1) * hlines, :size]
                else:
                    rest[d, offset : offset + hlines] = jnp.zeros((hlines, size), F32)
            offset += hlines
        if offset < rest.shape[1]:
            rest[:, offset:, :] = jnp.zeros((peers, rest.shape[1] - offset, 2 * n), F32)
        send[:, wets:, :] = rest[...].astype(BF16)
    for copy in stores:
        copy.wait()


def advance(mode, total, peers, ids, rates, state, fixed):
    mixed, pick, place, spread = fixed
    width, size = pick.shape
    wets = place.shape[0]
    vectors = state[-1].shape[0]
    extra = 3 * -(-2 * vectors // peers) + 2 * -(-vectors // peers)
    extra = -(-extra // 16) * 16
    sds = jax.ShapeDtypeStruct
    block = pltpu.HBM((vectors, width), F32)
    small = sds((2 * vectors, 2 * vectors), F32)
    shapes, specs = [block], [HBM]
    if mode == "last":
        shapes += [small]
        specs += [VMEM]
    else:
        shapes += [
            sds((2 * vectors, 2 * size), F32),
            sds((wets, 2 * vectors), F32),
            sds((peers, wets // 2 + extra, 2 * vectors), BF16),
        ]
        specs += [VMEM] * 3
    if mode != "first":
        shapes += [block, block, sds((vectors, 2 * vectors), F32), small]
        specs += [HBM, HBM, VMEM, VMEM]
    scratch = [
        pltpu.VMEM((width // size + 2, vectors, size), BF16),
        pltpu.VMEM((6 * vectors, width), BF16),
        pltpu.VMEM((3 * vectors, width), F32),
        pltpu.VMEM((vectors, width), F32),
        pltpu.VMEM(mixed.shape, BF16),
        pltpu.VMEM(spread.shape if mode != "last" else (16, 128), BF16),
        pltpu.VMEM((3 * vectors, 2 * size), F32),
        pltpu.SemaphoreType.DMA((5,)),
    ]
    if mode != "last":
        scratch += [pltpu.VMEM(small.shape, F32), pltpu.VMEM((peers, extra, 2 * vectors), F32)]
    if mode != "first":
        scratch += [pltpu.VMEM((vectors, 3 * vectors), F32)]
    held = 1 if mode == "first" else 3
    return pl.pallas_call(
        functools.partial(advance_kernel, mode, total, peers),
        in_specs=[SMEM, SMEM] + [VMEM] * (len(state) - held) + [HBM] * held + [VMEM, VMEM, HBM, HBM],
        out_specs=specs,
        out_shape=shapes,
        scratch_shapes=scratch,
        compiler_params=pltpu.CompilerParams(vmem_limit_bytes=LIMIT),
        name="advance_" + mode,
    )(ids, rates, *state, pick, place, mixed, spread)


def route_kernel(vectors, wets, received, pressed, send, rest):
    peers = received.shape[0]
    glines = -(-2 * vectors // peers)
    hlines = -(-vectors // peers)
    pressed[...] = jnp.sum(received[:, :wets, :].astype(F32), 0)
    rest[...] = received[:, wets:, :].astype(F32)
    sums = jnp.sum(rest[...], 0)
    mine = sums[:glines] + sums[glines : 2 * glines] + sums[2 * glines : 3 * glines]
    edge = 3 * glines
    nothing = jnp.zeros((hlines, 2 * vectors), F32)

    def halo(t):
        if not 0 <= t < peers:
            return nothing
        return rest[t, edge : edge + hlines] + rest[t, edge + hlines : edge + 2 * hlines]

    send[...] = jnp.zeros(send.shape, F32)
    for t in range(peers):
        send[t, :glines] = mine
        send[t, glines : glines + hlines] = halo(t - 1)
        send[t, glines + hlines : glines + 2 * hlines] = halo(t + 1)


def route(vectors, wets, received):
    peers, lines, lanes = received.shape
    return pl.pallas_call(
        functools.partial(route_kernel, vectors, wets),
        in_specs=[VMEM],
        out_specs=[VMEM] * 2,
        out_shape=[
            jax.ShapeDtypeStruct((wets, 2 * vectors), F32),
            jax.ShapeDtypeStruct((peers, 8, 2 * vectors), F32),
        ],
        scratch_shapes=[pltpu.VMEM((peers, lines - wets, lanes), F32)],
        compiler_params=pltpu.CompilerParams(vmem_limit_bytes=LIMIT),
        name="route",
    )(received)


def finish_kernel(total, gram, inner, lag, applied, residual, previous, out, coef, factor_t, mix, both, stack, sems):
    n = inner.shape[0]
    loads = []
    for k, source in enumerate((applied, residual, previous)):
        loads.append(pltpu.make_async_copy(source, stack.at[pl.ds(k * n, n)], sems.at[k]))
        loads[-1].start()
    blend(total, gram, lag, both, mix)
    for copy in loads:
        copy.wait()

    def next_residual():
        stack[:n, :] = exact(mix[...], stack[...])

    inverse, _, _ = settle(total, gram, inner, lag, both, [next_residual], coef, factor_t)
    out[...] = exact(inverse, stack[:n, :])


def finish(total, gram, inner, lag, held):
    vectors, width = held[0].shape
    return pl.pallas_call(
        functools.partial(finish_kernel, total),
        in_specs=[VMEM] * 3 + [HBM] * 3,
        out_specs=[VMEM] * 2,
        out_shape=[
            jax.ShapeDtypeStruct((vectors, width), F32),
            jax.ShapeDtypeStruct((3, vectors, vectors), F32),
        ],
        scratch_shapes=[
            pltpu.VMEM((vectors, 2 * vectors), F32),
            pltpu.VMEM((vectors, 3 * vectors), F32),
            pltpu.VMEM((vectors, 2 * vectors), F32),
            pltpu.VMEM((3 * vectors, width), F32),
            pltpu.SemaphoreType.DMA((3,)),
        ],
        compiler_params=pltpu.CompilerParams(vmem_limit_bytes=LIMIT),
        name="finish",
    )(gram, inner, lag, *held)


def local(n_row, n_col, start_block, struct_blocks, block_ids, rim_rows, wet_slots, wet_counts, added_mass, rates):
    peers = n_row * n_col
    vectors, width = start_block.shape
    total = float(width * peers)
    wcap = wet_slots.shape[0]
    wets = added_mass.shape[0] // n_row

    def exchange(parts):
        return lax.all_to_all(parts, AXES, 0, 0, tiled=True)

    def neighbours(halo):
        up = [(i, i + 1) for i in range(peers - 1)]
        down = [(i + 1, i) for i in range(peers - 1)]
        return lax.ppermute(halo, AXES, up), lax.ppermute(halo, AXES, down)

    def summed(gram):
        lines = gram.shape[0] // peers
        mine = exchange(gram.reshape(peers, lines, -1)).sum(0)
        return exchange(jnp.broadcast_to(mine[None], (peers, *mine.shape))).reshape(gram.shape)

    blocks = added_mass.reshape(-1, n_col, wcap).transpose(1, 0, 2)
    mass = lax.all_to_all(blocks, "col", 0, 0, tiled=True)
    mass = mass.reshape(n_col, n_row, 2, wets // 2, wcap)
    mixed, pick, place, halo = combine(
        rates, rim_rows[None, :], wet_slots[:wets, None], start_block, struct_blocks
    )
    below, above = neighbours(halo)
    spread, part = spread_mass(wet_counts, wet_slots[None, :], start_block, mass, below, above)
    mixed, spread = in_hbm(mixed), in_hbm(spread)
    fixed = (mixed, pick, place, spread)
    arrived = exchange(part.reshape(peers, wets // 2, 2 * vectors))
    step = functools.partial(advance, total=total, peers=peers, ids=block_ids, rates=rates, fixed=fixed)
    applied, edges, wet_held, send = step("first", state=(arrived, below, above, in_hbm(start_block)))
    inner = jnp.zeros((vectors, 2 * vectors), F32)
    unit = jnp.eye(vectors, dtype=F32)
    lag = jnp.concatenate([unit, unit], 1)
    residual, previous = start_block, jnp.zeros_like(start_block)
    coefficients = []
    for number in range(1, STEPS):
        pressed, again = route(vectors, wets // 2, exchange(send))
        received = exchange(again)
        state = (received, pressed, lag, edges, wet_held, in_hbm(applied), in_hbm(residual), in_hbm(previous))
        if number < STEPS - 1:
            applied, edges, wet_held, send, residual, previous, both, gram = step("mid", state=state)
        else:
            applied, products, residual, previous, both, gram = step("last", state=state)
        lag, inner, coef = factor(total, gram, inner, lag, both)
        coefficients.append(coef)
    final, coef = finish(total, summed(products), inner, lag, (in_hbm(applied), in_hbm(residual), in_hbm(previous)))
    coefficients.append(coef)
    return final, jnp.stack(coefficients)


def solution(mesh):
    return jax.shard_map(
        functools.partial(local, mesh.shape["row"], mesh.shape["col"]),
        mesh=mesh,
        in_specs=(
            P(None, AXES),
            P(None, AXES, None, None, None),
            P(AXES, None),
            P(AXES),
            P(AXES),
            P(AXES),
            P("col", "row"),
            P(),
        ),
        out_specs=(P(None, AXES), P()),
        check_vma=False,
    )
```

```python
import functools

import jax
import jax.numpy as jnp
from jax import lax
from jax.experimental import pallas as pl
from jax.experimental.pallas import tpu as pltpu
from jax.sharding import PartitionSpec as P

STEPS = 6
AXES = ("row", "col")
VMEM = pl.BlockSpec(memory_space=pltpu.VMEM)
SMEM = pl.BlockSpec(memory_space=pltpu.SMEM)
HBM = pl.BlockSpec(memory_space=pltpu.HBM)
ANY = pl.BlockSpec(memory_space=pl.ANY)
F32 = jnp.float32
BF16 = jnp.bfloat16
LIMIT = 40 * 1024 * 1024


def exact(left, right):
    return lax.dot_general(
        left, right, (((1,), (0,)), ((), ())), precision=lax.Precision.HIGHEST, preferred_element_type=F32
    )


def exact_rows(left, right):
    return lax.dot_general(
        left, right, (((1,), (1,)), ((), ())), precision=lax.Precision.HIGHEST, preferred_element_type=F32
    )


def rows(left, right):
    return lax.dot_general(left, right, (((1,), (1,)), ((), ())), preferred_element_type=F32)


def in_hbm(values):
    return pltpu.with_memory_space_constraint(values, pltpu.HBM)


def halves(values):
    high = values.astype(BF16)
    return high, (values - high.astype(F32)).astype(BF16)


def combine_kernel(rates, rim, wet, start, blocks, mixed, pick, place, halo):
    size = blocks.shape[-1]
    for k in range(blocks.shape[2]):
        whole = (
            blocks[0, 0, k].astype(F32)
            + rates[0] * blocks[1, 0, k].astype(F32)
            - rates[1] * blocks[2, 0, k].astype(F32)
        ).T
        high = whole.astype(BF16)
        mixed[0, k * size : (k + 1) * size, :size] = high
        mixed[0, k * size : (k + 1) * size, size:] = (whole - high.astype(F32)).astype(BF16)

    @pl.when(pl.program_id(0) == 0)
    def _():
        index = lax.broadcasted_iota(jnp.int32, pick.shape, 0)
        pick[...] = jnp.where(index == rim[...], 1.0, 0.0).astype(BF16)
        index = lax.broadcasted_iota(jnp.int32, place.shape, 1)
        place[...] = jnp.where(index == wet[...], 1.0, 0.0).astype(BF16)
        high, low = halves(start[...])
        halo[...] = jnp.dot(high, pick[...], preferred_element_type=F32) + jnp.dot(
            low, pick[...], preferred_element_type=F32
        )


def combine(rates, rim, wet, start, blocks):
    _, count, nnz, size, _ = blocks.shape
    vectors, width = start.shape
    whole = lambda shape: pl.BlockSpec(shape, lambda i: (0,) * len(shape))
    return pl.pallas_call(
        combine_kernel,
        grid=(count,),
        in_specs=[
            SMEM,
            whole(rim.shape),
            whole(wet.shape),
            whole(start.shape),
            pl.BlockSpec((3, 1, nnz, size, size), lambda i: (0, i, 0, 0, 0)),
        ],
        out_specs=[
            pl.BlockSpec((1, nnz * size, 2 * size), lambda i: (i, 0, 0)),
            whole((width, rim.shape[1])),
            whole((wet.shape[0], width)),
            whole((vectors, rim.shape[1])),
        ],
        out_shape=[
            pltpu.HBM((count, nnz * size, 2 * size), BF16),
            jax.ShapeDtypeStruct((width, rim.shape[1]), BF16),
            jax.ShapeDtypeStruct((wet.shape[0], width), BF16),
            jax.ShapeDtypeStruct((vectors, rim.shape[1]), F32),
        ],
        compiler_params=pltpu.CompilerParams(vmem_limit_bytes=LIMIT),
        name="combine",
    )(rates, rim, wet, start, blocks)


def spread_kernel(count, slots, start, mass, _ready, spread, part, own, total):
    n_col, n_row, _, half, wcap = mass.shape
    size = n_col * half
    step = pl.program_id(0)

    @pl.when(step == 0)
    def _():
        for h in range(2):
            for r in range(n_row):
                first = (h * n_row + r) * size
                own[first : first + size] = mass[:, r, h].reshape(size, wcap)
        total[...] = jnp.zeros_like(total)

    slot = lax.broadcasted_iota(jnp.int32, slots.shape, 1)
    live = jnp.where(slot < count[0], slots[...], -1)
    columns, vectors = spread.shape[1], start.shape[0]
    index = lax.broadcasted_iota(jnp.int32, (columns, wcap), 0) + step * columns
    onehot = jnp.where(index == live, 1.0, 0.0).astype(BF16)
    block = rows(own[...], onehot).astype(BF16)
    spread[...] = block
    total[...] += rows(block, start[...].astype(BF16))

    @pl.when(step == pl.num_programs(0) - 1)
    def _():
        part[:, :vectors] = total[: n_row * size].astype(BF16)
        part[:, vectors:] = total[n_row * size :].astype(BF16)


def spread_mass(count, slots, start, mass, *ready):
    n_col, n_row, _, half, wcap = mass.shape
    vectors, width = start.shape
    size = n_col * n_row * half
    columns = min(width, 512)
    return pl.pallas_call(
        spread_kernel,
        grid=(width // columns,),
        in_specs=[
            SMEM,
            pl.BlockSpec(slots.shape, lambda i: (0, 0)),
            pl.BlockSpec((vectors, columns), lambda i: (0, i)),
            pl.BlockSpec(mass.shape, lambda i: (0,) * 5),
            HBM,
        ],
        out_specs=[
            pl.BlockSpec((2 * size, columns), lambda i: (0, i)),
            pl.BlockSpec((size, 2 * vectors), lambda i: (0, 0)),
        ],
        out_shape=[
            pltpu.HBM((2 * size, width), BF16),
            jax.ShapeDtypeStruct((size, 2 * vectors), BF16),
        ],
        scratch_shapes=[pltpu.VMEM((2 * size, wcap), BF16), pltpu.VMEM((2 * size, vectors), F32)],
        compiler_params=pltpu.CompilerParams(vmem_limit_bytes=LIMIT),
        name="spread",
    )(count, slots, start, mass, *ready)


def halve_columns(top, low, s):
    a, b, c = top[:, s : s + 1], top[:, s + 1 : s + 2], low[:, s + 1 : s + 2]
    scale = 1.0 / (a * c - b * b)
    return (c * top - b * low) * scale, (a * low - b * top) * scale


def eliminate(matrix, beside, coef, factor_t):
    n = matrix.shape[0]
    groups = n // 8
    row_id = lax.broadcasted_iota(jnp.int32, (n, 2 * n), 0)
    lane_id = lax.broadcasted_iota(jnp.int32, (n, 2 * n), 1)
    factor_t[...] = jnp.where(row_id + n == lane_id, 1.0, 0.0)
    factor_t[:, :n] = matrix
    sub = lax.broadcasted_iota(jnp.int32, (8, 1), 0)
    if beside:
        work = [factor_t[g * 8 : (g + 1) * 8, :] for g in range(groups)]
        done = 0
        for j in range(0, n, 2):
            g, s = divmod(j, 8)
            new_top, new_low = halve_columns(work[g][s : s + 1, :], work[g][s + 1 : s + 2, :], j)
            for i in range(g, groups):
                left, right = work[i][:, j : j + 1], work[i][:, j + 1 : j + 2]
                if i == g:
                    left = jnp.where(sub > s + 1, left, 0.0)
                    right = jnp.where(sub > s + 1, right, 0.0)
                work[i] = work[i] - (left * new_top + right * new_low)
            goal = len(beside) * (j + 2) // n
            while done < goal:
                beside[done]()
                done += 1
        reduced = jnp.concatenate(work, 0)
    else:

        def group(step, _):
            work = [factor_t[g * 8 : (g + 1) * 8, :] for g in range(groups)]
            for s in range(0, 8, 2):
                new_top, new_low = halve_columns(work[0][s : s + 1, :], work[0][s + 1 : s + 2, :], s)
                for i in range(groups):
                    left, right = work[i][:, s : s + 1], work[i][:, s + 1 : s + 2]
                    keep = sub > s + 1 if i == 0 else step + i < groups
                    update = left * new_top + right * new_low
                    work[i] = work[i] - jnp.where(keep, update, 0.0)
            for i in range(groups):
                target = (i - 1) % groups
                factor_t[target * 8 : (target + 1) * 8, :] = pltpu.roll(work[i], 2 * n - 8, 1)
            return 0

        lax.fori_loop(0, groups, group, 0)
        reduced = pltpu.roll(factor_t[...], n, 1)
    above = pltpu.roll(reduced, 1, 0)
    odd = lax.broadcasted_iota(jnp.int32, (n, 1), 0) % 2 == 1
    pick = lambda values, where: jnp.sum(jnp.where(where, values, 0.0), 1, keepdims=True)
    under = pick(above, lane_id == row_id) / jnp.where(odd, pick(above, lane_id + 1 == row_id), 1.0)
    reduced = reduced - jnp.where(odd, under, 0.0) * above
    diagonal = pick(reduced, lane_id == row_id)
    scale = lax.rsqrt(diagonal)
    scale = scale * (1.5 - 0.5 * diagonal * scale * scale)
    reduced = reduced * scale
    factor_t[...] = reduced
    upper = jnp.where(row_id <= lane_id, reduced, 0.0)
    coef[2] = upper.T[:n, :]
    return factor_t[:, n:]


def congruent(factor, matrix):
    return exact(factor, exact_rows(matrix, factor))


def settle(total, gram, inner, lag, both, beside, coef, factor_t):
    n = gram.shape[0] // 2
    scale = 1.0 / total
    pull = lag[:, :n]
    aa = congruent(pull, gram[:n, :n] * scale)
    cc = congruent(pull, gram[n:, n:] * scale)
    self_ = both[:, :n]
    prev = both[:, n:]
    cp = inner[:, :n]
    pp = inner[:, n:]
    coef[0] = self_
    coef[1] = prev
    t_c = self_ - exact(self_, cc) - exact_rows(prev, cp)
    t_p = prev - exact(self_, cp) - exact(prev, pp)
    t_a = aa - exact_rows(self_, self_) - exact_rows(prev, prev)
    matrix = t_a - exact_rows(t_c, self_) - exact_rows(t_p, prev)
    inverse = eliminate(0.5 * (matrix + matrix.T), beside, coef, factor_t)
    return inverse, t_c, cc


def blend(total, gram, lag, both, mix):
    n = gram.shape[0] // 2
    scale = 1.0 / total
    pull, square = lag[:, :n], lag[:, n:]
    crossed = gram[:n, n:] * scale
    prev = exact(pull, gram[n:, :n] * scale)
    mix[:, :n] = pull
    mix[:, n : 2 * n] = -exact(pull, exact(crossed, square))
    mix[:, 2 * n :] = -prev
    both[:, :n] = congruent(pull, crossed)
    both[:, n:] = prev


def factor_kernel(total, gram, inner, lag, both, lag_out, inner_out, coef, factor_t):
    n = gram.shape[0] // 2
    inverse, t_c, cc = settle(total, gram, inner, lag, both, [], coef, factor_t)
    lag_out[:, :n] = inverse
    lag_out[:, n:] = exact(inverse.T, inverse)
    inner_out[:, :n] = exact(inverse, t_c)
    inner_out[:, n:] = cc


def factor(total, gram, inner, lag, both):
    n = gram.shape[0] // 2
    sds = jax.ShapeDtypeStruct
    return pl.pallas_call(
        functools.partial(factor_kernel, total),
        in_specs=[VMEM] * 4,
        out_specs=[VMEM] * 3,
        out_shape=[sds((n, 2 * n), F32), sds((n, 2 * n), F32), sds((3, n, n), F32)],
        scratch_shapes=[pltpu.VMEM((n, 2 * n), F32)],
        compiler_params=pltpu.CompilerParams(vmem_limit_bytes=LIMIT),
        cost_estimate=pl.CostEstimate(flops=100_000_000, bytes_accessed=10_000_000, transcendentals=0),
        name="factor",
    )(gram, inner, lag, both)


def thirds(values):
    high = values.astype(BF16)
    rest = values - high.astype(F32)
    return jnp.concatenate([high, *halves(rest)], 0)


def unpack(lines, received, target, lanes, offset):
    for s in range(received.shape[0]):
        if s * lines < target.shape[0]:
            target[s * lines : (s + 1) * lines, lanes] = received[s, offset : offset + lines]


def place_columns(extended, block, edge):
    size = extended.shape[2]
    count = extended.shape[0] - 2
    for i in range(count):
        extended[i] = block[:, i * size : (i + 1) * size]
    extended[count] = edge[:, :size].astype(BF16)
    extended[count + 1] = edge[:, size:].astype(BF16)


def block_row(ids, extended, mixed, i):
    picked = jnp.concatenate([extended[ids[i, k]] for k in range(ids.shape[1])], 1)
    pair = jnp.dot(picked, mixed[i], preferred_element_type=F32)
    size = pair.shape[1] // 2
    return pair[:, :size] + pair[:, size:]


def prepare_kernel(ids, below, above, start, mixed, out, extended):
    size = below.shape[1]
    place_columns(extended, start[...].astype(BF16), jnp.concatenate([below[...], above[...]], 1))
    for i in range(out.shape[1] // size):
        out[:, i * size : (i + 1) * size] = block_row(ids, extended, mixed, i)


def prepare(ids, below, above, start, mixed):
    vectors, width = start.shape
    size = below.shape[1]
    return pl.pallas_call(
        prepare_kernel,
        in_specs=[SMEM] + [VMEM] * 4,
        out_specs=VMEM,
        out_shape=pltpu.HBM((vectors, width), F32),
        scratch_shapes=[pltpu.VMEM((width // size + 2, vectors, size), BF16)],
        compiler_params=pltpu.CompilerParams(vmem_limit_bytes=LIMIT),
        name="prepare",
    )(ids, below, above, start, mixed)


def advance_kernel(mode, total, peers, *refs):
    it = iter(refs)
    take = lambda k: [next(it) for _ in range(k)]
    ids, rates = take(2)
    if mode == "first":
        arrived, below, above = take(3)
        held = take(2)
    else:
        received, pressed, lag, edges, wet_held = take(5)
        held = take(3)
    pick, place, mixed_in, spread_in = take(4)
    (applied_out,) = take(1)
    if mode == "last":
        (gram_s,) = take(1)
    else:
        edges_out, wet_out, send = take(3)
    if mode != "first":
        residual_out, previous_out, both, gram_in = take(4)
    extended, terms, stack, fresh, mixed, spread, edge_in, sems = take(8)
    if mode != "last":
        gram_s, rest = take(2)
    if mode != "first":
        (mix,) = take(1)

    n = fresh.shape[0]
    width = fresh.shape[1]
    size = edge_in.shape[1] // 2
    count = width // size
    glines = -(-2 * n // peers)
    hlines = -(-n // peers)
    loads = []
    for k, source in enumerate(held):
        loads.append(pltpu.make_async_copy(source, stack.at[pl.ds(k * n, n)], sems.at[k]))
        loads[-1].start()
    if mode != "first":
        load_mixed = pltpu.make_async_copy(mixed_in, mixed, sems.at[3])
        load_mixed.start()
    load_spread = []
    if mode != "last":
        for h in range(2):
            part = spread_in.at[pl.ds(h * spread.shape[1], spread.shape[1])]
            load_spread.append(pltpu.make_async_copy(part, spread.at[h], sems.at[4 + h]))
            load_spread[-1].start()

    stores = []
    if mode == "first":
        edge = jnp.concatenate([below[...], above[...]], 1)
        summed = jnp.sum(arrived[...].astype(F32), 0)
        wet = jnp.concatenate([summed[:, :n], summed[:, n:]], 0)
        edges_out[:n, :] = edge
        edges_out[n:, :] = jnp.zeros_like(edge)
        wet_out[:, :n] = wet
        wet_out[:, n:] = jnp.zeros_like(wet)
        for copy in loads:
            copy.wait()
        residual = stack[n : 2 * n, :]
    else:
        unpack(glines, received, gram_in, slice(None), 0)
        unpack(hlines, received, edge_in.at[pl.ds(0, n)], slice(0, size), glines)
        unpack(hlines, received, edge_in.at[pl.ds(0, n)], slice(size, 2 * size), glines + hlines)
        edge_in[n:, :] = edges[...]
        blend(total, gram_in, lag, both, mix)
        pull = lag[:, :n]
        edge = exact(mix[...], edge_in[...])
        summed = pressed[...]
        wet = exact_rows(jnp.concatenate([summed[:, :n], summed[:, n:]], 0), pull)
        wet = wet + exact_rows(wet_held[...], mix[:, n:])
        if mode != "last":
            edges_out[:n, :] = edge
            edges_out[n:, :] = exact(pull, edges[:n, :])
            wet_out[:, :n] = wet
            wet_out[:, n:] = exact_rows(wet_held[:, :n], pull)
        for copy in loads:
            copy.wait()
        residual = exact(mix[...], stack[...])
        previous = exact(pull, stack[n : 2 * n, :])
        stack[:n, :] = residual
        stack[n : 2 * n, :] = previous
        stores.append(pltpu.make_async_copy(stack.at[pl.ds(0, n)], residual_out, sems.at[0]))
        stores.append(pltpu.make_async_copy(stack.at[pl.ds(n, n)], previous_out, sems.at[1]))
        for copy in stores:
            copy.start()
        terms[4 * n : 5 * n, :], terms[5 * n :, :] = halves(previous)
    high, low = halves(residual)
    terms[2 * n : 3 * n, :] = high
    terms[3 * n : 4 * n, :] = low
    force = thirds(wet.T * rates[1])
    if mode != "first":
        place_columns(extended, high, edge)
        load_mixed.wait()
    for i in range(count):
        lanes = slice(i * size, (i + 1) * size)
        added = jnp.dot(force, place[:, lanes], preferred_element_type=F32)
        applied = stack[:n, lanes] if mode == "first" else block_row(ids, extended, mixed, i)
        applied = applied - (added[:n] + added[n : 2 * n] + added[2 * n :])
        fresh[:, lanes] = applied
        terms[:n, lanes], terms[n : 2 * n, lanes] = halves(applied)
    stores.append(pltpu.make_async_copy(fresh, applied_out, sems.at[2]))
    stores[-1].start()

    known = 4 * n if mode == "first" else 6 * n
    products = rows(terms[: 2 * n, :], terms[:known, :])
    products = products[:n] + products[n:]
    gram_s[:n, :n] = products[:, :n] + products[:, n : 2 * n]
    gram_s[:n, n:] = products[:, 2 * n : 3 * n] + products[:, 3 * n : 4 * n]
    if mode == "first":
        gram_s[n:, :n] = jnp.zeros((n, n), F32)
    else:
        gram_s[n:, :n] = products[:, 4 * n : 5 * n] + products[:, 5 * n :]
    squares = rows(terms[2 * n : 4 * n, :], terms[2 * n : 4 * n, :])
    squares = squares[:n] + squares[n:]
    gram_s[n:, n:] = squares[:, :n] + squares[:, n:]
    if mode != "last":
        rim = jnp.dot(terms[: 2 * n, :], pick[...], preferred_element_type=F32)
        edge_in[:n, :size] = rim[:n] + rim[n:]
        wets = wet_out.shape[0] // 2
        load_spread[0].wait()
        tops = rows(spread[0], terms[: 2 * n, :])
        tops = tops + pltpu.roll(tops, n, 1)
        load_spread[1].wait()
        ends = rows(spread[1], terms[: 2 * n, :])
        ends = ends + pltpu.roll(ends, n, 1)
        lane = lax.broadcasted_iota(jnp.int32, tops.shape, 1)
        send[:, :wets, :] = jnp.where(lane < n, tops, ends).astype(BF16).reshape(peers, wets, 2 * n)
        left = gram_s[...]
        offset = 0
        for _ in range(3):
            term = left.astype(BF16).astype(F32)
            left = left - term
            gram_s[...] = term
            for d in range(peers):
                if d * glines < 2 * n:
                    rest[d, offset : offset + glines] = gram_s[d * glines : (d + 1) * glines, :]
            offset += glines
        left = edge_in[:n, :size]
        for _ in range(2):
            term = left.astype(BF16).astype(F32)
            left = left - term
            edge_in[:n, :size] = term
            for d in range(peers):
                if d * hlines < n:
                    rest[d, offset : offset + hlines] = edge_in[d * hlines : (d + 1) * hlines, :size]
                else:
                    rest[d, offset : offset + hlines] = jnp.zeros((hlines, size), F32)
            offset += hlines
        if offset < rest.shape[1]:
            rest[:, offset:, :] = jnp.zeros((peers, rest.shape[1] - offset, 2 * n), F32)
        send[:, wets:, :] = rest[...].astype(BF16)
    for copy in stores:
        copy.wait()


def advance(mode, total, peers, ids, rates, state, fixed):
    mixed, pick, place, spread = fixed
    width, size = pick.shape
    wets = place.shape[0]
    vectors = state[-1].shape[0]
    extra = 3 * -(-2 * vectors // peers) + 2 * -(-vectors // peers)
    extra = -(-extra // 16) * 16
    sds = jax.ShapeDtypeStruct
    block = pltpu.HBM((vectors, width), F32)
    small = sds((2 * vectors, 2 * vectors), F32)
    shapes, specs = [block], [HBM]
    if mode == "last":
        shapes += [small]
        specs += [VMEM]
    else:
        shapes += [
            sds((2 * vectors, 2 * size), F32),
            sds((wets, 2 * vectors), F32),
            sds((peers, wets // 2 + extra, 2 * vectors), BF16),
        ]
        specs += [VMEM] * 3
    if mode != "first":
        shapes += [block, block, sds((vectors, 2 * vectors), F32), small]
        specs += [HBM, HBM, VMEM, VMEM]
    scratch = [
        pltpu.VMEM((width // size + 2, vectors, size), BF16),
        pltpu.VMEM((6 * vectors, width), BF16),
        pltpu.VMEM((3 * vectors, width), F32),
        pltpu.VMEM((vectors, width), F32),
        pltpu.VMEM(mixed.shape if mode != "first" else (16, 128), BF16),
        pltpu.VMEM((2, spread.shape[0] // 2, spread.shape[1]) if mode != "last" else (16, 128), BF16),
        pltpu.VMEM((3 * vectors, 2 * size), F32),
        pltpu.SemaphoreType.DMA((6,)),
    ]
    if mode != "last":
        scratch += [pltpu.VMEM(small.shape, F32), pltpu.VMEM((peers, extra, 2 * vectors), F32)]
    if mode != "first":
        scratch += [pltpu.VMEM((vectors, 3 * vectors), F32)]
    held = 2 if mode == "first" else 3
    return pl.pallas_call(
        functools.partial(advance_kernel, mode, total, peers),
        in_specs=[SMEM, SMEM] + [VMEM] * (len(state) - held) + [HBM] * held + [VMEM, VMEM, HBM, HBM],
        out_specs=specs,
        out_shape=shapes,
        scratch_shapes=scratch,
        compiler_params=pltpu.CompilerParams(vmem_limit_bytes=LIMIT),
        name="advance_" + mode,
    )(ids, rates, *state, pick, place, mixed, spread)


def route_kernel(vectors, wets, received, _lag, pressed, send, rest):
    peers = received.shape[0]
    glines = -(-2 * vectors // peers)
    hlines = -(-vectors // peers)
    pressed[...] = jnp.sum(received[:, :wets, :].astype(F32), 0)
    rest[...] = received[:, wets:, :].astype(F32)
    sums = jnp.sum(rest[...], 0)
    mine = sums[:glines] + sums[glines : 2 * glines] + sums[2 * glines : 3 * glines]
    edge = 3 * glines
    nothing = jnp.zeros((hlines, 2 * vectors), F32)

    def halo(t):
        if not 0 <= t < peers:
            return nothing
        return rest[t, edge : edge + hlines] + rest[t, edge + hlines : edge + 2 * hlines]

    send[...] = jnp.zeros(send.shape, F32)
    for t in range(peers):
        send[t, :glines] = mine
        send[t, glines : glines + hlines] = halo(t - 1)
        send[t, glines + hlines : glines + 2 * hlines] = halo(t + 1)


def route(vectors, wets, received, lag):
    peers, lines, lanes = received.shape
    return pl.pallas_call(
        functools.partial(route_kernel, vectors, wets),
        in_specs=[VMEM, VMEM],
        out_specs=[VMEM] * 2,
        out_shape=[
            jax.ShapeDtypeStruct((wets, 2 * vectors), F32),
            jax.ShapeDtypeStruct((peers, 8, 2 * vectors), F32),
        ],
        scratch_shapes=[pltpu.VMEM((peers, lines - wets, lanes), F32)],
        compiler_params=pltpu.CompilerParams(vmem_limit_bytes=LIMIT),
        name="route",
    )(received, lag)


def finish_kernel(total, gram, inner, lag, applied, residual, previous, out, coef, factor_t, mix, both, stack, sems):
    n = inner.shape[0]
    loads = []
    for k, source in enumerate((applied, residual, previous)):
        loads.append(pltpu.make_async_copy(source, stack.at[pl.ds(k * n, n)], sems.at[k]))
        loads[-1].start()
    blend(total, gram, lag, both, mix)
    for copy in loads:
        copy.wait()

    def next_residual():
        stack[:n, :] = exact(mix[...], stack[...])

    inverse, _, _ = settle(total, gram, inner, lag, both, [next_residual], coef, factor_t)
    out[...] = exact(inverse, stack[:n, :])


def finish(total, gram, inner, lag, held):
    vectors, width = held[0].shape
    return pl.pallas_call(
        functools.partial(finish_kernel, total),
        in_specs=[VMEM] * 3 + [HBM] * 3,
        out_specs=[VMEM] * 2,
        out_shape=[
            jax.ShapeDtypeStruct((vectors, width), F32),
            jax.ShapeDtypeStruct((3, vectors, vectors), F32),
        ],
        scratch_shapes=[
            pltpu.VMEM((vectors, 2 * vectors), F32),
            pltpu.VMEM((vectors, 3 * vectors), F32),
            pltpu.VMEM((vectors, 2 * vectors), F32),
            pltpu.VMEM((3 * vectors, width), F32),
            pltpu.SemaphoreType.DMA((3,)),
        ],
        compiler_params=pltpu.CompilerParams(vmem_limit_bytes=LIMIT),
        name="finish",
    )(gram, inner, lag, *held)


def local(n_row, n_col, start_block, struct_blocks, block_ids, rim_rows, wet_slots, wet_counts, added_mass, rates):
    peers = n_row * n_col
    vectors, width = start_block.shape
    total = float(width * peers)
    wcap = wet_slots.shape[0]
    wets = added_mass.shape[0] // n_row

    def exchange(parts):
        return lax.all_to_all(parts, AXES, 0, 0, tiled=True)

    def neighbours(halo):
        up = [(i, i + 1) for i in range(peers - 1)]
        down = [(i + 1, i) for i in range(peers - 1)]
        return lax.ppermute(halo, AXES, up), lax.ppermute(halo, AXES, down)

    def summed(gram):
        lines = gram.shape[0] // peers
        mine = exchange(gram.reshape(peers, lines, -1)).sum(0)
        return exchange(jnp.broadcast_to(mine[None], (peers, *mine.shape))).reshape(gram.shape)

    blocks = added_mass.reshape(-1, n_col, wcap).transpose(1, 0, 2)
    mass = lax.all_to_all(blocks, "col", 0, 0, tiled=True)
    mass = mass.reshape(n_col, n_row, 2, wets // 2, wcap)
    mixed, pick, place, halo = combine(
        rates, rim_rows[None, :], wet_slots[:wets, None], start_block, struct_blocks
    )
    below, above = neighbours(halo)
    base = in_hbm(prepare(block_ids, below, above, start_block, mixed))
    spread, part = spread_mass(wet_counts, wet_slots[None, :], start_block, mass, base)
    fixed = (in_hbm(mixed), pick, place, in_hbm(spread))
    arrived = exchange(part.reshape(peers, wets // 2, 2 * vectors))
    step = functools.partial(advance, total=total, peers=peers, ids=block_ids, rates=rates, fixed=fixed)
    applied, edges, wet_held, send = step("first", state=(arrived, below, above, base, in_hbm(start_block)))
    inner = jnp.zeros((vectors, 2 * vectors), F32)
    unit = jnp.eye(vectors, dtype=F32)
    lag = jnp.concatenate([unit, unit], 1)
    residual, previous = start_block, jnp.zeros_like(start_block)
    coefficients = []
    for number in range(1, STEPS):
        pressed, again = route(vectors, wets // 2, exchange(send), lag)
        received = exchange(again)
        state = (received, pressed, lag, edges, wet_held, in_hbm(applied), in_hbm(residual), in_hbm(previous))
        if number < STEPS - 1:
            applied, edges, wet_held, send, residual, previous, both, gram = step("mid", state=state)
        else:
            applied, products, residual, previous, both, gram = step("last", state=state)
        lag, inner, coef = factor(total, gram, inner, lag, both)
        coefficients.append(coef)
    final, coef = finish(total, summed(products), inner, lag, (in_hbm(applied), in_hbm(residual), in_hbm(previous)))
    coefficients.append(coef)
    return final, jnp.stack(coefficients)


def solution(mesh):
    return jax.shard_map(
        functools.partial(local, mesh.shape["row"], mesh.shape["col"]),
        mesh=mesh,
        in_specs=(
            P(None, AXES),
            P(None, AXES, None, None, None),
            P(AXES, None),
            P(AXES),
            P(AXES),
            P(AXES),
            P("col", "row"),
            P(),
        ),
        out_specs=(P(None, AXES), P()),
        check_vma=False,
    )
```

```python
import functools

import jax
import jax.numpy as jnp
from jax import lax
from jax.experimental import pallas as pl
from jax.experimental.pallas import tpu as pltpu
from jax.sharding import PartitionSpec as P

STEPS = 6
AXES = ("row", "col")
VMEM = pl.BlockSpec(memory_space=pltpu.VMEM)
SMEM = pl.BlockSpec(memory_space=pltpu.SMEM)
HBM = pl.BlockSpec(memory_space=pltpu.HBM)
ANY = pl.BlockSpec(memory_space=pl.ANY)
F32 = jnp.float32
BF16 = jnp.bfloat16
LIMIT = 40 * 1024 * 1024


def exact(left, right):
    return lax.dot_general(
        left, right, (((1,), (0,)), ((), ())), precision=lax.Precision.HIGHEST, preferred_element_type=F32
    )


def exact_rows(left, right):
    return lax.dot_general(
        left, right, (((1,), (1,)), ((), ())), precision=lax.Precision.HIGHEST, preferred_element_type=F32
    )


def rows(left, right):
    return lax.dot_general(left, right, (((1,), (1,)), ((), ())), preferred_element_type=F32)


def in_hbm(values):
    return pltpu.with_memory_space_constraint(values, pltpu.HBM)


def halves(values):
    high = values.astype(BF16)
    return high, (values - high.astype(F32)).astype(BF16)


def combine_kernel(rates, rim, wet, start, blocks, mixed, pick, place, halo):
    size = blocks.shape[-1]
    for k in range(blocks.shape[2]):
        whole = (
            blocks[0, 0, k].astype(F32)
            + rates[0] * blocks[1, 0, k].astype(F32)
            - rates[1] * blocks[2, 0, k].astype(F32)
        ).T
        high = whole.astype(BF16)
        mixed[0, k * size : (k + 1) * size, :size] = high
        mixed[0, k * size : (k + 1) * size, size:] = (whole - high.astype(F32)).astype(BF16)

    @pl.when(pl.program_id(0) == 0)
    def _():
        index = lax.broadcasted_iota(jnp.int32, pick.shape, 0)
        pick[...] = jnp.where(index == rim[...], 1.0, 0.0).astype(BF16)
        index = lax.broadcasted_iota(jnp.int32, place.shape, 1)
        place[...] = jnp.where(index == wet[...], 1.0, 0.0).astype(BF16)
        high, low = halves(start[...])
        halo[...] = jnp.dot(high, pick[...], preferred_element_type=F32) + jnp.dot(
            low, pick[...], preferred_element_type=F32
        )


def combine(rates, rim, wet, start, blocks):
    _, count, nnz, size, _ = blocks.shape
    vectors, width = start.shape
    whole = lambda shape: pl.BlockSpec(shape, lambda i: (0,) * len(shape))
    return pl.pallas_call(
        combine_kernel,
        grid=(count,),
        in_specs=[
            SMEM,
            whole(rim.shape),
            whole(wet.shape),
            whole(start.shape),
            pl.BlockSpec((3, 1, nnz, size, size), lambda i: (0, i, 0, 0, 0)),
        ],
        out_specs=[
            pl.BlockSpec((1, nnz * size, 2 * size), lambda i: (i, 0, 0)),
            whole((width, rim.shape[1])),
            whole((wet.shape[0], width)),
            whole((vectors, rim.shape[1])),
        ],
        out_shape=[
            pltpu.HBM((count, nnz * size, 2 * size), BF16),
            jax.ShapeDtypeStruct((width, rim.shape[1]), BF16),
            jax.ShapeDtypeStruct((wet.shape[0], width), BF16),
            jax.ShapeDtypeStruct((vectors, rim.shape[1]), F32),
        ],
        compiler_params=pltpu.CompilerParams(vmem_limit_bytes=LIMIT),
        name="combine",
    )(rates, rim, wet, start, blocks)


def live_slots(count, slots):
    slot = lax.broadcasted_iota(jnp.int32, slots.shape, 1)
    return jnp.where(slot < count[0], slots[...], -1)


def chosen(first, shape, live):
    index = lax.broadcasted_iota(jnp.int32, shape, 0) + first
    return jnp.where(index == live, 1.0, 0.0).astype(BF16)


def start_pressure_kernel(values, mass, part):
    n_col, n_row, _, half, wcap = mass.shape
    size, vectors = n_col * half, values.shape[0]
    for r in range(n_row):
        for h in range(2):
            own = mass[:, r, h].reshape(size, wcap)
            pressed = rows(own, values[...]).astype(BF16)
            part[r * size : (r + 1) * size, h * vectors : (h + 1) * vectors] = pressed


def start_pressure(values, mass, base):
    n_col, n_row, _, half, _ = mass.shape
    return pl.pallas_call(
        lambda values, mass, _base, part: start_pressure_kernel(values, mass, part),
        in_specs=[VMEM, VMEM, HBM],
        out_specs=VMEM,
        out_shape=jax.ShapeDtypeStruct((n_col * n_row * half, 2 * values.shape[0]), BF16),
        compiler_params=pltpu.CompilerParams(vmem_limit_bytes=LIMIT),
        name="start_pressure",
    )(values, mass, base)


def spread_kernel(count, slots, mass, spread, own):
    n_col, n_row, _, half, wcap = mass.shape
    size = n_col * half

    @pl.when(pl.program_id(0) == 0)
    def _():
        for h in range(2):
            for r in range(n_row):
                first = (h * n_row + r) * size
                own[first : first + size] = mass[:, r, h].reshape(size, wcap)

    columns = spread.shape[1]
    onehot = chosen(pl.program_id(0) * columns, (columns, wcap), live_slots(count, slots))
    spread[...] = rows(own[...], onehot).astype(BF16)


def spread_mass(count, slots, mass, width):
    n_col, n_row, _, half, wcap = mass.shape
    size = n_col * n_row * half
    columns = min(width, 512)
    return pl.pallas_call(
        spread_kernel,
        grid=(width // columns,),
        in_specs=[
            SMEM,
            pl.BlockSpec(slots.shape, lambda i: (0, 0)),
            pl.BlockSpec(mass.shape, lambda i: (0,) * 5),
        ],
        out_specs=pl.BlockSpec((2 * size, columns), lambda i: (0, i)),
        out_shape=pltpu.HBM((2 * size, width), BF16),
        scratch_shapes=[pltpu.VMEM((2 * size, wcap), BF16)],
        compiler_params=pltpu.CompilerParams(vmem_limit_bytes=LIMIT),
        cost_estimate=pl.CostEstimate(
            flops=4 * size * wcap * width, bytes_accessed=4 * size * width, transcendentals=0
        ),
        name="spread",
    )(count, slots, mass)


def halve_columns(top, low, s):
    a, b, c = top[:, s : s + 1], top[:, s + 1 : s + 2], low[:, s + 1 : s + 2]
    scale = 1.0 / (a * c - b * b)
    return (c * top - b * low) * scale, (a * low - b * top) * scale


def eliminate(matrix, beside, coef, factor_t):
    n = matrix.shape[0]
    groups = n // 8
    row_id = lax.broadcasted_iota(jnp.int32, (n, 2 * n), 0)
    lane_id = lax.broadcasted_iota(jnp.int32, (n, 2 * n), 1)
    factor_t[...] = jnp.where(row_id + n == lane_id, 1.0, 0.0)
    factor_t[:, :n] = matrix
    sub = lax.broadcasted_iota(jnp.int32, (8, 1), 0)
    if beside:
        work = [factor_t[g * 8 : (g + 1) * 8, :] for g in range(groups)]
        done = 0
        for j in range(0, n, 2):
            g, s = divmod(j, 8)
            new_top, new_low = halve_columns(work[g][s : s + 1, :], work[g][s + 1 : s + 2, :], j)
            for i in range(g, groups):
                left, right = work[i][:, j : j + 1], work[i][:, j + 1 : j + 2]
                if i == g:
                    left = jnp.where(sub > s + 1, left, 0.0)
                    right = jnp.where(sub > s + 1, right, 0.0)
                work[i] = work[i] - (left * new_top + right * new_low)
            goal = len(beside) * (j + 2) // n
            while done < goal:
                beside[done]()
                done += 1
        reduced = jnp.concatenate(work, 0)
    else:

        def group(step, _):
            work = [factor_t[g * 8 : (g + 1) * 8, :] for g in range(groups)]
            for s in range(0, 8, 2):
                new_top, new_low = halve_columns(work[0][s : s + 1, :], work[0][s + 1 : s + 2, :], s)
                for i in range(groups):
                    left, right = work[i][:, s : s + 1], work[i][:, s + 1 : s + 2]
                    keep = sub > s + 1 if i == 0 else step + i < groups
                    update = left * new_top + right * new_low
                    work[i] = work[i] - jnp.where(keep, update, 0.0)
            for i in range(groups):
                target = (i - 1) % groups
                factor_t[target * 8 : (target + 1) * 8, :] = pltpu.roll(work[i], 2 * n - 8, 1)
            return 0

        lax.fori_loop(0, groups, group, 0)
        reduced = pltpu.roll(factor_t[...], n, 1)
    above = pltpu.roll(reduced, 1, 0)
    odd = lax.broadcasted_iota(jnp.int32, (n, 1), 0) % 2 == 1
    pick = lambda values, where: jnp.sum(jnp.where(where, values, 0.0), 1, keepdims=True)
    under = pick(above, lane_id == row_id) / jnp.where(odd, pick(above, lane_id + 1 == row_id), 1.0)
    reduced = reduced - jnp.where(odd, under, 0.0) * above
    diagonal = pick(reduced, lane_id == row_id)
    scale = lax.rsqrt(diagonal)
    scale = scale * (1.5 - 0.5 * diagonal * scale * scale)
    reduced = reduced * scale
    factor_t[...] = reduced
    upper = jnp.where(row_id <= lane_id, reduced, 0.0)
    coef[2] = upper.T[:n, :]
    return factor_t[:, n:]


def congruent(factor, matrix):
    return exact(factor, exact_rows(matrix, factor))


def settle(total, gram, inner, lag, both, beside, coef, factor_t):
    n = gram.shape[0] // 2
    scale = 1.0 / total
    pull = lag[:, :n]
    aa = congruent(pull, gram[:n, :n] * scale)
    cc = congruent(pull, gram[n:, n:] * scale)
    self_ = both[:, :n]
    prev = both[:, n:]
    cp = inner[:, :n]
    pp = inner[:, n:]
    coef[0] = self_
    coef[1] = prev
    t_c = self_ - exact(self_, cc) - exact_rows(prev, cp)
    t_p = prev - exact(self_, cp) - exact(prev, pp)
    t_a = aa - exact_rows(self_, self_) - exact_rows(prev, prev)
    matrix = t_a - exact_rows(t_c, self_) - exact_rows(t_p, prev)
    inverse = eliminate(0.5 * (matrix + matrix.T), beside, coef, factor_t)
    return inverse, t_c, cc


def blend(total, gram, lag, both, mix):
    n = gram.shape[0] // 2
    scale = 1.0 / total
    pull, square = lag[:, :n], lag[:, n:]
    crossed = gram[:n, n:] * scale
    prev = exact(pull, gram[n:, :n] * scale)
    mix[:, :n] = pull
    mix[:, n : 2 * n] = -exact(pull, exact(crossed, square))
    mix[:, 2 * n :] = -prev
    both[:, :n] = congruent(pull, crossed)
    both[:, n:] = prev


def factor_kernel(total, gram, inner, lag, both, lag_out, inner_out, coef, factor_t):
    n = gram.shape[0] // 2
    inverse, t_c, cc = settle(total, gram, inner, lag, both, [], coef, factor_t)
    lag_out[:, :n] = inverse
    lag_out[:, n:] = exact(inverse.T, inverse)
    inner_out[:, :n] = exact(inverse, t_c)
    inner_out[:, n:] = cc


def factor(total, gram, inner, lag, both):
    n = gram.shape[0] // 2
    sds = jax.ShapeDtypeStruct
    return pl.pallas_call(
        functools.partial(factor_kernel, total),
        in_specs=[VMEM] * 4,
        out_specs=[VMEM] * 3,
        out_shape=[sds((n, 2 * n), F32), sds((n, 2 * n), F32), sds((3, n, n), F32)],
        scratch_shapes=[pltpu.VMEM((n, 2 * n), F32)],
        compiler_params=pltpu.CompilerParams(vmem_limit_bytes=LIMIT),
        cost_estimate=pl.CostEstimate(flops=100_000_000, bytes_accessed=10_000_000, transcendentals=0),
        name="factor",
    )(gram, inner, lag, both)


def thirds(values):
    high = values.astype(BF16)
    rest = values - high.astype(F32)
    return jnp.concatenate([high, *halves(rest)], 0)


def unpack(lines, received, target, lanes, offset):
    for s in range(received.shape[0]):
        if s * lines < target.shape[0]:
            target[s * lines : (s + 1) * lines, lanes] = received[s, offset : offset + lines]


def place_columns(extended, block, edge):
    size = extended.shape[2]
    count = extended.shape[0] - 2
    for i in range(count):
        extended[i] = block[:, i * size : (i + 1) * size]
    extended[count] = edge[:, :size].astype(BF16)
    extended[count + 1] = edge[:, size:].astype(BF16)


def block_row(ids, extended, mixed, i):
    picked = jnp.concatenate([extended[ids[i, k]] for k in range(ids.shape[1])], 1)
    pair = jnp.dot(picked, mixed[i], preferred_element_type=F32)
    size = pair.shape[1] // 2
    return pair[:, :size] + pair[:, size:]


def prepare_kernel(ids, count, slots, below, above, start, mixed, out, zeros, values, extended):
    size = below.shape[1]
    block = start[...].astype(BF16)
    place_columns(extended, block, jnp.concatenate([below[...], above[...]], 1))
    for i in range(out.shape[1] // size):
        out[:, i * size : (i + 1) * size] = block_row(ids, extended, mixed, i)
    zeros[...] = jnp.zeros_like(zeros)
    live = live_slots(count, slots)
    columns = min(out.shape[1], 512)
    total = jnp.zeros(values.shape, F32)
    for first in range(0, out.shape[1], columns):
        picked = chosen(first, (columns, slots.shape[1]), live)
        total = total + jnp.dot(block[:, first : first + columns], picked, preferred_element_type=F32)
    values[...] = total.astype(BF16)


def prepare(ids, count, slots, below, above, start, mixed):
    vectors, width = start.shape
    size = below.shape[1]
    return pl.pallas_call(
        prepare_kernel,
        in_specs=[SMEM, SMEM] + [VMEM] * 5,
        out_specs=[VMEM] * 3,
        out_shape=[
            pltpu.HBM((vectors, width), F32),
            pltpu.HBM((vectors, width), F32),
            jax.ShapeDtypeStruct((vectors, slots.shape[1]), BF16),
        ],
        scratch_shapes=[pltpu.VMEM((width // size + 2, vectors, size), BF16)],
        compiler_params=pltpu.CompilerParams(vmem_limit_bytes=LIMIT),
        name="prepare",
    )(ids, count, slots, below, above, start, mixed)


def advance_kernel(mode, total, peers, *refs):
    it = iter(refs)
    take = lambda k: [next(it) for _ in range(k)]
    ids, rates = take(2)
    if mode == "first":
        arrived, below, above = take(3)
        held = take(2)
    else:
        received, pressed, lag, edges, wet_held = take(5)
        held = take(3)
    pick, place, mixed_in, spread_in = take(4)
    (applied_out,) = take(1)
    if mode == "last":
        (gram_s,) = take(1)
    else:
        edges_out, wet_out, send = take(3)
    if mode != "first":
        residual_out, previous_out, both, gram_in = take(4)
    extended, terms, stack, fresh, mixed, spread, edge_in, sems = take(8)
    if mode != "last":
        gram_s, rest = take(2)
    if mode != "first":
        (mix,) = take(1)

    n = fresh.shape[0]
    width = fresh.shape[1]
    size = edge_in.shape[1] // 2
    count = width // size
    glines = -(-2 * n // peers)
    hlines = -(-n // peers)
    loads = []
    for k, source in enumerate(held):
        loads.append(pltpu.make_async_copy(source, stack.at[pl.ds(k * n, n)], sems.at[k]))
        loads[-1].start()
    if mode != "first":
        load_mixed = pltpu.make_async_copy(mixed_in, mixed, sems.at[3])
        load_mixed.start()
    load_spread = []
    if mode != "last":
        for h in range(2):
            part = spread_in.at[pl.ds(h * spread.shape[1], spread.shape[1])]
            load_spread.append(pltpu.make_async_copy(part, spread.at[h], sems.at[4 + h]))
            load_spread[-1].start()

    stores = []
    if mode == "first":
        edge = jnp.concatenate([below[...], above[...]], 1)
        summed = jnp.sum(arrived[...].astype(F32), 0)
        wet = jnp.concatenate([summed[:, :n], summed[:, n:]], 0)
        edges_out[:n, :] = edge
        edges_out[n:, :] = jnp.zeros_like(edge)
        wet_out[:, :n] = wet
        wet_out[:, n:] = jnp.zeros_like(wet)
        for copy in loads:
            copy.wait()
        residual = stack[n : 2 * n, :]
    else:
        unpack(glines, received, gram_in, slice(None), 0)
        unpack(hlines, received, edge_in.at[pl.ds(0, n)], slice(0, size), glines)
        unpack(hlines, received, edge_in.at[pl.ds(0, n)], slice(size, 2 * size), glines + hlines)
        edge_in[n:, :] = edges[...]
        blend(total, gram_in, lag, both, mix)
        pull = lag[:, :n]
        edge = exact(mix[...], edge_in[...])
        summed = pressed[...]
        wet = exact_rows(jnp.concatenate([summed[:, :n], summed[:, n:]], 0), pull)
        wet = wet + exact_rows(wet_held[...], mix[:, n:])
        if mode != "last":
            edges_out[:n, :] = edge
            edges_out[n:, :] = exact(pull, edges[:n, :])
            wet_out[:, :n] = wet
            wet_out[:, n:] = exact_rows(wet_held[:, :n], pull)
        for copy in loads:
            copy.wait()
        residual = exact(mix[...], stack[...])
        previous = exact(pull, stack[n : 2 * n, :])
        stack[:n, :] = residual
        stack[n : 2 * n, :] = previous
        stores.append(pltpu.make_async_copy(stack.at[pl.ds(0, n)], residual_out, sems.at[0]))
        stores.append(pltpu.make_async_copy(stack.at[pl.ds(n, n)], previous_out, sems.at[1]))
        for copy in stores:
            copy.start()
        terms[4 * n : 5 * n, :], terms[5 * n :, :] = halves(previous)
    high, low = halves(residual)
    terms[2 * n : 3 * n, :] = high
    terms[3 * n : 4 * n, :] = low
    force = thirds(wet.T * rates[1])
    if mode != "first":
        place_columns(extended, high, edge)
        load_mixed.wait()
    for i in range(count):
        lanes = slice(i * size, (i + 1) * size)
        added = jnp.dot(force, place[:, lanes], preferred_element_type=F32)
        applied = stack[:n, lanes] if mode == "first" else block_row(ids, extended, mixed, i)
        applied = applied - (added[:n] + added[n : 2 * n] + added[2 * n :])
        fresh[:, lanes] = applied
        terms[:n, lanes], terms[n : 2 * n, lanes] = halves(applied)
    stores.append(pltpu.make_async_copy(fresh, applied_out, sems.at[2]))
    stores[-1].start()

    known = 4 * n if mode == "first" else 6 * n
    products = rows(terms[: 2 * n, :], terms[:known, :])
    products = products[:n] + products[n:]
    gram_s[:n, :n] = products[:, :n] + products[:, n : 2 * n]
    gram_s[:n, n:] = products[:, 2 * n : 3 * n] + products[:, 3 * n : 4 * n]
    if mode == "first":
        gram_s[n:, :n] = jnp.zeros((n, n), F32)
    else:
        gram_s[n:, :n] = products[:, 4 * n : 5 * n] + products[:, 5 * n :]
    squares = rows(terms[2 * n : 4 * n, :], terms[2 * n : 4 * n, :])
    squares = squares[:n] + squares[n:]
    gram_s[n:, n:] = squares[:, :n] + squares[:, n:]
    if mode != "last":
        rim = jnp.dot(terms[: 2 * n, :], pick[...], preferred_element_type=F32)
        edge_in[:n, :size] = rim[:n] + rim[n:]
        wets = wet_out.shape[0] // 2
        for copy in load_spread:
            copy.wait()
        tops = rows(spread[0], terms[: 2 * n, :])
        tops = tops + pltpu.roll(tops, n, 1)
        ends = rows(spread[1], terms[: 2 * n, :])
        ends = ends + pltpu.roll(ends, n, 1)
        lane = lax.broadcasted_iota(jnp.int32, tops.shape, 1)
        send[:, :wets, :] = jnp.where(lane < n, tops, ends).astype(BF16).reshape(peers, wets, 2 * n)
        left = gram_s[...]
        offset = 0
        for _ in range(3):
            term = left.astype(BF16).astype(F32)
            left = left - term
            gram_s[...] = term
            for d in range(peers):
                if d * glines < 2 * n:
                    rest[d, offset : offset + glines] = gram_s[d * glines : (d + 1) * glines, :]
            offset += glines
        left = edge_in[:n, :size]
        for _ in range(2):
            term = left.astype(BF16).astype(F32)
            left = left - term
            edge_in[:n, :size] = term
            for d in range(peers):
                if d * hlines < n:
                    rest[d, offset : offset + hlines] = edge_in[d * hlines : (d + 1) * hlines, :size]
                else:
                    rest[d, offset : offset + hlines] = jnp.zeros((hlines, size), F32)
            offset += hlines
        if offset < rest.shape[1]:
            rest[:, offset:, :] = jnp.zeros((peers, rest.shape[1] - offset, 2 * n), F32)
        send[:, wets:, :] = rest[...].astype(BF16)
    for copy in stores:
        copy.wait()


def advance(mode, total, peers, ids, rates, state, fixed):
    mixed, pick, place, spread = fixed
    width, size = pick.shape
    wets = place.shape[0]
    vectors = state[-1].shape[0]
    extra = 3 * -(-2 * vectors // peers) + 2 * -(-vectors // peers)
    extra = -(-extra // 16) * 16
    sds = jax.ShapeDtypeStruct
    block = pltpu.HBM((vectors, width), F32)
    small = sds((2 * vectors, 2 * vectors), F32)
    shapes, specs = [block], [HBM]
    if mode == "last":
        shapes += [small]
        specs += [VMEM]
    else:
        shapes += [
            sds((2 * vectors, 2 * size), F32),
            sds((wets, 2 * vectors), F32),
            sds((peers, wets // 2 + extra, 2 * vectors), BF16),
        ]
        specs += [VMEM] * 3
    if mode != "first":
        shapes += [block, block, sds((vectors, 2 * vectors), F32), small]
        specs += [HBM, HBM, VMEM, VMEM]
    scratch = [
        pltpu.VMEM((width // size + 2, vectors, size), BF16),
        pltpu.VMEM((6 * vectors, width), BF16),
        pltpu.VMEM((3 * vectors, width), F32),
        pltpu.VMEM((vectors, width), F32),
        pltpu.VMEM(mixed.shape if mode != "first" else (16, 128), BF16),
        pltpu.VMEM((2, spread.shape[0] // 2, spread.shape[1]) if mode != "last" else (16, 128), BF16),
        pltpu.VMEM((3 * vectors, 2 * size), F32),
        pltpu.SemaphoreType.DMA((6,)),
    ]
    if mode != "last":
        scratch += [pltpu.VMEM(small.shape, F32), pltpu.VMEM((peers, extra, 2 * vectors), F32)]
    if mode != "first":
        scratch += [pltpu.VMEM((vectors, 3 * vectors), F32)]
    held = 2 if mode == "first" else 3
    return pl.pallas_call(
        functools.partial(advance_kernel, mode, total, peers),
        in_specs=[SMEM, SMEM] + [VMEM] * (len(state) - held) + [HBM] * held + [VMEM, VMEM, HBM, HBM],
        out_specs=specs,
        out_shape=shapes,
        scratch_shapes=scratch,
        compiler_params=pltpu.CompilerParams(vmem_limit_bytes=LIMIT),
        name="advance_" + mode,
    )(ids, rates, *state, pick, place, mixed, spread)


def route_kernel(vectors, wets, received, _lag, pressed, send, rest):
    peers = received.shape[0]
    glines = -(-2 * vectors // peers)
    hlines = -(-vectors // peers)
    pressed[...] = jnp.sum(received[:, :wets, :].astype(F32), 0)
    rest[...] = received[:, wets:, :].astype(F32)
    sums = jnp.sum(rest[...], 0)
    mine = sums[:glines] + sums[glines : 2 * glines] + sums[2 * glines : 3 * glines]
    edge = 3 * glines
    nothing = jnp.zeros((hlines, 2 * vectors), F32)

    def halo(t):
        if not 0 <= t < peers:
            return nothing
        return rest[t, edge : edge + hlines] + rest[t, edge + hlines : edge + 2 * hlines]

    send[...] = jnp.zeros(send.shape, F32)
    for t in range(peers):
        send[t, :glines] = mine
        send[t, glines : glines + hlines] = halo(t - 1)
        send[t, glines + hlines : glines + 2 * hlines] = halo(t + 1)


def route(vectors, wets, received, lag):
    peers, lines, lanes = received.shape
    return pl.pallas_call(
        functools.partial(route_kernel, vectors, wets),
        in_specs=[VMEM, VMEM],
        out_specs=[VMEM] * 2,
        out_shape=[
            jax.ShapeDtypeStruct((wets, 2 * vectors), F32),
            jax.ShapeDtypeStruct((peers, 8, 2 * vectors), F32),
        ],
        scratch_shapes=[pltpu.VMEM((peers, lines - wets, lanes), F32)],
        compiler_params=pltpu.CompilerParams(vmem_limit_bytes=LIMIT),
        name="route",
    )(received, lag)


def repeat_sum_kernel(received, _lag, send):
    mine = jnp.sum(received[...], 0)
    for t in range(send.shape[0]):
        send[t] = mine


def repeat_sum(received, lag):
    return pl.pallas_call(
        repeat_sum_kernel,
        in_specs=[VMEM, VMEM],
        out_specs=VMEM,
        out_shape=jax.ShapeDtypeStruct(received.shape, F32),
        compiler_params=pltpu.CompilerParams(vmem_limit_bytes=LIMIT),
        name="repeat_sum",
    )(received, lag)


def finish_kernel(total, gram, inner, lag, applied, residual, previous, *refs):
    *earlier, out, coefs, factor_t, mix, both, stack, sems = refs
    coef = coefs.at[len(earlier)]
    n = inner.shape[0]
    loads = []
    for k, source in enumerate((applied, residual, previous)):
        loads.append(pltpu.make_async_copy(source, stack.at[pl.ds(k * n, n)], sems.at[k]))
        loads[-1].start()
    blend(total, gram, lag, both, mix)
    for k, known in enumerate(earlier):
        coefs[k] = known[...]
    for copy in loads:
        copy.wait()

    def next_residual():
        stack[:n, :] = exact(mix[...], stack[...])

    inverse, _, _ = settle(total, gram, inner, lag, both, [next_residual], coef, factor_t)
    out[...] = exact(inverse, stack[:n, :])


def finish(total, gram, inner, lag, held, earlier):
    vectors, width = held[0].shape
    return pl.pallas_call(
        functools.partial(finish_kernel, total),
        in_specs=[VMEM] * 3 + [HBM] * 3 + [VMEM] * len(earlier),
        out_specs=[VMEM] * 2,
        out_shape=[
            pltpu.HBM((vectors, width), F32),
            pltpu.HBM((len(earlier) + 1, 3, vectors, vectors), F32),
        ],
        scratch_shapes=[
            pltpu.VMEM((vectors, 2 * vectors), F32),
            pltpu.VMEM((vectors, 3 * vectors), F32),
            pltpu.VMEM((vectors, 2 * vectors), F32),
            pltpu.VMEM((3 * vectors, width), F32),
            pltpu.SemaphoreType.DMA((3,)),
        ],
        compiler_params=pltpu.CompilerParams(vmem_limit_bytes=LIMIT),
        name="finish",
    )(gram, inner, lag, *held, *earlier)


def local(n_row, n_col, start_block, struct_blocks, block_ids, rim_rows, wet_slots, wet_counts, added_mass, rates):
    peers = n_row * n_col
    vectors, width = start_block.shape
    total = float(width * peers)
    wcap = wet_slots.shape[0]
    wets = added_mass.shape[0] // n_row

    def exchange(parts):
        return lax.all_to_all(parts, AXES, 0, 0, tiled=True)

    def neighbours(halo):
        up = [(i, i + 1) for i in range(peers - 1)]
        down = [(i + 1, i) for i in range(peers - 1)]
        return lax.ppermute(halo, AXES, up), lax.ppermute(halo, AXES, down)

    def summed(gram, lag):
        lines = gram.shape[0] // peers
        return exchange(repeat_sum(exchange(gram.reshape(peers, lines, -1)), lag)).reshape(gram.shape)

    blocks = added_mass.reshape(-1, n_col, wcap).transpose(1, 0, 2)
    mass = lax.all_to_all(blocks, "col", 0, 0, tiled=True)
    mass = mass.reshape(n_col, n_row, 2, wets // 2, wcap)
    mixed, pick, place, halo = combine(
        rates, rim_rows[None, :], wet_slots[:wets, None], start_block, struct_blocks
    )
    below, above = neighbours(halo)
    slots = wet_slots[None, :]
    base, zeros, values = prepare(block_ids, wet_counts, slots, below, above, start_block, mixed)
    base, zeros = in_hbm(base), in_hbm(zeros)
    part = start_pressure(values, mass, base)
    spread = spread_mass(wet_counts, slots, mass, width)
    fixed = (in_hbm(mixed), pick, place, in_hbm(spread))
    arrived = exchange(part.reshape(peers, wets // 2, 2 * vectors))
    step = functools.partial(advance, total=total, peers=peers, ids=block_ids, rates=rates, fixed=fixed)
    applied, edges, wet_held, send = step("first", state=(arrived, below, above, base, in_hbm(start_block)))
    inner = jnp.zeros((vectors, 2 * vectors), F32)
    unit = jnp.eye(vectors, dtype=F32)
    lag = jnp.concatenate([unit, unit], 1)
    residual, previous = start_block, zeros
    coefficients = []
    for number in range(1, STEPS):
        pressed, again = route(vectors, wets // 2, exchange(send), lag)
        received = exchange(again)
        state = (received, pressed, lag, edges, wet_held, in_hbm(applied), in_hbm(residual), in_hbm(previous))
        if number < STEPS - 1:
            applied, edges, wet_held, send, residual, previous, both, gram = step("mid", state=state)
        else:
            applied, products, residual, previous, both, gram = step("last", state=state)
        lag, inner, coef = factor(total, gram, inner, lag, both)
        coefficients.append(coef)
    held = (in_hbm(applied), in_hbm(residual), in_hbm(previous))
    final, coefs = finish(total, summed(products, lag), inner, lag, held, coefficients)
    return final, coefs


def solution(mesh):
    return jax.shard_map(
        functools.partial(local, mesh.shape["row"], mesh.shape["col"]),
        mesh=mesh,
        in_specs=(
            P(None, AXES),
            P(None, AXES, None, None, None),
            P(AXES, None),
            P(AXES),
            P(AXES),
            P(AXES),
            P("col", "row"),
            P(),
        ),
        out_specs=(P(None, AXES), P()),
        check_vma=False,
    )
```

```python
import functools

import jax
import jax.numpy as jnp
from jax import lax
from jax.experimental import pallas as pl
from jax.experimental.pallas import tpu as pltpu
from jax.sharding import PartitionSpec as P

STEPS = 6
AXES = ("row", "col")
VMEM = pl.BlockSpec(memory_space=pltpu.VMEM)
SMEM = pl.BlockSpec(memory_space=pltpu.SMEM)
HBM = pl.BlockSpec(memory_space=pltpu.HBM)
ANY = pl.BlockSpec(memory_space=pl.ANY)
F32 = jnp.float32
BF16 = jnp.bfloat16
LIMIT = 40 * 1024 * 1024


def exact(left, right):
    return lax.dot_general(
        left, right, (((1,), (0,)), ((), ())), precision=lax.Precision.HIGHEST, preferred_element_type=F32
    )


def exact_rows(left, right):
    return lax.dot_general(
        left, right, (((1,), (1,)), ((), ())), precision=lax.Precision.HIGHEST, preferred_element_type=F32
    )


def rows(left, right):
    return lax.dot_general(left, right, (((1,), (1,)), ((), ())), preferred_element_type=F32)


def in_hbm(values):
    return pltpu.with_memory_space_constraint(values, pltpu.HBM)


def halves(values):
    high = values.astype(BF16)
    return high, (values - high.astype(F32)).astype(BF16)


def by_owner_kernel(mass, out, sems):
    wcap = out.shape[2]
    copies = [
        pltpu.make_async_copy(mass.at[:, pl.ds(c * wcap, wcap)], out.at[c], sems.at[c])
        for c in range(out.shape[0])
    ]
    for copy in copies:
        copy.start()
    for copy in copies:
        copy.wait()


def by_owner(mass, n_col, wcap):
    return pl.pallas_call(
        by_owner_kernel,
        in_specs=[HBM],
        out_specs=HBM,
        out_shape=pltpu.HBM((n_col, mass.shape[0], wcap), BF16),
        scratch_shapes=[pltpu.SemaphoreType.DMA((n_col,))],
        name="by_owner",
    )(mass)


def combine_kernel(rates, rim, wet, start, blocks, mixed, pick, place, halo):
    size = blocks.shape[-1]
    for k in range(blocks.shape[2]):
        whole = (
            blocks[0, 0, k].astype(F32)
            + rates[0] * blocks[1, 0, k].astype(F32)
            - rates[1] * blocks[2, 0, k].astype(F32)
        ).T
        high = whole.astype(BF16)
        mixed[0, k * size : (k + 1) * size, :size] = high
        mixed[0, k * size : (k + 1) * size, size:] = (whole - high.astype(F32)).astype(BF16)

    @pl.when(pl.program_id(0) == 0)
    def _():
        index = lax.broadcasted_iota(jnp.int32, pick.shape, 0)
        pick[...] = jnp.where(index == rim[...], 1.0, 0.0).astype(BF16)
        index = lax.broadcasted_iota(jnp.int32, place.shape, 1)
        place[...] = jnp.where(index == wet[...], 1.0, 0.0).astype(BF16)
        high, low = halves(start[...])
        halo[...] = jnp.dot(high, pick[...], preferred_element_type=F32) + jnp.dot(
            low, pick[...], preferred_element_type=F32
        )


def combine(rates, rim, wet, start, blocks):
    _, count, nnz, size, _ = blocks.shape
    vectors, width = start.shape
    whole = lambda shape: pl.BlockSpec(shape, lambda i: (0,) * len(shape))
    return pl.pallas_call(
        combine_kernel,
        grid=(count,),
        in_specs=[
            SMEM,
            whole(rim.shape),
            whole(wet.shape),
            whole(start.shape),
            pl.BlockSpec((3, 1, nnz, size, size), lambda i: (0, i, 0, 0, 0)),
        ],
        out_specs=[
            pl.BlockSpec((1, nnz * size, 2 * size), lambda i: (i, 0, 0)),
            whole((width, rim.shape[1])),
            whole((wet.shape[0], width)),
            whole((vectors, rim.shape[1])),
        ],
        out_shape=[
            pltpu.HBM((count, nnz * size, 2 * size), BF16),
            jax.ShapeDtypeStruct((width, rim.shape[1]), BF16),
            jax.ShapeDtypeStruct((wet.shape[0], width), BF16),
            jax.ShapeDtypeStruct((vectors, rim.shape[1]), F32),
        ],
        compiler_params=pltpu.CompilerParams(vmem_limit_bytes=LIMIT),
        name="combine",
    )(rates, rim, wet, start, blocks)


def live_slots(count, slots):
    slot = lax.broadcasted_iota(jnp.int32, slots.shape, 1)
    return jnp.where(slot < count[0], slots[...], -1)


def chosen(first, shape, live):
    index = lax.broadcasted_iota(jnp.int32, shape, 0) + first
    return jnp.where(index == live, 1.0, 0.0).astype(BF16)


def start_pressure_kernel(values, mass, part):
    n_col, n_row, _, half, wcap = mass.shape
    size, vectors = n_col * half, values.shape[0]
    for r in range(n_row):
        for h in range(2):
            own = mass[:, r, h].reshape(size, wcap)
            pressed = rows(own, values[...]).astype(BF16)
            part[r * size : (r + 1) * size, h * vectors : (h + 1) * vectors] = pressed


def start_pressure(values, mass, base):
    n_col, n_row, _, half, _ = mass.shape
    return pl.pallas_call(
        lambda values, mass, _base, part: start_pressure_kernel(values, mass, part),
        in_specs=[VMEM, VMEM, HBM],
        out_specs=VMEM,
        out_shape=jax.ShapeDtypeStruct((n_col * n_row * half, 2 * values.shape[0]), BF16),
        compiler_params=pltpu.CompilerParams(vmem_limit_bytes=LIMIT),
        name="start_pressure",
    )(values, mass, base)


def spread_kernel(count, slots, mass, spread, own):
    n_col, n_row, _, half, wcap = mass.shape
    size = n_col * half

    @pl.when(pl.program_id(0) == 0)
    def _():
        for h in range(2):
            for r in range(n_row):
                first = (h * n_row + r) * size
                own[first : first + size] = mass[:, r, h].reshape(size, wcap)

    columns = spread.shape[1]
    onehot = chosen(pl.program_id(0) * columns, (columns, wcap), live_slots(count, slots))
    spread[...] = rows(own[...], onehot).astype(BF16)


def spread_mass(count, slots, mass, width):
    n_col, n_row, _, half, wcap = mass.shape
    size = n_col * n_row * half
    columns = min(width, 512)
    return pl.pallas_call(
        spread_kernel,
        grid=(width // columns,),
        in_specs=[
            SMEM,
            pl.BlockSpec(slots.shape, lambda i: (0, 0)),
            pl.BlockSpec(mass.shape, lambda i: (0,) * 5),
        ],
        out_specs=pl.BlockSpec((2 * size, columns), lambda i: (0, i)),
        out_shape=pltpu.HBM((2 * size, width), BF16),
        scratch_shapes=[pltpu.VMEM((2 * size, wcap), BF16)],
        compiler_params=pltpu.CompilerParams(vmem_limit_bytes=LIMIT),
        cost_estimate=pl.CostEstimate(
            flops=4 * size * wcap * width, bytes_accessed=4 * size * width, transcendentals=0
        ),
        name="spread",
    )(count, slots, mass)


def halve_columns(top, low, s):
    a, b, c = top[:, s : s + 1], top[:, s + 1 : s + 2], low[:, s + 1 : s + 2]
    scale = 1.0 / (a * c - b * b)
    return (c * top - b * low) * scale, (a * low - b * top) * scale


def eliminate(matrix, beside, coef, factor_t):
    n = matrix.shape[0]
    groups = n // 8
    row_id = lax.broadcasted_iota(jnp.int32, (n, 2 * n), 0)
    lane_id = lax.broadcasted_iota(jnp.int32, (n, 2 * n), 1)
    factor_t[...] = jnp.where(row_id + n == lane_id, 1.0, 0.0)
    factor_t[:, :n] = matrix
    sub = lax.broadcasted_iota(jnp.int32, (8, 1), 0)
    if beside:
        work = [factor_t[g * 8 : (g + 1) * 8, :] for g in range(groups)]
        done = 0
        for j in range(0, n, 2):
            g, s = divmod(j, 8)
            new_top, new_low = halve_columns(work[g][s : s + 1, :], work[g][s + 1 : s + 2, :], j)
            for i in range(g, groups):
                left, right = work[i][:, j : j + 1], work[i][:, j + 1 : j + 2]
                if i == g:
                    left = jnp.where(sub > s + 1, left, 0.0)
                    right = jnp.where(sub > s + 1, right, 0.0)
                work[i] = work[i] - (left * new_top + right * new_low)
            goal = len(beside) * (j + 2) // n
            while done < goal:
                beside[done]()
                done += 1
        reduced = jnp.concatenate(work, 0)
    else:

        def group(step, _):
            work = [factor_t[g * 8 : (g + 1) * 8, :] for g in range(groups)]
            for s in range(0, 8, 2):
                new_top, new_low = halve_columns(work[0][s : s + 1, :], work[0][s + 1 : s + 2, :], s)
                for i in range(groups):
                    left, right = work[i][:, s : s + 1], work[i][:, s + 1 : s + 2]
                    keep = sub > s + 1 if i == 0 else step + i < groups
                    update = left * new_top + right * new_low
                    work[i] = work[i] - jnp.where(keep, update, 0.0)
            for i in range(groups):
                target = (i - 1) % groups
                factor_t[target * 8 : (target + 1) * 8, :] = pltpu.roll(work[i], 2 * n - 8, 1)
            return 0

        lax.fori_loop(0, groups, group, 0)
        reduced = pltpu.roll(factor_t[...], n, 1)
    above = pltpu.roll(reduced, 1, 0)
    odd = lax.broadcasted_iota(jnp.int32, (n, 1), 0) % 2 == 1
    pick = lambda values, where: jnp.sum(jnp.where(where, values, 0.0), 1, keepdims=True)
    under = pick(above, lane_id == row_id) / jnp.where(odd, pick(above, lane_id + 1 == row_id), 1.0)
    reduced = reduced - jnp.where(odd, under, 0.0) * above
    diagonal = pick(reduced, lane_id == row_id)
    scale = lax.rsqrt(diagonal)
    scale = scale * (1.5 - 0.5 * diagonal * scale * scale)
    reduced = reduced * scale
    factor_t[...] = reduced
    upper = jnp.where(row_id <= lane_id, reduced, 0.0)
    coef[2] = upper.T[:n, :]
    return factor_t[:, n:]


def congruent(factor, matrix):
    return exact(factor, exact_rows(matrix, factor))


def settle(total, gram, inner, lag, both, beside, coef, factor_t):
    n = gram.shape[0] // 2
    scale = 1.0 / total
    pull = lag[:, :n]
    aa = congruent(pull, gram[:n, :n] * scale)
    cc = congruent(pull, gram[n:, n:] * scale)
    self_ = both[:, :n]
    prev = both[:, n:]
    cp = inner[:, :n]
    pp = inner[:, n:]
    coef[0] = self_
    coef[1] = prev
    t_c = self_ - exact(self_, cc) - exact_rows(prev, cp)
    t_p = prev - exact(self_, cp) - exact(prev, pp)
    t_a = aa - exact_rows(self_, self_) - exact_rows(prev, prev)
    matrix = t_a - exact_rows(t_c, self_) - exact_rows(t_p, prev)
    inverse = eliminate(0.5 * (matrix + matrix.T), beside, coef, factor_t)
    return inverse, t_c, cc


def put_weights(weights, mix, pull):
    n = mix.shape[0]
    high, low = halves(mix)
    pull_high, pull_low = halves(pull)
    for k in range(3):
        cut = slice(k * n, (k + 1) * n)
        weights[:n, 2 * k * n : (2 * k + 1) * n] = high[:, cut]
        weights[:n, (2 * k + 1) * n : (2 * k + 2) * n] = high[:, cut]
        weights[n : 2 * n, 2 * k * n : (2 * k + 1) * n] = low[:, cut]
        weights[n : 2 * n, (2 * k + 1) * n : (2 * k + 2) * n] = jnp.zeros((n, n), BF16)
    if weights.shape[0] > 2 * n:
        weights[2 * n :, :] = jnp.zeros((2 * n, 6 * n), BF16)
        weights[2 * n : 3 * n, 2 * n : 3 * n] = pull_high
        weights[2 * n : 3 * n, 3 * n : 4 * n] = pull_high
        weights[3 * n :, 2 * n : 3 * n] = pull_low


def blend(total, gram, lag, both, mix):
    n = gram.shape[0] // 2
    scale = 1.0 / total
    pull, square = lag[:, :n], lag[:, n:]
    crossed = gram[:n, n:] * scale
    prev = exact(pull, gram[n:, :n] * scale)
    mix[:, :n] = pull
    mix[:, n : 2 * n] = -exact(pull, exact(crossed, square))
    mix[:, 2 * n :] = -prev
    both[:, :n] = congruent(pull, crossed)
    both[:, n:] = prev


def factor_kernel(total, gram, inner, lag, both, lag_out, inner_out, coef, factor_t):
    n = gram.shape[0] // 2
    inverse, t_c, cc = settle(total, gram, inner, lag, both, [], coef, factor_t)
    lag_out[:, :n] = inverse
    lag_out[:, n:] = exact(inverse.T, inverse)
    inner_out[:, :n] = exact(inverse, t_c)
    inner_out[:, n:] = cc


def factor(total, gram, inner, lag, both):
    n = gram.shape[0] // 2
    sds = jax.ShapeDtypeStruct
    return pl.pallas_call(
        functools.partial(factor_kernel, total),
        in_specs=[VMEM] * 4,
        out_specs=[VMEM] * 3,
        out_shape=[sds((n, 2 * n), F32), sds((n, 2 * n), F32), sds((3, n, n), F32)],
        scratch_shapes=[pltpu.VMEM((n, 2 * n), F32)],
        compiler_params=pltpu.CompilerParams(vmem_limit_bytes=LIMIT),
        cost_estimate=pl.CostEstimate(flops=100_000_000, bytes_accessed=10_000_000, transcendentals=0),
        name="factor",
    )(gram, inner, lag, both)


def thirds(values):
    high = values.astype(BF16)
    rest = values - high.astype(F32)
    return jnp.concatenate([high, *halves(rest)], 0)


def unpack(lines, received, target, lanes, offset):
    for s in range(received.shape[0]):
        if s * lines < target.shape[0]:
            target[s * lines : (s + 1) * lines, lanes] = received[s, offset : offset + lines]


def place_columns(extended, block, edge):
    size = extended.shape[2]
    count = extended.shape[0] - 2
    for i in range(count):
        extended[i] = block[:, i * size : (i + 1) * size]
    extended[count] = edge[:, :size].astype(BF16)
    extended[count + 1] = edge[:, size:].astype(BF16)


def block_row(ids, extended, mixed, i):
    picked = jnp.concatenate([extended[ids[i, k]] for k in range(ids.shape[1])], 1)
    pair = jnp.dot(picked, mixed[i], preferred_element_type=F32)
    size = pair.shape[1] // 2
    return pair[:, :size] + pair[:, size:]


def prepare_kernel(ids, count, slots, below, above, start, mixed, out, values, extended):
    size = below.shape[1]
    block = start[...].astype(BF16)
    place_columns(extended, block, jnp.concatenate([below[...], above[...]], 1))
    for i in range(out.shape[1] // size):
        out[:, i * size : (i + 1) * size] = block_row(ids, extended, mixed, i)
    live = live_slots(count, slots)
    columns = min(out.shape[1], 512)
    total = jnp.zeros(values.shape, F32)
    for first in range(0, out.shape[1], columns):
        picked = chosen(first, (columns, slots.shape[1]), live)
        total = total + jnp.dot(block[:, first : first + columns], picked, preferred_element_type=F32)
    values[...] = total.astype(BF16)


def prepare(ids, count, slots, below, above, start, mixed):
    vectors, width = start.shape
    size = below.shape[1]
    return pl.pallas_call(
        prepare_kernel,
        in_specs=[SMEM, SMEM] + [VMEM] * 5,
        out_specs=[VMEM] * 2,
        out_shape=[
            pltpu.HBM((vectors, width), F32),
            jax.ShapeDtypeStruct((vectors, slots.shape[1]), BF16),
        ],
        scratch_shapes=[pltpu.VMEM((width // size + 2, vectors, size), BF16)],
        compiler_params=pltpu.CompilerParams(vmem_limit_bytes=LIMIT),
        name="prepare",
    )(ids, count, slots, below, above, start, mixed)


def advance_kernel(mode, total, peers, *refs):
    it = iter(refs)
    take = lambda k: [next(it) for _ in range(k)]
    ids, rates = take(2)
    if mode == "first":
        arrived, below, above = take(3)
        held = take(2)
    else:
        received, pressed, lag, edges, wet_held = take(5)
        held = take(1)
    pick, place, mixed_in, spread_in = take(4)
    (state_out,) = take(1)
    if mode == "last":
        (gram_s,) = take(1)
    else:
        edges_out, wet_out, send = take(3)
    if mode != "first":
        both, gram_in = take(2)
    extended, terms, stack, mixed, spread, edge_in, sems = take(7)
    if mode != "last":
        gram_s, rest = take(2)
    if mode != "first":
        mix, weights = take(2)

    n = terms.shape[0] // 6
    width = terms.shape[1]
    size = edge_in.shape[1] // 2
    count = width // size
    glines = -(-2 * n // peers)
    hlines = -(-n // peers)
    loads = []
    for k, source in enumerate(held):
        target = stack.at[pl.ds(k * n, n)] if mode == "first" else stack
        loads.append(pltpu.make_async_copy(source, target, sems.at[k]))
        loads[-1].start()
    if mode != "first":
        load_mixed = pltpu.make_async_copy(mixed_in, mixed, sems.at[3])
        load_mixed.start()
    load_spread = []
    if mode != "last":
        for h in range(2):
            part = spread_in.at[pl.ds(h * spread.shape[1], spread.shape[1])]
            load_spread.append(pltpu.make_async_copy(part, spread.at[h], sems.at[4 + h]))
            load_spread[-1].start()

    if mode == "first":
        edge = jnp.concatenate([below[...], above[...]], 1)
        summed = jnp.sum(arrived[...].astype(F32), 0)
        wet = jnp.concatenate([summed[:, :n], summed[:, n:]], 0)
        edges_out[:n, :] = edge
        edges_out[n:, :] = jnp.zeros_like(edge)
        wet_out[:, :n] = wet
        wet_out[:, n:] = jnp.zeros_like(wet)
        for copy in loads:
            copy.wait()
        residual = stack[n : 2 * n, :]
        terms[4 * n :, :] = jnp.zeros((2 * n, width), BF16)
    else:
        unpack(glines, received, gram_in, slice(None), 0)
        unpack(hlines, received, edge_in.at[pl.ds(0, n)], slice(0, size), glines)
        unpack(hlines, received, edge_in.at[pl.ds(0, n)], slice(size, 2 * size), glines + hlines)
        edge_in[n:, :] = edges[...]
        blend(total, gram_in, lag, both, mix)
        pull = lag[:, :n]
        put_weights(weights, mix[...], pull)
        edge = exact(mix[...], edge_in[...])
        summed = pressed[...]
        wet = exact_rows(jnp.concatenate([summed[:, :n], summed[:, n:]], 0), pull)
        wet = wet + exact_rows(wet_held[...], mix[:, n:])
        if mode != "last":
            edges_out[:n, :] = edge
            edges_out[n:, :] = exact(pull, edges[:n, :])
            wet_out[:, :n] = wet
            wet_out[:, n:] = exact_rows(wet_held[:, :n], pull)
        for copy in loads:
            copy.wait()
        mixture = jnp.dot(weights[...], stack[...], preferred_element_type=F32)
        residual = mixture[:n] + mixture[n : 2 * n]
        terms[4 * n : 5 * n, :], terms[5 * n :, :] = halves(mixture[2 * n : 3 * n] + mixture[3 * n :])
    high, low = halves(residual)
    terms[2 * n : 3 * n, :] = high
    terms[3 * n : 4 * n, :] = low
    force = thirds(wet.T * rates[1])
    if mode != "first":
        place_columns(extended, high, edge)
        load_mixed.wait()
    for i in range(count):
        lanes = slice(i * size, (i + 1) * size)
        added = jnp.dot(force, place[:, lanes], preferred_element_type=F32)
        applied = stack[:n, lanes] if mode == "first" else block_row(ids, extended, mixed, i)
        applied = applied - (added[:n] + added[n : 2 * n] + added[2 * n :])
        terms[:n, lanes], terms[n : 2 * n, lanes] = halves(applied)
    store = pltpu.make_async_copy(terms, state_out, sems.at[2])
    store.start()

    known = 4 * n if mode == "first" else 6 * n
    products = rows(terms[: 2 * n, :], terms[:known, :])
    products = products[:n] + products[n:]
    gram_s[:n, :n] = products[:, :n] + products[:, n : 2 * n]
    gram_s[:n, n:] = products[:, 2 * n : 3 * n] + products[:, 3 * n : 4 * n]
    if mode == "first":
        gram_s[n:, :n] = jnp.zeros((n, n), F32)
    else:
        gram_s[n:, :n] = products[:, 4 * n : 5 * n] + products[:, 5 * n :]
    squares = rows(terms[2 * n : 4 * n, :], terms[2 * n : 4 * n, :])
    squares = squares[:n] + squares[n:]
    gram_s[n:, n:] = squares[:, :n] + squares[:, n:]
    if mode != "last":
        rim = jnp.dot(terms[: 2 * n, :], pick[...], preferred_element_type=F32)
        edge_in[:n, :size] = rim[:n] + rim[n:]
        wets = wet_out.shape[0] // 2
        for copy in load_spread:
            copy.wait()
        tops = rows(spread[0], terms[: 2 * n, :])
        tops = tops + pltpu.roll(tops, n, 1)
        ends = rows(spread[1], terms[: 2 * n, :])
        ends = ends + pltpu.roll(ends, n, 1)
        lane = lax.broadcasted_iota(jnp.int32, tops.shape, 1)
        send[:, :wets, :] = jnp.where(lane < n, tops, ends).astype(BF16).reshape(peers, wets, 2 * n)
        left = gram_s[...]
        offset = 0
        for _ in range(3):
            term = left.astype(BF16).astype(F32)
            left = left - term
            gram_s[...] = term
            for d in range(peers):
                if d * glines < 2 * n:
                    rest[d, offset : offset + glines] = gram_s[d * glines : (d + 1) * glines, :]
            offset += glines
        left = edge_in[:n, :size]
        for _ in range(2):
            term = left.astype(BF16).astype(F32)
            left = left - term
            edge_in[:n, :size] = term
            for d in range(peers):
                if d * hlines < n:
                    rest[d, offset : offset + hlines] = edge_in[d * hlines : (d + 1) * hlines, :size]
                else:
                    rest[d, offset : offset + hlines] = jnp.zeros((hlines, size), F32)
            offset += hlines
        if offset < rest.shape[1]:
            rest[:, offset:, :] = jnp.zeros((peers, rest.shape[1] - offset, 2 * n), F32)
        send[:, wets:, :] = rest[...].astype(BF16)
    store.wait()


def advance(mode, total, peers, ids, rates, state, fixed):
    mixed, pick, place, spread = fixed
    width, size = pick.shape
    wets = place.shape[0]
    vectors = state[3].shape[0] if mode == "first" else state[2].shape[0]
    extra = 3 * -(-2 * vectors // peers) + 2 * -(-vectors // peers)
    extra = -(-extra // 16) * 16
    sds = jax.ShapeDtypeStruct
    block = pltpu.HBM((6 * vectors, width), BF16)
    small = sds((2 * vectors, 2 * vectors), F32)
    shapes, specs = [block], [HBM]
    if mode == "last":
        shapes += [small]
        specs += [VMEM]
    else:
        shapes += [
            sds((2 * vectors, 2 * size), F32),
            sds((wets, 2 * vectors), F32),
            sds((peers, wets // 2 + extra, 2 * vectors), BF16),
        ]
        specs += [VMEM] * 3
    if mode != "first":
        shapes += [sds((vectors, 2 * vectors), F32), small]
        specs += [VMEM, VMEM]
    scratch = [
        pltpu.VMEM((width // size + 2, vectors, size), BF16),
        pltpu.VMEM((6 * vectors, width), BF16),
        pltpu.VMEM((2 * vectors, width), F32) if mode == "first" else pltpu.VMEM((6 * vectors, width), BF16),
        pltpu.VMEM(mixed.shape if mode != "first" else (16, 128), BF16),
        pltpu.VMEM((2, spread.shape[0] // 2, spread.shape[1]) if mode != "last" else (16, 128), BF16),
        pltpu.VMEM((3 * vectors, 2 * size), F32),
        pltpu.SemaphoreType.DMA((6,)),
    ]
    if mode != "last":
        scratch += [pltpu.VMEM(small.shape, F32), pltpu.VMEM((peers, extra, 2 * vectors), F32)]
    if mode != "first":
        scratch += [pltpu.VMEM((vectors, 3 * vectors), F32), pltpu.VMEM((4 * vectors, 6 * vectors), BF16)]
    held = 2 if mode == "first" else 1
    return pl.pallas_call(
        functools.partial(advance_kernel, mode, total, peers),
        in_specs=[SMEM, SMEM] + [VMEM] * (len(state) - held) + [HBM] * held + [VMEM, VMEM, HBM, HBM],
        out_specs=specs,
        out_shape=shapes,
        scratch_shapes=scratch,
        compiler_params=pltpu.CompilerParams(vmem_limit_bytes=LIMIT),
        name="advance_" + mode,
    )(ids, rates, *state, pick, place, mixed, spread)


def route_kernel(vectors, wets, received, _lag, pressed, send, rest):
    peers = received.shape[0]
    glines = -(-2 * vectors // peers)
    hlines = -(-vectors // peers)
    pressed[...] = jnp.sum(received[:, :wets, :].astype(F32), 0)
    rest[...] = received[:, wets:, :].astype(F32)
    sums = jnp.sum(rest[...], 0)
    mine = sums[:glines] + sums[glines : 2 * glines] + sums[2 * glines : 3 * glines]
    edge = 3 * glines
    nothing = jnp.zeros((hlines, 2 * vectors), F32)

    def halo(t):
        if not 0 <= t < peers:
            return nothing
        return rest[t, edge : edge + hlines] + rest[t, edge + hlines : edge + 2 * hlines]

    send[...] = jnp.zeros(send.shape, F32)
    for t in range(peers):
        send[t, :glines] = mine
        send[t, glines : glines + hlines] = halo(t - 1)
        send[t, glines + hlines : glines + 2 * hlines] = halo(t + 1)


def route(vectors, wets, received, lag):
    peers, lines, lanes = received.shape
    return pl.pallas_call(
        functools.partial(route_kernel, vectors, wets),
        in_specs=[VMEM, VMEM],
        out_specs=[VMEM] * 2,
        out_shape=[
            jax.ShapeDtypeStruct((wets, 2 * vectors), F32),
            jax.ShapeDtypeStruct((peers, 8, 2 * vectors), F32),
        ],
        scratch_shapes=[pltpu.VMEM((peers, lines - wets, lanes), F32)],
        compiler_params=pltpu.CompilerParams(vmem_limit_bytes=LIMIT),
        name="route",
    )(received, lag)


def repeat_sum_kernel(received, _lag, send):
    mine = jnp.sum(received[...], 0)
    for t in range(send.shape[0]):
        send[t] = mine


def repeat_sum(received, lag):
    return pl.pallas_call(
        repeat_sum_kernel,
        in_specs=[VMEM, VMEM],
        out_specs=VMEM,
        out_shape=jax.ShapeDtypeStruct(received.shape, F32),
        compiler_params=pltpu.CompilerParams(vmem_limit_bytes=LIMIT),
        name="repeat_sum",
    )(received, lag)


def finish_kernel(total, gram, inner, lag, state, *refs):
    *earlier, out, coefs, factor_t, mix, weights, both, stack, fresh, sem = refs
    coef = coefs.at[len(earlier)]
    n = inner.shape[0]
    load = pltpu.make_async_copy(state, stack, sem)
    load.start()
    blend(total, gram, lag, both, mix)
    for k, known in enumerate(earlier):
        coefs[k] = known[...]
    put_weights(weights, mix[...], lag[:, :n])
    load.wait()

    def next_residual():
        mixture = jnp.dot(weights[...], stack[...], preferred_element_type=F32)
        fresh[...] = mixture[:n] + mixture[n:]

    inverse, _, _ = settle(total, gram, inner, lag, both, [next_residual], coef, factor_t)
    out[...] = exact(inverse, fresh[...])


def finish(total, gram, inner, lag, state, earlier):
    vectors, width = lag.shape[0], state.shape[1]
    return pl.pallas_call(
        functools.partial(finish_kernel, total),
        in_specs=[VMEM] * 3 + [HBM] + [VMEM] * len(earlier),
        out_specs=[VMEM] * 2,
        out_shape=[
            pltpu.HBM((vectors, width), F32),
            pltpu.HBM((len(earlier) + 1, 3, vectors, vectors), F32),
        ],
        scratch_shapes=[
            pltpu.VMEM((vectors, 2 * vectors), F32),
            pltpu.VMEM((vectors, 3 * vectors), F32),
            pltpu.VMEM((2 * vectors, 6 * vectors), BF16),
            pltpu.VMEM((vectors, 2 * vectors), F32),
            pltpu.VMEM((6 * vectors, width), BF16),
            pltpu.VMEM((vectors, width), F32),
            pltpu.SemaphoreType.DMA,
        ],
        compiler_params=pltpu.CompilerParams(vmem_limit_bytes=LIMIT),
        name="finish",
    )(gram, inner, lag, state, *earlier)


def local(n_row, n_col, start_block, struct_blocks, block_ids, rim_rows, wet_slots, wet_counts, added_mass, rates):
    peers = n_row * n_col
    vectors, width = start_block.shape
    total = float(width * peers)
    wcap = wet_slots.shape[0]
    wets = added_mass.shape[0] // n_row

    def exchange(parts):
        return lax.all_to_all(parts, AXES, 0, 0, tiled=True)

    def neighbours(halo):
        up = [(i, i + 1) for i in range(peers - 1)]
        down = [(i + 1, i) for i in range(peers - 1)]
        return lax.ppermute(halo, AXES, up), lax.ppermute(halo, AXES, down)

    def summed(gram, lag):
        lines = gram.shape[0] // peers
        return exchange(repeat_sum(exchange(gram.reshape(peers, lines, -1)), lag)).reshape(gram.shape)

    blocks = by_owner(in_hbm(added_mass), n_col, wcap)
    mass = lax.all_to_all(blocks, "col", 0, 0, tiled=True)
    mass = mass.reshape(n_col, n_row, 2, wets // 2, wcap)
    mixed, pick, place, halo = combine(
        rates, rim_rows[None, :], wet_slots[:wets, None], start_block, struct_blocks
    )
    below, above = neighbours(halo)
    slots = wet_slots[None, :]
    base, values = prepare(block_ids, wet_counts, slots, below, above, start_block, mixed)
    base = in_hbm(base)
    part = start_pressure(values, mass, base)
    spread = spread_mass(wet_counts, slots, mass, width)
    fixed = (in_hbm(mixed), pick, place, in_hbm(spread))
    arrived = exchange(part.reshape(peers, wets // 2, 2 * vectors))
    step = functools.partial(advance, total=total, peers=peers, ids=block_ids, rates=rates, fixed=fixed)
    state, edges, wet_held, send = step("first", state=(arrived, below, above, base, in_hbm(start_block)))
    inner = jnp.zeros((vectors, 2 * vectors), F32)
    unit = jnp.eye(vectors, dtype=F32)
    lag = jnp.concatenate([unit, unit], 1)
    coefficients = []
    for number in range(1, STEPS):
        pressed, again = route(vectors, wets // 2, exchange(send), lag)
        received = exchange(again)
        known = (received, pressed, lag, edges, wet_held, in_hbm(state))
        if number < STEPS - 1:
            state, edges, wet_held, send, both, gram = step("mid", state=known)
        else:
            state, products, both, gram = step("last", state=known)
        lag, inner, coef = factor(total, gram, inner, lag, both)
        coefficients.append(coef)
    final, coefs = finish(total, summed(products, lag), inner, lag, in_hbm(state), coefficients)
    return final, coefs


def solution(mesh):
    return jax.shard_map(
        functools.partial(local, mesh.shape["row"], mesh.shape["col"]),
        mesh=mesh,
        in_specs=(
            P(None, AXES),
            P(None, AXES, None, None, None),
            P(AXES, None),
            P(AXES),
            P(AXES),
            P(AXES),
            P("col", "row"),
            P(),
        ),
        out_specs=(P(None, AXES), P()),
        check_vma=False,
    )
```

```python
import functools

import jax
import jax.numpy as jnp
from jax import lax
from jax.experimental import pallas as pl
from jax.experimental.pallas import tpu as pltpu
from jax.sharding import PartitionSpec as P

STEPS = 6
AXES = ("row", "col")
VMEM = pl.BlockSpec(memory_space=pltpu.VMEM)
SMEM = pl.BlockSpec(memory_space=pltpu.SMEM)
HBM = pl.BlockSpec(memory_space=pltpu.HBM)
ANY = pl.BlockSpec(memory_space=pl.ANY)
F32 = jnp.float32
BF16 = jnp.bfloat16
LIMIT = 40 * 1024 * 1024


def exact(left, right):
    return lax.dot_general(
        left, right, (((1,), (0,)), ((), ())), precision=lax.Precision.HIGHEST, preferred_element_type=F32
    )


def exact_rows(left, right):
    return lax.dot_general(
        left, right, (((1,), (1,)), ((), ())), precision=lax.Precision.HIGHEST, preferred_element_type=F32
    )


def rows(left, right):
    return lax.dot_general(left, right, (((1,), (1,)), ((), ())), preferred_element_type=F32)


def in_hbm(values):
    return pltpu.with_memory_space_constraint(values, pltpu.HBM)


def halves(values):
    high = values.astype(BF16)
    return high, (values - high.astype(F32)).astype(BF16)


def by_owner_kernel(mass, out):
    out[0] = mass[...]


def by_owner(mass, n_col, wcap):
    size = mass.shape[0]
    return pl.pallas_call(
        by_owner_kernel,
        grid=(n_col,),
        in_specs=[pl.BlockSpec((size, wcap), lambda c: (0, c))],
        out_specs=pl.BlockSpec((1, size, wcap), lambda c: (c, 0, 0)),
        out_shape=jax.ShapeDtypeStruct((n_col, size, wcap), BF16),
        compiler_params=pltpu.CompilerParams(vmem_limit_bytes=LIMIT),
        name="by_owner",
    )(mass)


def combine_kernel(rates, rim, wet, start, blocks, mixed, pick, place, halo):
    size = blocks.shape[-1]
    for k in range(blocks.shape[2]):
        whole = (
            blocks[0, 0, k].astype(F32)
            + rates[0] * blocks[1, 0, k].astype(F32)
            - rates[1] * blocks[2, 0, k].astype(F32)
        ).T
        high = whole.astype(BF16)
        mixed[0, k * size : (k + 1) * size, :size] = high
        mixed[0, k * size : (k + 1) * size, size:] = (whole - high.astype(F32)).astype(BF16)

    @pl.when(pl.program_id(0) == 0)
    def _():
        index = lax.broadcasted_iota(jnp.int32, pick.shape, 0)
        pick[...] = jnp.where(index == rim[...], 1.0, 0.0).astype(BF16)
        index = lax.broadcasted_iota(jnp.int32, place.shape, 1)
        place[...] = jnp.where(index == wet[...], 1.0, 0.0).astype(BF16)
        high, low = halves(start[...])
        halo[...] = jnp.dot(high, pick[...], preferred_element_type=F32) + jnp.dot(
            low, pick[...], preferred_element_type=F32
        )


def combine(rates, rim, wet, start, blocks):
    _, count, nnz, size, _ = blocks.shape
    vectors, width = start.shape
    whole = lambda shape: pl.BlockSpec(shape, lambda i: (0,) * len(shape))
    return pl.pallas_call(
        combine_kernel,
        grid=(count,),
        in_specs=[
            SMEM,
            whole(rim.shape),
            whole(wet.shape),
            whole(start.shape),
            pl.BlockSpec((3, 1, nnz, size, size), lambda i: (0, i, 0, 0, 0)),
        ],
        out_specs=[
            pl.BlockSpec((1, nnz * size, 2 * size), lambda i: (i, 0, 0)),
            whole((width, rim.shape[1])),
            whole((wet.shape[0], width)),
            whole((vectors, rim.shape[1])),
        ],
        out_shape=[
            pltpu.HBM((count, nnz * size, 2 * size), BF16),
            jax.ShapeDtypeStruct((width, rim.shape[1]), BF16),
            jax.ShapeDtypeStruct((wet.shape[0], width), BF16),
            jax.ShapeDtypeStruct((vectors, rim.shape[1]), F32),
        ],
        compiler_params=pltpu.CompilerParams(vmem_limit_bytes=LIMIT),
        name="combine",
    )(rates, rim, wet, start, blocks)


def live_slots(count, slots):
    slot = lax.broadcasted_iota(jnp.int32, slots.shape, 1)
    return jnp.where(slot < count[0], slots[...], -1)


def chosen(first, shape, live):
    index = lax.broadcasted_iota(jnp.int32, shape, 0) + first
    return jnp.where(index == live, 1.0, 0.0).astype(BF16)


def start_pressure_kernel(values, mass, part):
    n_col, n_row, _, half, wcap = mass.shape
    size, vectors = n_col * half, values.shape[0]
    for r in range(n_row):
        for h in range(2):
            own = mass[:, r, h].reshape(size, wcap)
            pressed = rows(own, values[...]).astype(BF16)
            part[r * size : (r + 1) * size, h * vectors : (h + 1) * vectors] = pressed


def start_pressure(values, mass, base):
    n_col, n_row, _, half, _ = mass.shape
    return pl.pallas_call(
        lambda values, mass, _base, part: start_pressure_kernel(values, mass, part),
        in_specs=[VMEM, VMEM, HBM],
        out_specs=VMEM,
        out_shape=jax.ShapeDtypeStruct((n_col * n_row * half, 2 * values.shape[0]), BF16),
        compiler_params=pltpu.CompilerParams(vmem_limit_bytes=LIMIT),
        name="start_pressure",
    )(values, mass, base)


def spread_kernel(count, slots, mass, spread, own):
    n_col, n_row, _, half, wcap = mass.shape
    size = n_col * half

    @pl.when(pl.program_id(0) == 0)
    def _():
        for h in range(2):
            for r in range(n_row):
                first = (h * n_row + r) * size
                own[first : first + size] = mass[:, r, h].reshape(size, wcap)

    columns = spread.shape[1]
    onehot = chosen(pl.program_id(0) * columns, (columns, wcap), live_slots(count, slots))
    spread[...] = rows(own[...], onehot).astype(BF16)


def spread_mass(count, slots, mass, width):
    n_col, n_row, _, half, wcap = mass.shape
    size = n_col * n_row * half
    columns = min(width, 512)
    return pl.pallas_call(
        spread_kernel,
        grid=(width // columns,),
        in_specs=[
            SMEM,
            pl.BlockSpec(slots.shape, lambda i: (0, 0)),
            pl.BlockSpec(mass.shape, lambda i: (0,) * 5),
        ],
        out_specs=pl.BlockSpec((2 * size, columns), lambda i: (0, i)),
        out_shape=pltpu.HBM((2 * size, width), BF16),
        scratch_shapes=[pltpu.VMEM((2 * size, wcap), BF16)],
        compiler_params=pltpu.CompilerParams(vmem_limit_bytes=LIMIT),
        cost_estimate=pl.CostEstimate(
            flops=4 * size * wcap * width, bytes_accessed=4 * size * width, transcendentals=0
        ),
        name="spread",
    )(count, slots, mass)


def halve_columns(top, low, s):
    a, b, c = top[:, s : s + 1], top[:, s + 1 : s + 2], low[:, s + 1 : s + 2]
    scale = 1.0 / (a * c - b * b)
    return (c * top - b * low) * scale, (a * low - b * top) * scale


def eliminate(matrix, beside, coef, factor_t):
    n = matrix.shape[0]
    groups = n // 8
    row_id = lax.broadcasted_iota(jnp.int32, (n, 2 * n), 0)
    lane_id = lax.broadcasted_iota(jnp.int32, (n, 2 * n), 1)
    factor_t[...] = jnp.where(row_id + n == lane_id, 1.0, 0.0)
    factor_t[:, :n] = matrix
    sub = lax.broadcasted_iota(jnp.int32, (8, 1), 0)
    if beside:
        work = [factor_t[g * 8 : (g + 1) * 8, :] for g in range(groups)]
        done = 0
        for j in range(0, n, 2):
            g, s = divmod(j, 8)
            new_top, new_low = halve_columns(work[g][s : s + 1, :], work[g][s + 1 : s + 2, :], j)
            for i in range(g, groups):
                left, right = work[i][:, j : j + 1], work[i][:, j + 1 : j + 2]
                if i == g:
                    left = jnp.where(sub > s + 1, left, 0.0)
                    right = jnp.where(sub > s + 1, right, 0.0)
                work[i] = work[i] - (left * new_top + right * new_low)
            goal = len(beside) * (j + 2) // n
            while done < goal:
                beside[done]()
                done += 1
        reduced = jnp.concatenate(work, 0)
    else:

        def group(step, _):
            work = [factor_t[g * 8 : (g + 1) * 8, :] for g in range(groups)]
            for s in range(0, 8, 2):
                new_top, new_low = halve_columns(work[0][s : s + 1, :], work[0][s + 1 : s + 2, :], s)
                for i in range(groups):
                    left, right = work[i][:, s : s + 1], work[i][:, s + 1 : s + 2]
                    keep = sub > s + 1 if i == 0 else step + i < groups
                    update = left * new_top + right * new_low
                    work[i] = work[i] - jnp.where(keep, update, 0.0)
            for i in range(groups):
                target = (i - 1) % groups
                factor_t[target * 8 : (target + 1) * 8, :] = pltpu.roll(work[i], 2 * n - 8, 1)
            return 0

        lax.fori_loop(0, groups, group, 0)
        reduced = pltpu.roll(factor_t[...], n, 1)
    above = pltpu.roll(reduced, 1, 0)
    odd = lax.broadcasted_iota(jnp.int32, (n, 1), 0) % 2 == 1
    pick = lambda values, where: jnp.sum(jnp.where(where, values, 0.0), 1, keepdims=True)
    under = pick(above, lane_id == row_id) / jnp.where(odd, pick(above, lane_id + 1 == row_id), 1.0)
    reduced = reduced - jnp.where(odd, under, 0.0) * above
    diagonal = pick(reduced, lane_id == row_id)
    scale = lax.rsqrt(diagonal)
    scale = scale * (1.5 - 0.5 * diagonal * scale * scale)
    reduced = reduced * scale
    factor_t[...] = reduced
    upper = jnp.where(row_id <= lane_id, reduced, 0.0)
    coef[2] = upper.T[:n, :]
    return factor_t[:, n:]


def congruent(factor, matrix):
    return exact(factor, exact_rows(matrix, factor))


def settle(total, gram, inner, lag, both, beside, coef, factor_t):
    n = gram.shape[0] // 2
    scale = 1.0 / total
    pull = lag[:, :n]
    aa = congruent(pull, gram[:n, :n] * scale)
    cc = congruent(pull, gram[n:, n:] * scale)
    self_ = both[:, :n]
    prev = both[:, n:]
    cp = inner[:, :n]
    pp = inner[:, n:]
    coef[0] = self_
    coef[1] = prev
    t_c = self_ - exact(self_, cc) - exact_rows(prev, cp)
    t_p = prev - exact(self_, cp) - exact(prev, pp)
    t_a = aa - exact_rows(self_, self_) - exact_rows(prev, prev)
    matrix = t_a - exact_rows(t_c, self_) - exact_rows(t_p, prev)
    inverse = eliminate(0.5 * (matrix + matrix.T), beside, coef, factor_t)
    return inverse, t_c, cc


def put_weights(weights, mix, pull):
    n = mix.shape[0]
    high, low = halves(mix)
    pull_high, pull_low = halves(pull)
    for k in range(3):
        cut = slice(k * n, (k + 1) * n)
        weights[:n, 2 * k * n : (2 * k + 1) * n] = high[:, cut]
        weights[:n, (2 * k + 1) * n : (2 * k + 2) * n] = high[:, cut]
        weights[n : 2 * n, 2 * k * n : (2 * k + 1) * n] = low[:, cut]
        weights[n : 2 * n, (2 * k + 1) * n : (2 * k + 2) * n] = jnp.zeros((n, n), BF16)
    if weights.shape[0] > 2 * n:
        weights[2 * n :, :] = jnp.zeros((2 * n, 6 * n), BF16)
        weights[2 * n : 3 * n, 2 * n : 3 * n] = pull_high
        weights[2 * n : 3 * n, 3 * n : 4 * n] = pull_high
        weights[3 * n :, 2 * n : 3 * n] = pull_low


def blend(total, gram, lag, both, mix):
    n = gram.shape[0] // 2
    scale = 1.0 / total
    pull, square = lag[:, :n], lag[:, n:]
    crossed = gram[:n, n:] * scale
    prev = exact(pull, gram[n:, :n] * scale)
    mix[:, :n] = pull
    mix[:, n : 2 * n] = -exact(pull, exact(crossed, square))
    mix[:, 2 * n :] = -prev
    both[:, :n] = congruent(pull, crossed)
    both[:, n:] = prev


def factor_kernel(total, gram, inner, lag, both, lag_out, inner_out, coef, factor_t):
    n = gram.shape[0] // 2
    inverse, t_c, cc = settle(total, gram, inner, lag, both, [], coef, factor_t)
    lag_out[:, :n] = inverse
    lag_out[:, n:] = exact(inverse.T, inverse)
    inner_out[:, :n] = exact(inverse, t_c)
    inner_out[:, n:] = cc


def factor(total, gram, inner, lag, both):
    n = gram.shape[0] // 2
    sds = jax.ShapeDtypeStruct
    return pl.pallas_call(
        functools.partial(factor_kernel, total),
        in_specs=[VMEM] * 4,
        out_specs=[VMEM] * 3,
        out_shape=[sds((n, 2 * n), F32), sds((n, 2 * n), F32), sds((3, n, n), F32)],
        scratch_shapes=[pltpu.VMEM((n, 2 * n), F32)],
        compiler_params=pltpu.CompilerParams(vmem_limit_bytes=LIMIT),
        cost_estimate=pl.CostEstimate(flops=100_000_000, bytes_accessed=10_000_000, transcendentals=0),
        name="factor",
    )(gram, inner, lag, both)


def thirds(values):
    high = values.astype(BF16)
    rest = values - high.astype(F32)
    return jnp.concatenate([high, *halves(rest)], 0)


def unpack(lines, received, target, lanes, offset):
    for s in range(received.shape[0]):
        if s * lines < target.shape[0]:
            target[s * lines : (s + 1) * lines, lanes] = received[s, offset : offset + lines]


def place_columns(extended, block, edge):
    size = extended.shape[2]
    count = extended.shape[0] - 2
    for i in range(count):
        extended[i] = block[:, i * size : (i + 1) * size]
    extended[count] = edge[:, :size].astype(BF16)
    extended[count + 1] = edge[:, size:].astype(BF16)


def block_row(ids, extended, mixed, i):
    picked = jnp.concatenate([extended[ids[i, k]] for k in range(ids.shape[1])], 1)
    pair = jnp.dot(picked, mixed[i], preferred_element_type=F32)
    size = pair.shape[1] // 2
    return pair[:, :size] + pair[:, size:]


def prepare_kernel(ids, count, slots, below, above, start, mixed, out, values, extended):
    size = below.shape[1]
    block = start[...].astype(BF16)
    place_columns(extended, block, jnp.concatenate([below[...], above[...]], 1))
    for i in range(out.shape[1] // size):
        out[:, i * size : (i + 1) * size] = block_row(ids, extended, mixed, i)
    live = live_slots(count, slots)
    columns = min(out.shape[1], 512)
    total = jnp.zeros(values.shape, F32)
    for first in range(0, out.shape[1], columns):
        picked = chosen(first, (columns, slots.shape[1]), live)
        total = total + jnp.dot(block[:, first : first + columns], picked, preferred_element_type=F32)
    values[...] = total.astype(BF16)


def prepare(ids, count, slots, below, above, start, mixed):
    vectors, width = start.shape
    size = below.shape[1]
    return pl.pallas_call(
        prepare_kernel,
        in_specs=[SMEM, SMEM] + [VMEM] * 5,
        out_specs=[VMEM] * 2,
        out_shape=[
            pltpu.HBM((vectors, width), F32),
            jax.ShapeDtypeStruct((vectors, slots.shape[1]), BF16),
        ],
        scratch_shapes=[pltpu.VMEM((width // size + 2, vectors, size), BF16)],
        compiler_params=pltpu.CompilerParams(vmem_limit_bytes=LIMIT),
        name="prepare",
    )(ids, count, slots, below, above, start, mixed)


def advance_kernel(mode, total, peers, *refs):
    it = iter(refs)
    take = lambda k: [next(it) for _ in range(k)]
    ids, rates = take(2)
    if mode == "first":
        arrived, below, above = take(3)
        held = take(2)
    else:
        received, pressed, lag, edges, wet_held = take(5)
        held = take(1)
    pick, place, mixed_in, spread_in = take(4)
    (state_out,) = take(1)
    if mode == "last":
        (gram_s,) = take(1)
    else:
        edges_out, wet_out, send = take(3)
    if mode != "first":
        both, gram_in = take(2)
    extended, terms, stack, mixed, spread, edge_in, sems = take(7)
    if mode != "last":
        gram_s, rest = take(2)
    if mode != "first":
        mix, weights = take(2)

    n = terms.shape[0] // 6
    width = terms.shape[1]
    size = edge_in.shape[1] // 2
    count = width // size
    glines = -(-2 * n // peers)
    hlines = -(-n // peers)
    loads = []
    for k, source in enumerate(held):
        target = stack.at[pl.ds(k * n, n)] if mode == "first" else stack
        loads.append(pltpu.make_async_copy(source, target, sems.at[k]))
        loads[-1].start()
    if mode != "first":
        load_mixed = pltpu.make_async_copy(mixed_in, mixed, sems.at[3])
        load_mixed.start()
    load_spread = []
    if mode != "last":
        for h in range(2):
            part = spread_in.at[pl.ds(h * spread.shape[1], spread.shape[1])]
            load_spread.append(pltpu.make_async_copy(part, spread.at[h], sems.at[4 + h]))
            load_spread[-1].start()

    if mode == "first":
        edge = jnp.concatenate([below[...], above[...]], 1)
        summed = jnp.sum(arrived[...].astype(F32), 0)
        wet = jnp.concatenate([summed[:, :n], summed[:, n:]], 0)
        edges_out[:n, :] = edge
        edges_out[n:, :] = jnp.zeros_like(edge)
        wet_out[:, :n] = wet
        wet_out[:, n:] = jnp.zeros_like(wet)
        for copy in loads:
            copy.wait()
        residual = stack[n : 2 * n, :]
        terms[4 * n :, :] = jnp.zeros((2 * n, width), BF16)
    else:
        unpack(glines, received, gram_in, slice(None), 0)
        unpack(hlines, received, edge_in.at[pl.ds(0, n)], slice(0, size), glines)
        unpack(hlines, received, edge_in.at[pl.ds(0, n)], slice(size, 2 * size), glines + hlines)
        edge_in[n:, :] = edges[...]
        blend(total, gram_in, lag, both, mix)
        pull = lag[:, :n]
        put_weights(weights, mix[...], pull)
        edge = exact(mix[...], edge_in[...])
        summed = pressed[...]
        wet = exact_rows(jnp.concatenate([summed[:, :n], summed[:, n:]], 0), pull)
        wet = wet + exact_rows(wet_held[...], mix[:, n:])
        if mode != "last":
            edges_out[:n, :] = edge
            edges_out[n:, :] = exact(pull, edges[:n, :])
            wet_out[:, :n] = wet
            wet_out[:, n:] = exact_rows(wet_held[:, :n], pull)
        for copy in loads:
            copy.wait()
        mixture = jnp.dot(weights[...], stack[...], preferred_element_type=F32)
        residual = mixture[:n] + mixture[n : 2 * n]
        terms[4 * n : 5 * n, :], terms[5 * n :, :] = halves(mixture[2 * n : 3 * n] + mixture[3 * n :])
    high, low = halves(residual)
    terms[2 * n : 3 * n, :] = high
    terms[3 * n : 4 * n, :] = low
    force = thirds(wet.T * rates[1])
    if mode != "first":
        place_columns(extended, high, edge)
        load_mixed.wait()
    for i in range(count):
        lanes = slice(i * size, (i + 1) * size)
        added = jnp.dot(force, place[:, lanes], preferred_element_type=F32)
        applied = stack[:n, lanes] if mode == "first" else block_row(ids, extended, mixed, i)
        applied = applied - (added[:n] + added[n : 2 * n] + added[2 * n :])
        terms[:n, lanes], terms[n : 2 * n, lanes] = halves(applied)
    store = pltpu.make_async_copy(terms, state_out, sems.at[2])
    store.start()

    known = 4 * n if mode == "first" else 6 * n
    products = rows(terms[: 2 * n, :], terms[:known, :])
    products = products[:n] + products[n:]
    gram_s[:n, :n] = products[:, :n] + products[:, n : 2 * n]
    gram_s[:n, n:] = products[:, 2 * n : 3 * n] + products[:, 3 * n : 4 * n]
    if mode == "first":
        gram_s[n:, :n] = jnp.zeros((n, n), F32)
    else:
        gram_s[n:, :n] = products[:, 4 * n : 5 * n] + products[:, 5 * n :]
    squares = rows(terms[2 * n : 4 * n, :], terms[2 * n : 4 * n, :])
    squares = squares[:n] + squares[n:]
    gram_s[n:, n:] = squares[:, :n] + squares[:, n:]
    if mode != "last":
        rim = jnp.dot(terms[: 2 * n, :], pick[...], preferred_element_type=F32)
        edge_in[:n, :size] = rim[:n] + rim[n:]
        wets = wet_out.shape[0] // 2
        for copy in load_spread:
            copy.wait()
        tops = rows(spread[0], terms[: 2 * n, :])
        tops = tops + pltpu.roll(tops, n, 1)
        ends = rows(spread[1], terms[: 2 * n, :])
        ends = ends + pltpu.roll(ends, n, 1)
        lane = lax.broadcasted_iota(jnp.int32, tops.shape, 1)
        send[:, :wets, :] = jnp.where(lane < n, tops, ends).astype(BF16).reshape(peers, wets, 2 * n)
        left = gram_s[...]
        offset = 0
        for _ in range(3):
            term = left.astype(BF16).astype(F32)
            left = left - term
            gram_s[...] = term
            for d in range(peers):
                if d * glines < 2 * n:
                    rest[d, offset : offset + glines] = gram_s[d * glines : (d + 1) * glines, :]
            offset += glines
        left = edge_in[:n, :size]
        for _ in range(2):
            term = left.astype(BF16).astype(F32)
            left = left - term
            edge_in[:n, :size] = term
            for d in range(peers):
                if d * hlines < n:
                    rest[d, offset : offset + hlines] = edge_in[d * hlines : (d + 1) * hlines, :size]
                else:
                    rest[d, offset : offset + hlines] = jnp.zeros((hlines, size), F32)
            offset += hlines
        if offset < rest.shape[1]:
            rest[:, offset:, :] = jnp.zeros((peers, rest.shape[1] - offset, 2 * n), F32)
        send[:, wets:, :] = rest[...].astype(BF16)
    store.wait()


def advance(mode, total, peers, ids, rates, state, fixed):
    mixed, pick, place, spread = fixed
    width, size = pick.shape
    wets = place.shape[0]
    vectors = state[3].shape[0] if mode == "first" else state[2].shape[0]
    extra = 3 * -(-2 * vectors // peers) + 2 * -(-vectors // peers)
    extra = -(-extra // 16) * 16
    sds = jax.ShapeDtypeStruct
    block = pltpu.HBM((6 * vectors, width), BF16)
    small = sds((2 * vectors, 2 * vectors), F32)
    shapes, specs = [block], [HBM]
    if mode == "last":
        shapes += [small]
        specs += [VMEM]
    else:
        shapes += [
            sds((2 * vectors, 2 * size), F32),
            sds((wets, 2 * vectors), F32),
            sds((peers, wets // 2 + extra, 2 * vectors), BF16),
        ]
        specs += [VMEM] * 3
    if mode != "first":
        shapes += [sds((vectors, 2 * vectors), F32), small]
        specs += [VMEM, VMEM]
    scratch = [
        pltpu.VMEM((width // size + 2, vectors, size), BF16),
        pltpu.VMEM((6 * vectors, width), BF16),
        pltpu.VMEM((2 * vectors, width), F32) if mode == "first" else pltpu.VMEM((6 * vectors, width), BF16),
        pltpu.VMEM(mixed.shape if mode != "first" else (16, 128), BF16),
        pltpu.VMEM((2, spread.shape[0] // 2, spread.shape[1]) if mode != "last" else (16, 128), BF16),
        pltpu.VMEM((3 * vectors, 2 * size), F32),
        pltpu.SemaphoreType.DMA((6,)),
    ]
    if mode != "last":
        scratch += [pltpu.VMEM(small.shape, F32), pltpu.VMEM((peers, extra, 2 * vectors), F32)]
    if mode != "first":
        scratch += [pltpu.VMEM((vectors, 3 * vectors), F32), pltpu.VMEM((4 * vectors, 6 * vectors), BF16)]
    held = 2 if mode == "first" else 1
    return pl.pallas_call(
        functools.partial(advance_kernel, mode, total, peers),
        in_specs=[SMEM, SMEM] + [VMEM] * (len(state) - held) + [HBM] * held + [VMEM, VMEM, HBM, HBM],
        out_specs=specs,
        out_shape=shapes,
        scratch_shapes=scratch,
        compiler_params=pltpu.CompilerParams(vmem_limit_bytes=LIMIT),
        name="advance_" + mode,
    )(ids, rates, *state, pick, place, mixed, spread)


def route_kernel(vectors, wets, received, _lag, pressed, send, rest):
    peers = received.shape[0]
    glines = -(-2 * vectors // peers)
    hlines = -(-vectors // peers)
    pressed[...] = jnp.sum(received[:, :wets, :].astype(F32), 0)
    rest[...] = received[:, wets:, :].astype(F32)
    sums = jnp.sum(rest[...], 0)
    mine = sums[:glines] + sums[glines : 2 * glines] + sums[2 * glines : 3 * glines]
    edge = 3 * glines
    nothing = jnp.zeros((hlines, 2 * vectors), F32)

    def halo(t):
        if not 0 <= t < peers:
            return nothing
        return rest[t, edge : edge + hlines] + rest[t, edge + hlines : edge + 2 * hlines]

    send[...] = jnp.zeros(send.shape, F32)
    for t in range(peers):
        send[t, :glines] = mine
        send[t, glines : glines + hlines] = halo(t - 1)
        send[t, glines + hlines : glines + 2 * hlines] = halo(t + 1)


def route(vectors, wets, received, lag):
    peers, lines, lanes = received.shape
    return pl.pallas_call(
        functools.partial(route_kernel, vectors, wets),
        in_specs=[VMEM, VMEM],
        out_specs=[VMEM] * 2,
        out_shape=[
            jax.ShapeDtypeStruct((wets, 2 * vectors), F32),
            jax.ShapeDtypeStruct((peers, 8, 2 * vectors), F32),
        ],
        scratch_shapes=[pltpu.VMEM((peers, lines - wets, lanes), F32)],
        compiler_params=pltpu.CompilerParams(vmem_limit_bytes=LIMIT),
        name="route",
    )(received, lag)


def repeat_sum_kernel(received, _lag, send):
    mine = jnp.sum(received[...], 0)
    for t in range(send.shape[0]):
        send[t] = mine


def repeat_sum(received, lag):
    return pl.pallas_call(
        repeat_sum_kernel,
        in_specs=[VMEM, VMEM],
        out_specs=VMEM,
        out_shape=jax.ShapeDtypeStruct(received.shape, F32),
        compiler_params=pltpu.CompilerParams(vmem_limit_bytes=LIMIT),
        name="repeat_sum",
    )(received, lag)


def finish_kernel(total, gram, inner, lag, state, *refs):
    *earlier, out, coefs, factor_t, mix, weights, both, stack, fresh, sem = refs
    coef = coefs.at[len(earlier)]
    n = inner.shape[0]
    load = pltpu.make_async_copy(state, stack, sem)
    load.start()
    blend(total, gram, lag, both, mix)
    for k, known in enumerate(earlier):
        coefs[k] = known[...]
    put_weights(weights, mix[...], lag[:, :n])
    load.wait()

    def next_residual():
        mixture = jnp.dot(weights[...], stack[...], preferred_element_type=F32)
        fresh[...] = mixture[:n] + mixture[n:]

    inverse, _, _ = settle(total, gram, inner, lag, both, [next_residual], coef, factor_t)
    out[...] = exact(inverse, fresh[...])


def finish(total, gram, inner, lag, state, earlier):
    vectors, width = lag.shape[0], state.shape[1]
    return pl.pallas_call(
        functools.partial(finish_kernel, total),
        in_specs=[VMEM] * 3 + [HBM] + [VMEM] * len(earlier),
        out_specs=[VMEM] * 2,
        out_shape=[
            pltpu.HBM((vectors, width), F32),
            pltpu.HBM((len(earlier) + 1, 3, vectors, vectors), F32),
        ],
        scratch_shapes=[
            pltpu.VMEM((vectors, 2 * vectors), F32),
            pltpu.VMEM((vectors, 3 * vectors), F32),
            pltpu.VMEM((2 * vectors, 6 * vectors), BF16),
            pltpu.VMEM((vectors, 2 * vectors), F32),
            pltpu.VMEM((6 * vectors, width), BF16),
            pltpu.VMEM((vectors, width), F32),
            pltpu.SemaphoreType.DMA,
        ],
        compiler_params=pltpu.CompilerParams(vmem_limit_bytes=LIMIT),
        name="finish",
    )(gram, inner, lag, state, *earlier)


def local(n_row, n_col, start_block, struct_blocks, block_ids, rim_rows, wet_slots, wet_counts, added_mass, rates):
    peers = n_row * n_col
    vectors, width = start_block.shape
    total = float(width * peers)
    wcap = wet_slots.shape[0]
    wets = added_mass.shape[0] // n_row

    def exchange(parts):
        return lax.all_to_all(parts, AXES, 0, 0, tiled=True)

    def neighbours(halo):
        up = [(i, i + 1) for i in range(peers - 1)]
        down = [(i + 1, i) for i in range(peers - 1)]
        return lax.ppermute(halo, AXES, up), lax.ppermute(halo, AXES, down)

    def summed(gram, lag):
        lines = gram.shape[0] // peers
        return exchange(repeat_sum(exchange(gram.reshape(peers, lines, -1)), lag)).reshape(gram.shape)

    blocks = by_owner(added_mass, n_col, wcap)
    mass = lax.all_to_all(blocks, "col", 0, 0, tiled=True)
    mass = mass.reshape(n_col, n_row, 2, wets // 2, wcap)
    mixed, pick, place, halo = combine(
        rates, rim_rows[None, :], wet_slots[:wets, None], start_block, struct_blocks
    )
    below, above = neighbours(halo)
    slots = wet_slots[None, :]
    base, values = prepare(block_ids, wet_counts, slots, below, above, start_block, mixed)
    base = in_hbm(base)
    part = start_pressure(values, mass, base)
    spread = spread_mass(wet_counts, slots, mass, width)
    fixed = (in_hbm(mixed), pick, place, in_hbm(spread))
    arrived = exchange(part.reshape(peers, wets // 2, 2 * vectors))
    step = functools.partial(advance, total=total, peers=peers, ids=block_ids, rates=rates, fixed=fixed)
    state, edges, wet_held, send = step("first", state=(arrived, below, above, base, in_hbm(start_block)))
    inner = jnp.zeros((vectors, 2 * vectors), F32)
    unit = jnp.eye(vectors, dtype=F32)
    lag = jnp.concatenate([unit, unit], 1)
    coefficients = []
    for number in range(1, STEPS):
        pressed, again = route(vectors, wets // 2, exchange(send), lag)
        received = exchange(again)
        known = (received, pressed, lag, edges, wet_held, in_hbm(state))
        if number < STEPS - 1:
            state, edges, wet_held, send, both, gram = step("mid", state=known)
        else:
            state, products, both, gram = step("last", state=known)
        lag, inner, coef = factor(total, gram, inner, lag, both)
        coefficients.append(coef)
    final, coefs = finish(total, summed(products, lag), inner, lag, in_hbm(state), coefficients)
    return final, coefs


def solution(mesh):
    return jax.shard_map(
        functools.partial(local, mesh.shape["row"], mesh.shape["col"]),
        mesh=mesh,
        in_specs=(
            P(None, AXES),
            P(None, AXES, None, None, None),
            P(AXES, None),
            P(AXES),
            P(AXES),
            P(AXES),
            P("col", "row"),
            P(),
        ),
        out_specs=(P(None, AXES), P()),
        check_vma=False,
    )
```

```python
import functools

import jax
import jax.numpy as jnp
from jax import lax
from jax.experimental import pallas as pl
from jax.experimental.pallas import tpu as pltpu
from jax.sharding import PartitionSpec as P

STEPS = 6
AXES = ("row", "col")
VMEM = pl.BlockSpec(memory_space=pltpu.VMEM)
SMEM = pl.BlockSpec(memory_space=pltpu.SMEM)
HBM = pl.BlockSpec(memory_space=pltpu.HBM)
ANY = pl.BlockSpec(memory_space=pl.ANY)
F32 = jnp.float32
BF16 = jnp.bfloat16
LIMIT = 40 * 1024 * 1024


def exact(left, right):
    return lax.dot_general(
        left, right, (((1,), (0,)), ((), ())), precision=lax.Precision.HIGHEST, preferred_element_type=F32
    )


def exact_rows(left, right):
    return lax.dot_general(
        left, right, (((1,), (1,)), ((), ())), precision=lax.Precision.HIGHEST, preferred_element_type=F32
    )


def rows(left, right):
    return lax.dot_general(left, right, (((1,), (1,)), ((), ())), preferred_element_type=F32)


def in_hbm(values):
    return pltpu.with_memory_space_constraint(values, pltpu.HBM)


def halves(values):
    high = values.astype(BF16)
    return high, (values - high.astype(F32)).astype(BF16)


def by_owner_kernel(mass, out):
    out[0] = mass[...]


def by_owner(mass, n_col, wcap):
    size = mass.shape[0]
    return pl.pallas_call(
        by_owner_kernel,
        grid=(n_col,),
        in_specs=[pl.BlockSpec((size, wcap), lambda c: (0, c))],
        out_specs=pl.BlockSpec((1, size, wcap), lambda c: (c, 0, 0)),
        out_shape=jax.ShapeDtypeStruct((n_col, size, wcap), BF16),
        compiler_params=pltpu.CompilerParams(vmem_limit_bytes=LIMIT),
        name="by_owner",
    )(mass)


def combine_kernel(rates, rim, wet, start, blocks, mixed, pick, place, halo):
    size = blocks.shape[-1]
    for k in range(blocks.shape[2]):
        whole = (
            blocks[0, 0, k].astype(F32)
            + rates[0] * blocks[1, 0, k].astype(F32)
            - rates[1] * blocks[2, 0, k].astype(F32)
        ).T
        high = whole.astype(BF16)
        mixed[0, k * size : (k + 1) * size, :size] = high
        mixed[0, k * size : (k + 1) * size, size:] = (whole - high.astype(F32)).astype(BF16)

    @pl.when(pl.program_id(0) == 0)
    def _():
        index = lax.broadcasted_iota(jnp.int32, pick.shape, 0)
        pick[...] = jnp.where(index == rim[...], 1.0, 0.0).astype(BF16)
        index = lax.broadcasted_iota(jnp.int32, place.shape, 1)
        place[...] = jnp.where(index == wet[...], 1.0, 0.0).astype(BF16)
        high, low = halves(start[...])
        halo[...] = jnp.dot(high, pick[...], preferred_element_type=F32) + jnp.dot(
            low, pick[...], preferred_element_type=F32
        )


def combine(rates, rim, wet, start, blocks):
    _, count, nnz, size, _ = blocks.shape
    vectors, width = start.shape
    whole = lambda shape: pl.BlockSpec(shape, lambda i: (0,) * len(shape))
    return pl.pallas_call(
        combine_kernel,
        grid=(count,),
        in_specs=[
            SMEM,
            whole(rim.shape),
            whole(wet.shape),
            whole(start.shape),
            pl.BlockSpec((3, 1, nnz, size, size), lambda i: (0, i, 0, 0, 0)),
        ],
        out_specs=[
            pl.BlockSpec((1, nnz * size, 2 * size), lambda i: (i, 0, 0)),
            whole((width, rim.shape[1])),
            whole((wet.shape[0], width)),
            whole((vectors, rim.shape[1])),
        ],
        out_shape=[
            pltpu.HBM((count, nnz * size, 2 * size), BF16),
            jax.ShapeDtypeStruct((width, rim.shape[1]), BF16),
            jax.ShapeDtypeStruct((wet.shape[0], width), BF16),
            jax.ShapeDtypeStruct((vectors, rim.shape[1]), F32),
        ],
        compiler_params=pltpu.CompilerParams(vmem_limit_bytes=LIMIT),
        name="combine",
    )(rates, rim, wet, start, blocks)


def live_slots(count, slots):
    slot = lax.broadcasted_iota(jnp.int32, slots.shape, 1)
    return jnp.where(slot < count[0], slots[...], -1)


def chosen(first, shape, live):
    index = lax.broadcasted_iota(jnp.int32, shape, 0) + first
    return jnp.where(index == live, 1.0, 0.0).astype(BF16)


def start_pressure_kernel(values, mass, part):
    n_col, n_row, _, half, wcap = mass.shape
    size, vectors = n_col * half, values.shape[0]
    for r in range(n_row):
        for h in range(2):
            own = mass[:, r, h].reshape(size, wcap)
            pressed = rows(own, values[...]).astype(BF16)
            part[r * size : (r + 1) * size, h * vectors : (h + 1) * vectors] = pressed


def start_pressure(values, mass, base):
    n_col, n_row, _, half, _ = mass.shape
    return pl.pallas_call(
        lambda values, mass, _base, part: start_pressure_kernel(values, mass, part),
        in_specs=[VMEM, VMEM, HBM],
        out_specs=VMEM,
        out_shape=jax.ShapeDtypeStruct((n_col * n_row * half, 2 * values.shape[0]), BF16),
        compiler_params=pltpu.CompilerParams(vmem_limit_bytes=LIMIT),
        name="start_pressure",
    )(values, mass, base)


def spread_kernel(count, slots, mass, spread, own):
    n_col, n_row, _, half, wcap = mass.shape
    size = n_col * half

    @pl.when(pl.program_id(0) == 0)
    def _():
        for h in range(2):
            for r in range(n_row):
                first = (h * n_row + r) * size
                own[first : first + size] = mass[:, r, h].reshape(size, wcap)

    columns = spread.shape[1]
    onehot = chosen(pl.program_id(0) * columns, (columns, wcap), live_slots(count, slots))
    spread[...] = rows(own[...], onehot).astype(BF16)


def spread_mass(count, slots, mass, width):
    n_col, n_row, _, half, wcap = mass.shape
    size = n_col * n_row * half
    columns = min(width, 512)
    return pl.pallas_call(
        spread_kernel,
        grid=(width // columns,),
        in_specs=[
            SMEM,
            pl.BlockSpec(slots.shape, lambda i: (0, 0)),
            pl.BlockSpec(mass.shape, lambda i: (0,) * 5),
        ],
        out_specs=pl.BlockSpec((2 * size, columns), lambda i: (0, i)),
        out_shape=pltpu.HBM((2 * size, width), BF16),
        scratch_shapes=[pltpu.VMEM((2 * size, wcap), BF16)],
        compiler_params=pltpu.CompilerParams(vmem_limit_bytes=LIMIT),
        cost_estimate=pl.CostEstimate(
            flops=4 * size * wcap * width, bytes_accessed=4 * size * width, transcendentals=0
        ),
        name="spread",
    )(count, slots, mass)


def pivot_rows(top, s):
    lanes = top[0].shape[1]
    at = lambda i, j: jnp.broadcast_to(top[i][:, s + j : s + j + 1], (1, lanes))
    a, b, c = at(0, 0), at(0, 1), at(1, 1)
    p2, q2, p3, q3 = at(2, 0), at(2, 1), at(3, 0), at(3, 1)
    d22, d23, d33 = at(2, 2), at(2, 3), at(3, 3)
    scale = 1.0 / (a * c - b * b)
    first = ((c * top[0] - b * top[1]) * scale, (a * top[1] - b * top[0]) * scale)
    y02, y03 = (c * p2 - b * q2) * scale, (c * p3 - b * q3) * scale
    y12, y13 = (a * q2 - b * p2) * scale, (a * q3 - b * p3) * scale
    a2 = d22 - p2 * y02 - q2 * y12
    b2 = d23 - p2 * y03 - q2 * y13
    c2 = d33 - p3 * y03 - q3 * y13
    scale2 = 1.0 / (a2 * c2 - b2 * b2)
    third = top[2] - p2 * first[0] - q2 * first[1]
    fourth = top[3] - p3 * first[0] - q3 * first[1]
    v2 = (c2 * third - b2 * fourth) * scale2
    v3 = (a2 * fourth - b2 * third) * scale2
    v0 = first[0] - y02 * v2 - y03 * v3
    v1 = first[1] - y12 * v2 - y13 * v3
    return first, (v0, v1, v2, v3)


def eliminate_four(work, s, j, keep):
    sub = lax.broadcasted_iota(jnp.int32, (8, 1), 0)
    first, full = pivot_rows([work[0][s + k : s + k + 1, :] for k in range(4)], j)
    out = []
    for i, group in enumerate(work):
        columns = [group[:, j + k : j + k + 1] for k in range(4)]
        half = columns[0] * full[0] + columns[1] * full[1]
        update = half + (columns[2] * full[2] + columns[3] * full[3])
        if i == 0:
            pair = columns[0] * first[0] + columns[1] * first[1]
            update = jnp.where(sub > s + 3, update, jnp.where(sub > s + 1, pair, 0.0))
        elif keep is not None:
            update = jnp.where(keep(i), update, 0.0)
        out.append(group - update)
    return out


def eliminate(matrix, beside, coef, factor_t):
    n = matrix.shape[0]
    groups = n // 8
    row_id = lax.broadcasted_iota(jnp.int32, (n, 2 * n), 0)
    lane_id = lax.broadcasted_iota(jnp.int32, (n, 2 * n), 1)
    factor_t[...] = jnp.where(row_id + n == lane_id, 1.0, 0.0)
    factor_t[:, :n] = matrix
    if beside:
        work = [factor_t[g * 8 : (g + 1) * 8, :] for g in range(groups)]
        done = 0
        for j in range(0, n, 4):
            g, s = divmod(j, 8)
            work[g:] = eliminate_four(work[g:], s, j, None)
            goal = len(beside) * (j + 4) // n
            while done < goal:
                beside[done]()
                done += 1
        reduced = jnp.concatenate(work, 0)
    else:

        def group(step, _):
            work = [factor_t[g * 8 : (g + 1) * 8, :] for g in range(groups)]
            for s in range(0, 8, 4):
                work = eliminate_four(work, s, s, lambda i: step + i < groups)
            for i in range(groups):
                target = (i - 1) % groups
                factor_t[target * 8 : (target + 1) * 8, :] = pltpu.roll(work[i], 2 * n - 8, 1)
            return 0

        lax.fori_loop(0, groups, group, 0)
        reduced = pltpu.roll(factor_t[...], n, 1)
    above = pltpu.roll(reduced, 1, 0)
    odd = lax.broadcasted_iota(jnp.int32, (n, 1), 0) % 2 == 1
    pick = lambda values, where: jnp.sum(jnp.where(where, values, 0.0), 1, keepdims=True)
    under = pick(above, lane_id == row_id) / jnp.where(odd, pick(above, lane_id + 1 == row_id), 1.0)
    reduced = reduced - jnp.where(odd, under, 0.0) * above
    diagonal = pick(reduced, lane_id == row_id)
    scale = lax.rsqrt(diagonal)
    scale = scale * (1.5 - 0.5 * diagonal * scale * scale)
    reduced = reduced * scale
    factor_t[...] = reduced
    upper = jnp.where(row_id <= lane_id, reduced, 0.0)
    coef[2] = upper.T[:n, :]
    return factor_t[:, n:]


def congruent(factor, matrix):
    return exact(factor, exact_rows(matrix, factor))


def settle(total, gram, inner, lag, both, beside, coef, factor_t):
    n = gram.shape[0] // 2
    scale = 1.0 / total
    pull = lag[:, :n]
    aa = congruent(pull, gram[:n, :n] * scale)
    cc = congruent(pull, gram[n:, n:] * scale)
    self_ = both[:, :n]
    prev = both[:, n:]
    cp = inner[:, :n]
    pp = inner[:, n:]
    coef[0] = self_
    coef[1] = prev
    t_c = self_ - exact(self_, cc) - exact_rows(prev, cp)
    t_p = prev - exact(self_, cp) - exact(prev, pp)
    t_a = aa - exact_rows(self_, self_) - exact_rows(prev, prev)
    matrix = t_a - exact_rows(t_c, self_) - exact_rows(t_p, prev)
    inverse = eliminate(0.5 * (matrix + matrix.T), beside, coef, factor_t)
    return inverse, t_c, cc


def put_weights(weights, mix, pull):
    n = mix.shape[0]
    high, low = halves(mix)
    pull_high, pull_low = halves(pull)
    for k in range(3):
        cut = slice(k * n, (k + 1) * n)
        weights[:n, 2 * k * n : (2 * k + 1) * n] = high[:, cut]
        weights[:n, (2 * k + 1) * n : (2 * k + 2) * n] = high[:, cut]
        weights[n : 2 * n, 2 * k * n : (2 * k + 1) * n] = low[:, cut]
        weights[n : 2 * n, (2 * k + 1) * n : (2 * k + 2) * n] = jnp.zeros((n, n), BF16)
    if weights.shape[0] > 2 * n:
        weights[2 * n :, :] = jnp.zeros((2 * n, 6 * n), BF16)
        weights[2 * n : 3 * n, 2 * n : 3 * n] = pull_high
        weights[2 * n : 3 * n, 3 * n : 4 * n] = pull_high
        weights[3 * n :, 2 * n : 3 * n] = pull_low


def blend(total, gram, lag, both, mix):
    n = gram.shape[0] // 2
    scale = 1.0 / total
    pull, square = lag[:, :n], lag[:, n:]
    crossed = gram[:n, n:] * scale
    prev = exact(pull, gram[n:, :n] * scale)
    mix[:, :n] = pull
    mix[:, n : 2 * n] = -exact(pull, exact(crossed, square))
    mix[:, 2 * n :] = -prev
    both[:, :n] = congruent(pull, crossed)
    both[:, n:] = prev


def factor_kernel(total, gram, inner, lag, both, lag_out, inner_out, coef, factor_t):
    n = gram.shape[0] // 2
    inverse, t_c, cc = settle(total, gram, inner, lag, both, [], coef, factor_t)
    lag_out[:, :n] = inverse
    lag_out[:, n:] = exact(inverse.T, inverse)
    inner_out[:, :n] = exact(inverse, t_c)
    inner_out[:, n:] = cc


def factor(total, gram, inner, lag, both):
    n = gram.shape[0] // 2
    sds = jax.ShapeDtypeStruct
    return pl.pallas_call(
        functools.partial(factor_kernel, total),
        in_specs=[VMEM] * 4,
        out_specs=[VMEM] * 3,
        out_shape=[sds((n, 2 * n), F32), sds((n, 2 * n), F32), sds((3, n, n), F32)],
        scratch_shapes=[pltpu.VMEM((n, 2 * n), F32)],
        compiler_params=pltpu.CompilerParams(vmem_limit_bytes=LIMIT),
        cost_estimate=pl.CostEstimate(flops=100_000_000, bytes_accessed=10_000_000, transcendentals=0),
        name="factor",
    )(gram, inner, lag, both)


def thirds(values):
    high = values.astype(BF16)
    rest = values - high.astype(F32)
    return jnp.concatenate([high, *halves(rest)], 0)


def unpack(lines, received, target, lanes, offset):
    for s in range(received.shape[0]):
        if s * lines < target.shape[0]:
            target[s * lines : (s + 1) * lines, lanes] = received[s, offset : offset + lines]


def place_columns(extended, block, edge):
    size = extended.shape[2]
    count = extended.shape[0] - 2
    for i in range(count):
        extended[i] = block[:, i * size : (i + 1) * size]
    extended[count] = edge[:, :size].astype(BF16)
    extended[count + 1] = edge[:, size:].astype(BF16)


def block_row(ids, extended, mixed, i):
    picked = jnp.concatenate([extended[ids[i, k]] for k in range(ids.shape[1])], 1)
    pair = jnp.dot(picked, mixed[i], preferred_element_type=F32)
    size = pair.shape[1] // 2
    return pair[:, :size] + pair[:, size:]


def prepare_kernel(ids, count, slots, below, above, start, mixed, out, values, extended):
    size = below.shape[1]
    block = start[...].astype(BF16)
    place_columns(extended, block, jnp.concatenate([below[...], above[...]], 1))
    for i in range(out.shape[1] // size):
        out[:, i * size : (i + 1) * size] = block_row(ids, extended, mixed, i)
    live = live_slots(count, slots)
    columns = min(out.shape[1], 512)
    total = jnp.zeros(values.shape, F32)
    for first in range(0, out.shape[1], columns):
        picked = chosen(first, (columns, slots.shape[1]), live)
        total = total + jnp.dot(block[:, first : first + columns], picked, preferred_element_type=F32)
    values[...] = total.astype(BF16)


def prepare(ids, count, slots, below, above, start, mixed):
    vectors, width = start.shape
    size = below.shape[1]
    return pl.pallas_call(
        prepare_kernel,
        in_specs=[SMEM, SMEM] + [VMEM] * 5,
        out_specs=[VMEM] * 2,
        out_shape=[
            pltpu.HBM((vectors, width), F32),
            jax.ShapeDtypeStruct((vectors, slots.shape[1]), BF16),
        ],
        scratch_shapes=[pltpu.VMEM((width // size + 2, vectors, size), BF16)],
        compiler_params=pltpu.CompilerParams(vmem_limit_bytes=LIMIT),
        name="prepare",
    )(ids, count, slots, below, above, start, mixed)


def advance_kernel(mode, total, peers, *refs):
    it = iter(refs)
    take = lambda k: [next(it) for _ in range(k)]
    ids, rates = take(2)
    if mode == "first":
        arrived, below, above = take(3)
        held = take(2)
    else:
        received, pressed, lag, edges, wet_held = take(5)
        held = take(1)
    pick, place, mixed_in, spread_in = take(4)
    (state_out,) = take(1)
    if mode == "last":
        (gram_s,) = take(1)
    else:
        edges_out, wet_out, send = take(3)
    if mode != "first":
        both, gram_in = take(2)
    extended, terms, stack, mixed, spread, edge_in, sems = take(7)
    if mode != "last":
        gram_s, rest = take(2)
    if mode != "first":
        mix, weights = take(2)

    n = terms.shape[0] // 6
    width = terms.shape[1]
    size = edge_in.shape[1] // 2
    count = width // size
    glines = -(-2 * n // peers)
    hlines = -(-n // peers)
    loads = []
    for k, source in enumerate(held):
        target = stack.at[pl.ds(k * n, n)] if mode == "first" else stack
        loads.append(pltpu.make_async_copy(source, target, sems.at[k]))
        loads[-1].start()
    if mode != "first":
        load_mixed = pltpu.make_async_copy(mixed_in, mixed, sems.at[3])
        load_mixed.start()
    load_spread = []
    if mode != "last":
        for h in range(2):
            part = spread_in.at[pl.ds(h * spread.shape[1], spread.shape[1])]
            load_spread.append(pltpu.make_async_copy(part, spread.at[h], sems.at[4 + h]))
            load_spread[-1].start()

    if mode == "first":
        edge = jnp.concatenate([below[...], above[...]], 1)
        summed = jnp.sum(arrived[...].astype(F32), 0)
        wet = jnp.concatenate([summed[:, :n], summed[:, n:]], 0)
        edges_out[:n, :] = edge
        edges_out[n:, :] = jnp.zeros_like(edge)
        wet_out[:, :n] = wet
        wet_out[:, n:] = jnp.zeros_like(wet)
        for copy in loads:
            copy.wait()
        residual = stack[n : 2 * n, :]
        terms[4 * n :, :] = jnp.zeros((2 * n, width), BF16)
    else:
        unpack(glines, received, gram_in, slice(None), 0)
        unpack(hlines, received, edge_in.at[pl.ds(0, n)], slice(0, size), glines)
        unpack(hlines, received, edge_in.at[pl.ds(0, n)], slice(size, 2 * size), glines + hlines)
        edge_in[n:, :] = edges[...]
        blend(total, gram_in, lag, both, mix)
        pull = lag[:, :n]
        put_weights(weights, mix[...], pull)
        edge = exact(mix[...], edge_in[...])
        summed = pressed[...]
        wet = exact_rows(jnp.concatenate([summed[:, :n], summed[:, n:]], 0), pull)
        wet = wet + exact_rows(wet_held[...], mix[:, n:])
        if mode != "last":
            edges_out[:n, :] = edge
            edges_out[n:, :] = exact(pull, edges[:n, :])
            wet_out[:, :n] = wet
            wet_out[:, n:] = exact_rows(wet_held[:, :n], pull)
        for copy in loads:
            copy.wait()
        mixture = jnp.dot(weights[...], stack[...], preferred_element_type=F32)
        residual = mixture[:n] + mixture[n : 2 * n]
        terms[4 * n : 5 * n, :], terms[5 * n :, :] = halves(mixture[2 * n : 3 * n] + mixture[3 * n :])
    high, low = halves(residual)
    terms[2 * n : 3 * n, :] = high
    terms[3 * n : 4 * n, :] = low
    force = thirds(wet.T * rates[1])
    if mode != "first":
        place_columns(extended, high, edge)
        load_mixed.wait()
    for i in range(count):
        lanes = slice(i * size, (i + 1) * size)
        added = jnp.dot(force, place[:, lanes], preferred_element_type=F32)
        applied = stack[:n, lanes] if mode == "first" else block_row(ids, extended, mixed, i)
        applied = applied - (added[:n] + added[n : 2 * n] + added[2 * n :])
        terms[:n, lanes], terms[n : 2 * n, lanes] = halves(applied)
    store = pltpu.make_async_copy(terms, state_out, sems.at[2])
    store.start()

    known = 4 * n if mode == "first" else 6 * n
    products = rows(terms[: 2 * n, :], terms[:known, :])
    products = products[:n] + products[n:]
    gram_s[:n, :n] = products[:, :n] + products[:, n : 2 * n]
    gram_s[:n, n:] = products[:, 2 * n : 3 * n] + products[:, 3 * n : 4 * n]
    if mode == "first":
        gram_s[n:, :n] = jnp.zeros((n, n), F32)
    else:
        gram_s[n:, :n] = products[:, 4 * n : 5 * n] + products[:, 5 * n :]
    squares = rows(terms[2 * n : 4 * n, :], terms[2 * n : 4 * n, :])
    squares = squares[:n] + squares[n:]
    gram_s[n:, n:] = squares[:, :n] + squares[:, n:]
    if mode != "last":
        rim = jnp.dot(terms[: 2 * n, :], pick[...], preferred_element_type=F32)
        edge_in[:n, :size] = rim[:n] + rim[n:]
        wets = wet_out.shape[0] // 2
        for copy in load_spread:
            copy.wait()
        tops = rows(spread[0], terms[: 2 * n, :])
        tops = tops + pltpu.roll(tops, n, 1)
        ends = rows(spread[1], terms[: 2 * n, :])
        ends = ends + pltpu.roll(ends, n, 1)
        lane = lax.broadcasted_iota(jnp.int32, tops.shape, 1)
        send[:, :wets, :] = jnp.where(lane < n, tops, ends).astype(BF16).reshape(peers, wets, 2 * n)
        left = gram_s[...]
        offset = 0
        for _ in range(3):
            term = left.astype(BF16).astype(F32)
            left = left - term
            gram_s[...] = term
            for d in range(peers):
                if d * glines < 2 * n:
                    rest[d, offset : offset + glines] = gram_s[d * glines : (d + 1) * glines, :]
            offset += glines
        left = edge_in[:n, :size]
        for _ in range(2):
            term = left.astype(BF16).astype(F32)
            left = left - term
            edge_in[:n, :size] = term
            for d in range(peers):
                if d * hlines < n:
                    rest[d, offset : offset + hlines] = edge_in[d * hlines : (d + 1) * hlines, :size]
                else:
                    rest[d, offset : offset + hlines] = jnp.zeros((hlines, size), F32)
            offset += hlines
        if offset < rest.shape[1]:
            rest[:, offset:, :] = jnp.zeros((peers, rest.shape[1] - offset, 2 * n), F32)
        send[:, wets:, :] = rest[...].astype(BF16)
    store.wait()


def advance(mode, total, peers, ids, rates, state, fixed):
    mixed, pick, place, spread = fixed
    width, size = pick.shape
    wets = place.shape[0]
    vectors = state[3].shape[0] if mode == "first" else state[2].shape[0]
    extra = 3 * -(-2 * vectors // peers) + 2 * -(-vectors // peers)
    extra = -(-extra // 16) * 16
    sds = jax.ShapeDtypeStruct
    block = pltpu.HBM((6 * vectors, width), BF16)
    small = sds((2 * vectors, 2 * vectors), F32)
    shapes, specs = [block], [HBM]
    if mode == "last":
        shapes += [small]
        specs += [VMEM]
    else:
        shapes += [
            sds((2 * vectors, 2 * size), F32),
            sds((wets, 2 * vectors), F32),
            sds((peers, wets // 2 + extra, 2 * vectors), BF16),
        ]
        specs += [VMEM] * 3
    if mode != "first":
        shapes += [sds((vectors, 2 * vectors), F32), small]
        specs += [VMEM, VMEM]
    scratch = [
        pltpu.VMEM((width // size + 2, vectors, size), BF16),
        pltpu.VMEM((6 * vectors, width), BF16),
        pltpu.VMEM((2 * vectors, width), F32) if mode == "first" else pltpu.VMEM((6 * vectors, width), BF16),
        pltpu.VMEM(mixed.shape if mode != "first" else (16, 128), BF16),
        pltpu.VMEM((2, spread.shape[0] // 2, spread.shape[1]) if mode != "last" else (16, 128), BF16),
        pltpu.VMEM((3 * vectors, 2 * size), F32),
        pltpu.SemaphoreType.DMA((6,)),
    ]
    if mode != "last":
        scratch += [pltpu.VMEM(small.shape, F32), pltpu.VMEM((peers, extra, 2 * vectors), F32)]
    if mode != "first":
        scratch += [pltpu.VMEM((vectors, 3 * vectors), F32), pltpu.VMEM((4 * vectors, 6 * vectors), BF16)]
    held = 2 if mode == "first" else 1
    return pl.pallas_call(
        functools.partial(advance_kernel, mode, total, peers),
        in_specs=[SMEM, SMEM] + [VMEM] * (len(state) - held) + [HBM] * held + [VMEM, VMEM, HBM, HBM],
        out_specs=specs,
        out_shape=shapes,
        scratch_shapes=scratch,
        compiler_params=pltpu.CompilerParams(vmem_limit_bytes=LIMIT),
        name="advance_" + mode,
    )(ids, rates, *state, pick, place, mixed, spread)


def route_kernel(vectors, wets, received, _lag, pressed, send, rest):
    peers = received.shape[0]
    glines = -(-2 * vectors // peers)
    hlines = -(-vectors // peers)
    pressed[...] = jnp.sum(received[:, :wets, :].astype(F32), 0)
    rest[...] = received[:, wets:, :].astype(F32)
    sums = jnp.sum(rest[...], 0)
    mine = sums[:glines] + sums[glines : 2 * glines] + sums[2 * glines : 3 * glines]
    edge = 3 * glines
    nothing = jnp.zeros((hlines, 2 * vectors), F32)

    def halo(t):
        if not 0 <= t < peers:
            return nothing
        return rest[t, edge : edge + hlines] + rest[t, edge + hlines : edge + 2 * hlines]

    send[...] = jnp.zeros(send.shape, F32)
    for t in range(peers):
        send[t, :glines] = mine
        send[t, glines : glines + hlines] = halo(t - 1)
        send[t, glines + hlines : glines + 2 * hlines] = halo(t + 1)


def route(vectors, wets, received, lag):
    peers, lines, lanes = received.shape
    return pl.pallas_call(
        functools.partial(route_kernel, vectors, wets),
        in_specs=[VMEM, VMEM],
        out_specs=[VMEM] * 2,
        out_shape=[
            jax.ShapeDtypeStruct((wets, 2 * vectors), F32),
            jax.ShapeDtypeStruct((peers, 8, 2 * vectors), F32),
        ],
        scratch_shapes=[pltpu.VMEM((peers, lines - wets, lanes), F32)],
        compiler_params=pltpu.CompilerParams(vmem_limit_bytes=LIMIT),
        name="route",
    )(received, lag)


def repeat_sum_kernel(received, _lag, send):
    mine = jnp.sum(received[...], 0)
    for t in range(send.shape[0]):
        send[t] = mine


def repeat_sum(received, lag):
    return pl.pallas_call(
        repeat_sum_kernel,
        in_specs=[VMEM, VMEM],
        out_specs=VMEM,
        out_shape=jax.ShapeDtypeStruct(received.shape, F32),
        compiler_params=pltpu.CompilerParams(vmem_limit_bytes=LIMIT),
        name="repeat_sum",
    )(received, lag)


def finish_kernel(total, gram, inner, lag, state, *refs):
    *earlier, out, coefs, factor_t, mix, weights, both, stack, fresh, sem = refs
    coef = coefs.at[len(earlier)]
    n = inner.shape[0]
    load = pltpu.make_async_copy(state, stack, sem)
    load.start()
    blend(total, gram, lag, both, mix)
    for k, known in enumerate(earlier):
        coefs[k] = known[...]
    put_weights(weights, mix[...], lag[:, :n])
    load.wait()

    def next_residual():
        mixture = jnp.dot(weights[...], stack[...], preferred_element_type=F32)
        fresh[...] = mixture[:n] + mixture[n:]

    inverse, _, _ = settle(total, gram, inner, lag, both, [next_residual], coef, factor_t)
    out[...] = exact(inverse, fresh[...])


def finish(total, gram, inner, lag, state, earlier):
    vectors, width = lag.shape[0], state.shape[1]
    return pl.pallas_call(
        functools.partial(finish_kernel, total),
        in_specs=[VMEM] * 3 + [HBM] + [VMEM] * len(earlier),
        out_specs=[VMEM] * 2,
        out_shape=[
            pltpu.HBM((vectors, width), F32),
            pltpu.HBM((len(earlier) + 1, 3, vectors, vectors), F32),
        ],
        scratch_shapes=[
            pltpu.VMEM((vectors, 2 * vectors), F32),
            pltpu.VMEM((vectors, 3 * vectors), F32),
            pltpu.VMEM((2 * vectors, 6 * vectors), BF16),
            pltpu.VMEM((vectors, 2 * vectors), F32),
            pltpu.VMEM((6 * vectors, width), BF16),
            pltpu.VMEM((vectors, width), F32),
            pltpu.SemaphoreType.DMA,
        ],
        compiler_params=pltpu.CompilerParams(vmem_limit_bytes=LIMIT),
        name="finish",
    )(gram, inner, lag, state, *earlier)


def local(n_row, n_col, start_block, struct_blocks, block_ids, rim_rows, wet_slots, wet_counts, added_mass, rates):
    peers = n_row * n_col
    vectors, width = start_block.shape
    total = float(width * peers)
    wcap = wet_slots.shape[0]
    wets = added_mass.shape[0] // n_row

    def exchange(parts):
        return lax.all_to_all(parts, AXES, 0, 0, tiled=True)

    def neighbours(halo):
        up = [(i, i + 1) for i in range(peers - 1)]
        down = [(i + 1, i) for i in range(peers - 1)]
        return lax.ppermute(halo, AXES, up), lax.ppermute(halo, AXES, down)

    def summed(gram, lag):
        lines = gram.shape[0] // peers
        return exchange(repeat_sum(exchange(gram.reshape(peers, lines, -1)), lag)).reshape(gram.shape)

    blocks = by_owner(added_mass, n_col, wcap)
    mass = lax.all_to_all(blocks, "col", 0, 0, tiled=True)
    mass = mass.reshape(n_col, n_row, 2, wets // 2, wcap)
    mixed, pick, place, halo = combine(
        rates, rim_rows[None, :], wet_slots[:wets, None], start_block, struct_blocks
    )
    below, above = neighbours(halo)
    slots = wet_slots[None, :]
    base, values = prepare(block_ids, wet_counts, slots, below, above, start_block, mixed)
    base = in_hbm(base)
    part = start_pressure(values, mass, base)
    spread = spread_mass(wet_counts, slots, mass, width)
    fixed = (in_hbm(mixed), pick, place, in_hbm(spread))
    arrived = exchange(part.reshape(peers, wets // 2, 2 * vectors))
    step = functools.partial(advance, total=total, peers=peers, ids=block_ids, rates=rates, fixed=fixed)
    state, edges, wet_held, send = step("first", state=(arrived, below, above, base, in_hbm(start_block)))
    inner = jnp.zeros((vectors, 2 * vectors), F32)
    unit = jnp.eye(vectors, dtype=F32)
    lag = jnp.concatenate([unit, unit], 1)
    coefficients = []
    for number in range(1, STEPS):
        pressed, again = route(vectors, wets // 2, exchange(send), lag)
        received = exchange(again)
        known = (received, pressed, lag, edges, wet_held, in_hbm(state))
        if number < STEPS - 1:
            state, edges, wet_held, send, both, gram = step("mid", state=known)
        else:
            state, products, both, gram = step("last", state=known)
        lag, inner, coef = factor(total, gram, inner, lag, both)
        coefficients.append(coef)
    final, coefs = finish(total, summed(products, lag), inner, lag, in_hbm(state), coefficients)
    return final, coefs


def solution(mesh):
    return jax.shard_map(
        functools.partial(local, mesh.shape["row"], mesh.shape["col"]),
        mesh=mesh,
        in_specs=(
            P(None, AXES),
            P(None, AXES, None, None, None),
            P(AXES, None),
            P(AXES),
            P(AXES),
            P(AXES),
            P("col", "row"),
            P(),
        ),
        out_specs=(P(None, AXES), P()),
        check_vma=False,
    )
```

```python
import functools

import jax
import jax.numpy as jnp
from jax import lax
from jax.experimental import pallas as pl
from jax.experimental.pallas import tpu as pltpu
from jax.sharding import PartitionSpec as P

STEPS = 6
AXES = ("row", "col")
VMEM = pl.BlockSpec(memory_space=pltpu.VMEM)
SMEM = pl.BlockSpec(memory_space=pltpu.SMEM)
HBM = pl.BlockSpec(memory_space=pltpu.HBM)
ANY = pl.BlockSpec(memory_space=pl.ANY)
F32 = jnp.float32
BF16 = jnp.bfloat16
LIMIT = 40 * 1024 * 1024


def exact(left, right):
    return lax.dot_general(
        left, right, (((1,), (0,)), ((), ())), precision=lax.Precision.HIGHEST, preferred_element_type=F32
    )


def exact_rows(left, right):
    return lax.dot_general(
        left, right, (((1,), (1,)), ((), ())), precision=lax.Precision.HIGHEST, preferred_element_type=F32
    )


def rows(left, right):
    return lax.dot_general(left, right, (((1,), (1,)), ((), ())), preferred_element_type=F32)


def in_hbm(values):
    return pltpu.with_memory_space_constraint(values, pltpu.HBM)


def halves(values):
    high = values.astype(BF16)
    return high, (values - high.astype(F32)).astype(BF16)


def by_owner_kernel(mass, out):
    out[0] = mass[...]


def by_owner(mass, n_col, wcap):
    size = mass.shape[0]
    return pl.pallas_call(
        by_owner_kernel,
        grid=(n_col,),
        in_specs=[pl.BlockSpec((size, wcap), lambda c: (0, c))],
        out_specs=pl.BlockSpec((1, size, wcap), lambda c: (c, 0, 0)),
        out_shape=pltpu.HBM((n_col, size, wcap), BF16),
        compiler_params=pltpu.CompilerParams(vmem_limit_bytes=LIMIT),
        name="by_owner",
    )(mass)


def combine_kernel(rates, count, rim, wet, slots, start, blocks, mixed, pick, place, halo, values):
    size = blocks.shape[-1]
    for k in range(blocks.shape[2]):
        whole = (
            blocks[0, 0, k].astype(F32)
            + rates[0] * blocks[1, 0, k].astype(F32)
            - rates[1] * blocks[2, 0, k].astype(F32)
        ).T
        high = whole.astype(BF16)
        mixed[0, k * size : (k + 1) * size, :size] = high
        mixed[0, k * size : (k + 1) * size, size:] = (whole - high.astype(F32)).astype(BF16)

    @pl.when(pl.program_id(0) == 0)
    def _():
        index = lax.broadcasted_iota(jnp.int32, pick.shape, 0)
        pick[...] = jnp.where(index == rim[...], 1.0, 0.0).astype(BF16)
        index = lax.broadcasted_iota(jnp.int32, place.shape, 1)
        place[...] = jnp.where(index == wet[...], 1.0, 0.0).astype(BF16)
        high, low = halves(start[...])
        halo[...] = jnp.dot(high, pick[...], preferred_element_type=F32) + jnp.dot(
            low, pick[...], preferred_element_type=F32
        )
        live = live_slots(count, slots)
        columns = min(start.shape[1], 512)
        total = jnp.zeros(values.shape, F32)
        for first in range(0, start.shape[1], columns):
            picked = chosen(first, (columns, slots.shape[1]), live)
            total = total + jnp.dot(high[:, first : first + columns], picked, preferred_element_type=F32)
        values[...] = total.astype(BF16)


def combine(rates, count, rim, wet, slots, start, blocks):
    _, block_rows, nnz, size, _ = blocks.shape
    vectors, width = start.shape
    whole = lambda shape: pl.BlockSpec(shape, lambda i: (0,) * len(shape))
    return pl.pallas_call(
        combine_kernel,
        grid=(block_rows,),
        in_specs=[
            SMEM,
            SMEM,
            whole(rim.shape),
            whole(wet.shape),
            whole(slots.shape),
            whole(start.shape),
            pl.BlockSpec((3, 1, nnz, size, size), lambda i: (0, i, 0, 0, 0)),
        ],
        out_specs=[
            pl.BlockSpec((1, nnz * size, 2 * size), lambda i: (i, 0, 0)),
            whole((width, rim.shape[1])),
            whole((wet.shape[0], width)),
            whole((vectors, rim.shape[1])),
            whole((vectors, slots.shape[1])),
        ],
        out_shape=[
            pltpu.HBM((block_rows, nnz * size, 2 * size), BF16),
            jax.ShapeDtypeStruct((width, rim.shape[1]), BF16),
            jax.ShapeDtypeStruct((wet.shape[0], width), BF16),
            jax.ShapeDtypeStruct((vectors, rim.shape[1]), F32),
            jax.ShapeDtypeStruct((vectors, slots.shape[1]), BF16),
        ],
        compiler_params=pltpu.CompilerParams(vmem_limit_bytes=LIMIT),
        name="combine",
    )(rates, count, rim, wet, slots, start, blocks)


def live_slots(count, slots):
    slot = lax.broadcasted_iota(jnp.int32, slots.shape, 1)
    return jnp.where(slot < count[0], slots[...], -1)


def chosen(first, shape, live):
    index = lax.broadcasted_iota(jnp.int32, shape, 0) + first
    return jnp.where(index == live, 1.0, 0.0).astype(BF16)


def start_pressure_kernel(values, mass, part):
    n_col, n_row, _, half, wcap = mass.shape
    size, vectors = n_col * half, values.shape[0]
    for r in range(n_row):
        for h in range(2):
            own = mass[:, r, h].reshape(size, wcap)
            pressed = rows(own, values[...]).astype(BF16)
            part[r * size : (r + 1) * size, h * vectors : (h + 1) * vectors] = pressed


def start_pressure(values, mass):
    n_col, n_row, _, half, _ = mass.shape
    return pl.pallas_call(
        start_pressure_kernel,
        in_specs=[VMEM, VMEM],
        out_specs=VMEM,
        out_shape=jax.ShapeDtypeStruct((n_col * n_row * half, 2 * values.shape[0]), BF16),
        compiler_params=pltpu.CompilerParams(vmem_limit_bytes=LIMIT),
        name="start_pressure",
    )(values, mass)


def spread_kernel(count, slots, mass, spread, own):
    n_col, n_row, _, half, wcap = mass.shape
    size = n_col * half

    @pl.when(pl.program_id(0) == 0)
    def _():
        for h in range(2):
            for r in range(n_row):
                first = (h * n_row + r) * size
                own[first : first + size] = mass[:, r, h].reshape(size, wcap)

    columns = spread.shape[1]
    onehot = chosen(pl.program_id(0) * columns, (columns, wcap), live_slots(count, slots))
    spread[...] = rows(own[...], onehot).astype(BF16)


def spread_mass(count, slots, mass, width):
    n_col, n_row, _, half, wcap = mass.shape
    size = n_col * n_row * half
    columns = min(width, 512)
    return pl.pallas_call(
        spread_kernel,
        grid=(width // columns,),
        in_specs=[
            SMEM,
            pl.BlockSpec(slots.shape, lambda i: (0, 0)),
            pl.BlockSpec(mass.shape, lambda i: (0,) * 5),
        ],
        out_specs=pl.BlockSpec((2 * size, columns), lambda i: (0, i)),
        out_shape=pltpu.HBM((2 * size, width), BF16),
        scratch_shapes=[pltpu.VMEM((2 * size, wcap), BF16)],
        compiler_params=pltpu.CompilerParams(vmem_limit_bytes=LIMIT),
        cost_estimate=pl.CostEstimate(
            flops=4 * size * wcap * width, bytes_accessed=4 * size * width, transcendentals=0
        ),
        name="spread",
    )(count, slots, mass)


def pivot_rows(top, s):
    lanes = top[0].shape[1]
    at = lambda i, j: jnp.broadcast_to(top[i][:, s + j : s + j + 1], (1, lanes))
    a, b, c = at(0, 0), at(0, 1), at(1, 1)
    p2, q2, p3, q3 = at(2, 0), at(2, 1), at(3, 0), at(3, 1)
    d22, d23, d33 = at(2, 2), at(2, 3), at(3, 3)
    scale = 1.0 / (a * c - b * b)
    first = ((c * top[0] - b * top[1]) * scale, (a * top[1] - b * top[0]) * scale)
    y02, y03 = (c * p2 - b * q2) * scale, (c * p3 - b * q3) * scale
    y12, y13 = (a * q2 - b * p2) * scale, (a * q3 - b * p3) * scale
    a2 = d22 - p2 * y02 - q2 * y12
    b2 = d23 - p2 * y03 - q2 * y13
    c2 = d33 - p3 * y03 - q3 * y13
    scale2 = 1.0 / (a2 * c2 - b2 * b2)
    third = top[2] - p2 * first[0] - q2 * first[1]
    fourth = top[3] - p3 * first[0] - q3 * first[1]
    v2 = (c2 * third - b2 * fourth) * scale2
    v3 = (a2 * fourth - b2 * third) * scale2
    v0 = first[0] - y02 * v2 - y03 * v3
    v1 = first[1] - y12 * v2 - y13 * v3
    return first, (v0, v1, v2, v3)


def eliminate_four(work, s, j, keep):
    sub = lax.broadcasted_iota(jnp.int32, (8, 1), 0)
    first, full = pivot_rows([work[0][s + k : s + k + 1, :] for k in range(4)], j)
    out = []
    for i, group in enumerate(work):
        columns = [group[:, j + k : j + k + 1] for k in range(4)]
        half = columns[0] * full[0] + columns[1] * full[1]
        update = half + (columns[2] * full[2] + columns[3] * full[3])
        if i == 0:
            pair = columns[0] * first[0] + columns[1] * first[1]
            update = jnp.where(sub > s + 3, update, jnp.where(sub > s + 1, pair, 0.0))
        elif keep is not None:
            update = jnp.where(keep(i), update, 0.0)
        out.append(group - update)
    return out


def eliminate(matrix, beside, coef, factor_t):
    n = matrix.shape[0]
    groups = n // 8
    row_id = lax.broadcasted_iota(jnp.int32, (n, 2 * n), 0)
    lane_id = lax.broadcasted_iota(jnp.int32, (n, 2 * n), 1)
    factor_t[...] = jnp.where(row_id + n == lane_id, 1.0, 0.0)
    factor_t[:, :n] = matrix
    if beside:
        work = [factor_t[g * 8 : (g + 1) * 8, :] for g in range(groups)]
        done = 0
        for j in range(0, n, 4):
            g, s = divmod(j, 8)
            work[g:] = eliminate_four(work[g:], s, j, None)
            goal = len(beside) * (j + 4) // n
            while done < goal:
                beside[done]()
                done += 1
        reduced = jnp.concatenate(work, 0)
    else:

        def group(step, _):
            work = [factor_t[g * 8 : (g + 1) * 8, :] for g in range(groups)]
            for s in range(0, 8, 4):
                work = eliminate_four(work, s, s, lambda i: step + i < groups)
            for i in range(groups):
                target = (i - 1) % groups
                factor_t[target * 8 : (target + 1) * 8, :] = pltpu.roll(work[i], 2 * n - 8, 1)
            return 0

        lax.fori_loop(0, groups, group, 0)
        reduced = pltpu.roll(factor_t[...], n, 1)
    above = pltpu.roll(reduced, 1, 0)
    odd = lax.broadcasted_iota(jnp.int32, (n, 1), 0) % 2 == 1
    pick = lambda values, where: jnp.sum(jnp.where(where, values, 0.0), 1, keepdims=True)
    under = pick(above, lane_id == row_id) / jnp.where(odd, pick(above, lane_id + 1 == row_id), 1.0)
    reduced = reduced - jnp.where(odd, under, 0.0) * above
    diagonal = pick(reduced, lane_id == row_id)
    scale = lax.rsqrt(diagonal)
    scale = scale * (1.5 - 0.5 * diagonal * scale * scale)
    reduced = reduced * scale
    factor_t[...] = reduced
    upper = jnp.where(row_id <= lane_id, reduced, 0.0)
    coef[2] = upper.T[:n, :]
    return factor_t[:, n:]


def congruent(factor, matrix):
    return exact(factor, exact_rows(matrix, factor))


def settle(total, gram, inner, lag, both, beside, coef, factor_t):
    n = gram.shape[0] // 2
    scale = 1.0 / total
    pull = lag[:, :n]
    aa = congruent(pull, gram[:n, :n] * scale)
    cc = congruent(pull, gram[n:, n:] * scale)
    self_ = both[:, :n]
    prev = both[:, n:]
    cp = inner[:, :n]
    pp = inner[:, n:]
    coef[0] = self_
    coef[1] = prev
    t_c = self_ - exact(self_, cc) - exact_rows(prev, cp)
    t_p = prev - exact(self_, cp) - exact(prev, pp)
    t_a = aa - exact_rows(self_, self_) - exact_rows(prev, prev)
    matrix = t_a - exact_rows(t_c, self_) - exact_rows(t_p, prev)
    inverse = eliminate(0.5 * (matrix + matrix.T), beside, coef, factor_t)
    return inverse, t_c, cc


def put_weights(weights, mix, pull):
    n = mix.shape[0]
    high, low = halves(mix)
    pull_high, pull_low = halves(pull)
    for k in range(3):
        cut = slice(k * n, (k + 1) * n)
        weights[:n, 2 * k * n : (2 * k + 1) * n] = high[:, cut]
        weights[:n, (2 * k + 1) * n : (2 * k + 2) * n] = high[:, cut]
        weights[n : 2 * n, 2 * k * n : (2 * k + 1) * n] = low[:, cut]
        weights[n : 2 * n, (2 * k + 1) * n : (2 * k + 2) * n] = jnp.zeros((n, n), BF16)
    if weights.shape[0] > 2 * n:
        weights[2 * n :, :] = jnp.zeros((2 * n, 6 * n), BF16)
        weights[2 * n : 3 * n, 2 * n : 3 * n] = pull_high
        weights[2 * n : 3 * n, 3 * n : 4 * n] = pull_high
        weights[3 * n :, 2 * n : 3 * n] = pull_low


def blend(total, gram, lag, both, mix):
    n = gram.shape[0] // 2
    scale = 1.0 / total
    pull, square = lag[:, :n], lag[:, n:]
    crossed = gram[:n, n:] * scale
    prev = exact(pull, gram[n:, :n] * scale)
    mix[:, :n] = pull
    mix[:, n : 2 * n] = -exact(pull, exact(crossed, square))
    mix[:, 2 * n :] = -prev
    both[:, :n] = congruent(pull, crossed)
    both[:, n:] = prev


def factor_kernel(total, gram, inner, lag, both, lag_out, inner_out, coef, factor_t):
    n = gram.shape[0] // 2
    inverse, t_c, cc = settle(total, gram, inner, lag, both, [], coef, factor_t)
    lag_out[:, :n] = inverse
    lag_out[:, n:] = exact(inverse.T, inverse)
    inner_out[:, :n] = exact(inverse, t_c)
    inner_out[:, n:] = cc


def factor(total, gram, inner, lag, both):
    n = gram.shape[0] // 2
    sds = jax.ShapeDtypeStruct
    return pl.pallas_call(
        functools.partial(factor_kernel, total),
        in_specs=[VMEM] * 4,
        out_specs=[VMEM] * 3,
        out_shape=[sds((n, 2 * n), F32), sds((n, 2 * n), F32), sds((3, n, n), F32)],
        scratch_shapes=[pltpu.VMEM((n, 2 * n), F32)],
        compiler_params=pltpu.CompilerParams(vmem_limit_bytes=LIMIT),
        cost_estimate=pl.CostEstimate(flops=100_000_000, bytes_accessed=10_000_000, transcendentals=0),
        name="factor",
    )(gram, inner, lag, both)


def thirds(values):
    high = values.astype(BF16)
    rest = values - high.astype(F32)
    return jnp.concatenate([high, *halves(rest)], 0)


def unpack(lines, received, target, lanes, offset):
    for s in range(received.shape[0]):
        if s * lines < target.shape[0]:
            target[s * lines : (s + 1) * lines, lanes] = received[s, offset : offset + lines]


def place_columns(extended, block, edge):
    size = extended.shape[2]
    count = extended.shape[0] - 2
    for i in range(count):
        extended[i] = block[:, i * size : (i + 1) * size]
    extended[count] = edge[:, :size].astype(BF16)
    extended[count + 1] = edge[:, size:].astype(BF16)


def block_row(ids, extended, mixed, i):
    picked = jnp.concatenate([extended[ids[i, k]] for k in range(ids.shape[1])], 1)
    pair = jnp.dot(picked, mixed[i], preferred_element_type=F32)
    size = pair.shape[1] // 2
    return pair[:, :size] + pair[:, size:]


def advance_kernel(mode, total, peers, *refs):
    it = iter(refs)
    take = lambda k: [next(it) for _ in range(k)]
    ids, rates = take(2)
    if mode == "first":
        arrived, below, above = take(3)
    else:
        received, pressed, lag, edges, wet_held = take(5)
    (held,) = take(1)
    pick, place, mixed_in, spread_in = take(4)
    (state_out,) = take(1)
    if mode == "last":
        (gram_s,) = take(1)
    else:
        edges_out, wet_out, send = take(3)
    if mode != "first":
        both, gram_in = take(2)
    extended, terms, stack, mixed, spread, edge_in, sems = take(7)
    if mode != "last":
        gram_s, rest = take(2)
    if mode != "first":
        mix, weights = take(2)

    n = terms.shape[0] // 6
    width = terms.shape[1]
    size = edge_in.shape[1] // 2
    count = width // size
    glines = -(-2 * n // peers)
    hlines = -(-n // peers)
    load = pltpu.make_async_copy(held, stack, sems.at[0])
    load.start()
    load_mixed = pltpu.make_async_copy(mixed_in, mixed, sems.at[1])
    load_mixed.start()
    load_spread = []
    if mode != "last":
        for h in range(2):
            part = spread_in.at[pl.ds(h * spread.shape[1], spread.shape[1])]
            load_spread.append(pltpu.make_async_copy(part, spread.at[h], sems.at[3 + h]))
            load_spread[-1].start()

    if mode == "first":
        edge = jnp.concatenate([below[...], above[...]], 1)
        summed = jnp.sum(arrived[...].astype(F32), 0)
        wet = jnp.concatenate([summed[:, :n], summed[:, n:]], 0)
        edges_out[:n, :] = edge
        edges_out[n:, :] = jnp.zeros_like(edge)
        wet_out[:, :n] = wet
        wet_out[:, n:] = jnp.zeros_like(wet)
        load.wait()
        residual = stack[...]
        terms[4 * n :, :] = jnp.zeros((2 * n, width), BF16)
    else:
        unpack(glines, received, gram_in, slice(None), 0)
        unpack(hlines, received, edge_in.at[pl.ds(0, n)], slice(0, size), glines)
        unpack(hlines, received, edge_in.at[pl.ds(0, n)], slice(size, 2 * size), glines + hlines)
        edge_in[n:, :] = edges[...]
        blend(total, gram_in, lag, both, mix)
        pull = lag[:, :n]
        put_weights(weights, mix[...], pull)
        edge = exact(mix[...], edge_in[...])
        summed = pressed[...]
        wet = exact_rows(jnp.concatenate([summed[:, :n], summed[:, n:]], 0), pull)
        wet = wet + exact_rows(wet_held[...], mix[:, n:])
        if mode != "last":
            edges_out[:n, :] = edge
            edges_out[n:, :] = exact(pull, edges[:n, :])
            wet_out[:, :n] = wet
            wet_out[:, n:] = exact_rows(wet_held[:, :n], pull)
        load.wait()
        mixture = jnp.dot(weights[...], stack[...], preferred_element_type=F32)
        residual = mixture[:n] + mixture[n : 2 * n]
        terms[4 * n : 5 * n, :], terms[5 * n :, :] = halves(mixture[2 * n : 3 * n] + mixture[3 * n :])
    high, low = halves(residual)
    terms[2 * n : 3 * n, :] = high
    terms[3 * n : 4 * n, :] = low
    force = thirds(wet.T * rates[1])
    place_columns(extended, high, edge)
    load_mixed.wait()
    for i in range(count):
        lanes = slice(i * size, (i + 1) * size)
        added = jnp.dot(force, place[:, lanes], preferred_element_type=F32)
        applied = block_row(ids, extended, mixed, i) - (added[:n] + added[n : 2 * n] + added[2 * n :])
        terms[:n, lanes], terms[n : 2 * n, lanes] = halves(applied)
    store = pltpu.make_async_copy(terms, state_out, sems.at[2])
    store.start()

    known = 4 * n if mode == "first" else 6 * n
    products = rows(terms[: 2 * n, :], terms[:known, :])
    products = products[:n] + products[n:]
    gram_s[:n, :n] = products[:, :n] + products[:, n : 2 * n]
    gram_s[:n, n:] = products[:, 2 * n : 3 * n] + products[:, 3 * n : 4 * n]
    if mode == "first":
        gram_s[n:, :n] = jnp.zeros((n, n), F32)
    else:
        gram_s[n:, :n] = products[:, 4 * n : 5 * n] + products[:, 5 * n :]
    squares = rows(terms[2 * n : 4 * n, :], terms[2 * n : 4 * n, :])
    squares = squares[:n] + squares[n:]
    gram_s[n:, n:] = squares[:, :n] + squares[:, n:]
    if mode != "last":
        rim = jnp.dot(terms[: 2 * n, :], pick[...], preferred_element_type=F32)
        edge_in[:n, :size] = rim[:n] + rim[n:]
        wets = wet_out.shape[0] // 2
        for copy in load_spread:
            copy.wait()
        tops = rows(spread[0], terms[: 2 * n, :])
        tops = tops + pltpu.roll(tops, n, 1)
        ends = rows(spread[1], terms[: 2 * n, :])
        ends = ends + pltpu.roll(ends, n, 1)
        lane = lax.broadcasted_iota(jnp.int32, tops.shape, 1)
        send[:, :wets, :] = jnp.where(lane < n, tops, ends).astype(BF16).reshape(peers, wets, 2 * n)
        left = gram_s[...]
        offset = 0
        for _ in range(3):
            term = left.astype(BF16).astype(F32)
            left = left - term
            gram_s[...] = term
            for d in range(peers):
                if d * glines < 2 * n:
                    rest[d, offset : offset + glines] = gram_s[d * glines : (d + 1) * glines, :]
            offset += glines
        left = edge_in[:n, :size]
        for _ in range(2):
            term = left.astype(BF16).astype(F32)
            left = left - term
            edge_in[:n, :size] = term
            for d in range(peers):
                if d * hlines < n:
                    rest[d, offset : offset + hlines] = edge_in[d * hlines : (d + 1) * hlines, :size]
                else:
                    rest[d, offset : offset + hlines] = jnp.zeros((hlines, size), F32)
            offset += hlines
        if offset < rest.shape[1]:
            rest[:, offset:, :] = jnp.zeros((peers, rest.shape[1] - offset, 2 * n), F32)
        send[:, wets:, :] = rest[...].astype(BF16)
    store.wait()


def advance(mode, total, peers, ids, rates, state, fixed):
    mixed, pick, place, spread = fixed
    width, size = pick.shape
    wets = place.shape[0]
    vectors = state[3].shape[0] if mode == "first" else state[2].shape[0]
    extra = 3 * -(-2 * vectors // peers) + 2 * -(-vectors // peers)
    extra = -(-extra // 16) * 16
    sds = jax.ShapeDtypeStruct
    block = pltpu.HBM((6 * vectors, width), BF16)
    small = sds((2 * vectors, 2 * vectors), F32)
    shapes, specs = [block], [HBM]
    if mode == "last":
        shapes += [small]
        specs += [VMEM]
    else:
        shapes += [
            sds((2 * vectors, 2 * size), F32),
            sds((wets, 2 * vectors), F32),
            sds((peers, wets // 2 + extra, 2 * vectors), BF16),
        ]
        specs += [VMEM] * 3
    if mode != "first":
        shapes += [sds((vectors, 2 * vectors), F32), small]
        specs += [VMEM, VMEM]
    scratch = [
        pltpu.VMEM((width // size + 2, vectors, size), BF16),
        pltpu.VMEM((6 * vectors, width), BF16),
        pltpu.VMEM((vectors, width), F32) if mode == "first" else pltpu.VMEM((6 * vectors, width), BF16),
        pltpu.VMEM(mixed.shape, BF16),
        pltpu.VMEM((2, spread.shape[0] // 2, spread.shape[1]) if mode != "last" else (16, 128), BF16),
        pltpu.VMEM((3 * vectors, 2 * size), F32),
        pltpu.SemaphoreType.DMA((5,)),
    ]
    if mode != "last":
        scratch += [pltpu.VMEM(small.shape, F32), pltpu.VMEM((peers, extra, 2 * vectors), F32)]
    if mode != "first":
        scratch += [pltpu.VMEM((vectors, 3 * vectors), F32), pltpu.VMEM((4 * vectors, 6 * vectors), BF16)]
    return pl.pallas_call(
        functools.partial(advance_kernel, mode, total, peers),
        in_specs=[SMEM, SMEM] + [VMEM] * (len(state) - 1) + [HBM, VMEM, VMEM, HBM, HBM],
        out_specs=specs,
        out_shape=shapes,
        scratch_shapes=scratch,
        compiler_params=pltpu.CompilerParams(vmem_limit_bytes=LIMIT),
        name="advance_" + mode,
    )(ids, rates, *state, pick, place, mixed, spread)


def route_kernel(vectors, wets, received, _lag, pressed, send, rest):
    peers = received.shape[0]
    glines = -(-2 * vectors // peers)
    hlines = -(-vectors // peers)
    pressed[...] = jnp.sum(received[:, :wets, :].astype(F32), 0)
    rest[...] = received[:, wets:, :].astype(F32)
    sums = jnp.sum(rest[...], 0)
    mine = sums[:glines] + sums[glines : 2 * glines] + sums[2 * glines : 3 * glines]
    edge = 3 * glines
    nothing = jnp.zeros((hlines, 2 * vectors), F32)

    def halo(t):
        if not 0 <= t < peers:
            return nothing
        return rest[t, edge : edge + hlines] + rest[t, edge + hlines : edge + 2 * hlines]

    send[...] = jnp.zeros(send.shape, F32)
    for t in range(peers):
        send[t, :glines] = mine
        send[t, glines : glines + hlines] = halo(t - 1)
        send[t, glines + hlines : glines + 2 * hlines] = halo(t + 1)


def route(vectors, wets, received, lag):
    peers, lines, lanes = received.shape
    return pl.pallas_call(
        functools.partial(route_kernel, vectors, wets),
        in_specs=[VMEM, VMEM],
        out_specs=[VMEM] * 2,
        out_shape=[
            jax.ShapeDtypeStruct((wets, 2 * vectors), F32),
            jax.ShapeDtypeStruct((peers, 8, 2 * vectors), F32),
        ],
        scratch_shapes=[pltpu.VMEM((peers, lines - wets, lanes), F32)],
        compiler_params=pltpu.CompilerParams(vmem_limit_bytes=LIMIT),
        name="route",
    )(received, lag)


def repeat_sum_kernel(received, _lag, send):
    mine = jnp.sum(received[...], 0)
    for t in range(send.shape[0]):
        send[t] = mine


def repeat_sum(received, lag):
    return pl.pallas_call(
        repeat_sum_kernel,
        in_specs=[VMEM, VMEM],
        out_specs=VMEM,
        out_shape=jax.ShapeDtypeStruct(received.shape, F32),
        compiler_params=pltpu.CompilerParams(vmem_limit_bytes=LIMIT),
        name="repeat_sum",
    )(received, lag)


def finish_kernel(total, gram, inner, lag, state, *refs):
    *earlier, out, coefs, factor_t, mix, weights, both, stack, fresh, sem = refs
    coef = coefs.at[len(earlier)]
    n = inner.shape[0]
    load = pltpu.make_async_copy(state, stack, sem)
    load.start()
    blend(total, gram, lag, both, mix)
    for k, known in enumerate(earlier):
        coefs[k] = known[...]
    put_weights(weights, mix[...], lag[:, :n])
    load.wait()

    def next_residual():
        mixture = jnp.dot(weights[...], stack[...], preferred_element_type=F32)
        fresh[...] = mixture[:n] + mixture[n:]

    inverse, _, _ = settle(total, gram, inner, lag, both, [next_residual], coef, factor_t)
    out[...] = exact(inverse, fresh[...])


def finish(total, gram, inner, lag, state, earlier):
    vectors, width = lag.shape[0], state.shape[1]
    return pl.pallas_call(
        functools.partial(finish_kernel, total),
        in_specs=[VMEM] * 3 + [HBM] + [VMEM] * len(earlier),
        out_specs=[VMEM] * 2,
        out_shape=[
            pltpu.HBM((vectors, width), F32),
            pltpu.HBM((len(earlier) + 1, 3, vectors, vectors), F32),
        ],
        scratch_shapes=[
            pltpu.VMEM((vectors, 2 * vectors), F32),
            pltpu.VMEM((vectors, 3 * vectors), F32),
            pltpu.VMEM((2 * vectors, 6 * vectors), BF16),
            pltpu.VMEM((vectors, 2 * vectors), F32),
            pltpu.VMEM((6 * vectors, width), BF16),
            pltpu.VMEM((vectors, width), F32),
            pltpu.SemaphoreType.DMA,
        ],
        compiler_params=pltpu.CompilerParams(vmem_limit_bytes=LIMIT),
        name="finish",
    )(gram, inner, lag, state, *earlier)


def local(n_row, n_col, start_block, struct_blocks, block_ids, rim_rows, wet_slots, wet_counts, added_mass, rates):
    peers = n_row * n_col
    vectors, width = start_block.shape
    total = float(width * peers)
    wcap = wet_slots.shape[0]
    wets = added_mass.shape[0] // n_row

    def exchange(parts):
        return lax.all_to_all(parts, AXES, 0, 0, tiled=True)

    def neighbours(halo):
        up = [(i, i + 1) for i in range(peers - 1)]
        down = [(i + 1, i) for i in range(peers - 1)]
        return lax.ppermute(halo, AXES, up), lax.ppermute(halo, AXES, down)

    def summed(gram, lag):
        lines = gram.shape[0] // peers
        return exchange(repeat_sum(exchange(gram.reshape(peers, lines, -1)), lag)).reshape(gram.shape)

    blocks = by_owner(in_hbm(added_mass), n_col, wcap)
    mass = lax.all_to_all(blocks, "col", 0, 0, tiled=True)
    mass = mass.reshape(n_col, n_row, 2, wets // 2, wcap)
    slots = wet_slots[None, :]
    mixed, pick, place, halo, values = combine(
        rates, wet_counts, rim_rows[None, :], wet_slots[:wets, None], slots, start_block, struct_blocks
    )
    below, above = neighbours(halo)
    part = start_pressure(values, mass)
    spread = spread_mass(wet_counts, slots, mass, width)
    fixed = (in_hbm(mixed), pick, place, in_hbm(spread))
    arrived = exchange(part.reshape(peers, wets // 2, 2 * vectors))
    step = functools.partial(advance, total=total, peers=peers, ids=block_ids, rates=rates, fixed=fixed)
    state, edges, wet_held, send = step("first", state=(arrived, below, above, in_hbm(start_block)))
    inner = jnp.zeros((vectors, 2 * vectors), F32)
    unit = jnp.eye(vectors, dtype=F32)
    lag = jnp.concatenate([unit, unit], 1)
    coefficients = []
    for number in range(1, STEPS):
        pressed, again = route(vectors, wets // 2, exchange(send), lag)
        received = exchange(again)
        known = (received, pressed, lag, edges, wet_held, in_hbm(state))
        if number < STEPS - 1:
            state, edges, wet_held, send, both, gram = step("mid", state=known)
        else:
            state, products, both, gram = step("last", state=known)
        lag, inner, coef = factor(total, gram, inner, lag, both)
        coefficients.append(coef)
    final, coefs = finish(total, summed(products, lag), inner, lag, in_hbm(state), coefficients)
    return final, coefs


def solution(mesh):
    return jax.shard_map(
        functools.partial(local, mesh.shape["row"], mesh.shape["col"]),
        mesh=mesh,
        in_specs=(
            P(None, AXES),
            P(None, AXES, None, None, None),
            P(AXES, None),
            P(AXES),
            P(AXES),
            P(AXES),
            P("col", "row"),
            P(),
        ),
        out_specs=(P(None, AXES), P()),
        check_vma=False,
    )
```

```python
import functools

import jax
import jax.numpy as jnp
from jax import lax
from jax.experimental import pallas as pl
from jax.experimental.pallas import tpu as pltpu
from jax.sharding import PartitionSpec as P

STEPS = 6
AXES = ("row", "col")
VMEM = pl.BlockSpec(memory_space=pltpu.VMEM)
SMEM = pl.BlockSpec(memory_space=pltpu.SMEM)
HBM = pl.BlockSpec(memory_space=pltpu.HBM)
ANY = pl.BlockSpec(memory_space=pl.ANY)
F32 = jnp.float32
BF16 = jnp.bfloat16
LIMIT = 40 * 1024 * 1024


def exact(left, right):
    return lax.dot_general(
        left, right, (((1,), (0,)), ((), ())), precision=lax.Precision.HIGHEST, preferred_element_type=F32
    )


def exact_rows(left, right):
    return lax.dot_general(
        left, right, (((1,), (1,)), ((), ())), precision=lax.Precision.HIGHEST, preferred_element_type=F32
    )


def rows(left, right):
    return lax.dot_general(left, right, (((1,), (1,)), ((), ())), preferred_element_type=F32)


def in_hbm(values):
    return pltpu.with_memory_space_constraint(values, pltpu.HBM)


def halves(values):
    high = values.astype(BF16)
    return high, (values - high.astype(F32)).astype(BF16)


def by_owner_kernel(mass, out, held, sems):
    wcap = out.shape[2]
    reads, writes = [], []
    for c in range(out.shape[0]):
        reads.append(pltpu.make_async_copy(mass.at[:, pl.ds(c * wcap, wcap)], held.at[c], sems.at[0, c]))
        writes.append(pltpu.make_async_copy(held.at[c], out.at[c], sems.at[1, c]))
        reads[-1].start()
    for read, write in zip(reads, writes):
        read.wait()
        write.start()
    for write in writes:
        write.wait()


def by_owner(mass, n_col, wcap):
    shape = (n_col, mass.shape[0], wcap)
    return pl.pallas_call(
        by_owner_kernel,
        in_specs=[HBM],
        out_specs=HBM,
        out_shape=pltpu.HBM(shape, BF16),
        scratch_shapes=[pltpu.VMEM(shape, BF16), pltpu.SemaphoreType.DMA((2, n_col))],
        compiler_params=pltpu.CompilerParams(vmem_limit_bytes=LIMIT),
        name="by_owner",
    )(mass)


def combine_kernel(rates, count, rim, wet, slots, start, blocks, mixed, pick, place, halo, values):
    size = blocks.shape[-1]
    for k in range(blocks.shape[2]):
        whole = (
            blocks[0, 0, k].astype(F32)
            + rates[0] * blocks[1, 0, k].astype(F32)
            - rates[1] * blocks[2, 0, k].astype(F32)
        ).T
        high = whole.astype(BF16)
        mixed[0, k * size : (k + 1) * size, :size] = high
        mixed[0, k * size : (k + 1) * size, size:] = (whole - high.astype(F32)).astype(BF16)

    @pl.when(pl.program_id(0) == 0)
    def _():
        index = lax.broadcasted_iota(jnp.int32, pick.shape, 0)
        pick[...] = jnp.where(index == rim[...], 1.0, 0.0).astype(BF16)
        index = lax.broadcasted_iota(jnp.int32, place.shape, 1)
        place[...] = jnp.where(index == wet[...], 1.0, 0.0).astype(BF16)
        high, low = halves(start[...])
        halo[...] = jnp.dot(high, pick[...], preferred_element_type=F32) + jnp.dot(
            low, pick[...], preferred_element_type=F32
        )
        live = live_slots(count, slots)
        columns = min(start.shape[1], 512)
        total = jnp.zeros(values.shape, F32)
        for first in range(0, start.shape[1], columns):
            picked = chosen(first, (columns, slots.shape[1]), live)
            total = total + jnp.dot(high[:, first : first + columns], picked, preferred_element_type=F32)
        values[...] = total.astype(BF16)


def combine(rates, count, rim, wet, slots, start, blocks):
    _, block_rows, nnz, size, _ = blocks.shape
    vectors, width = start.shape
    whole = lambda shape: pl.BlockSpec(shape, lambda i: (0,) * len(shape))
    return pl.pallas_call(
        combine_kernel,
        grid=(block_rows,),
        in_specs=[
            SMEM,
            SMEM,
            whole(rim.shape),
            whole(wet.shape),
            whole(slots.shape),
            whole(start.shape),
            pl.BlockSpec((3, 1, nnz, size, size), lambda i: (0, i, 0, 0, 0)),
        ],
        out_specs=[
            pl.BlockSpec((1, nnz * size, 2 * size), lambda i: (i, 0, 0)),
            whole((width, rim.shape[1])),
            whole((wet.shape[0], width)),
            whole((vectors, rim.shape[1])),
            whole((vectors, slots.shape[1])),
        ],
        out_shape=[
            pltpu.HBM((block_rows, nnz * size, 2 * size), BF16),
            jax.ShapeDtypeStruct((width, rim.shape[1]), BF16),
            jax.ShapeDtypeStruct((wet.shape[0], width), BF16),
            jax.ShapeDtypeStruct((vectors, rim.shape[1]), F32),
            jax.ShapeDtypeStruct((vectors, slots.shape[1]), BF16),
        ],
        compiler_params=pltpu.CompilerParams(vmem_limit_bytes=LIMIT),
        name="combine",
    )(rates, count, rim, wet, slots, start, blocks)


def live_slots(count, slots):
    slot = lax.broadcasted_iota(jnp.int32, slots.shape, 1)
    return jnp.where(slot < count[0], slots[...], -1)


def chosen(first, shape, live):
    index = lax.broadcasted_iota(jnp.int32, shape, 0) + first
    return jnp.where(index == live, 1.0, 0.0).astype(BF16)


def start_pressure_kernel(values, mass, part):
    n_col, n_row, _, half, wcap = mass.shape
    size, vectors = n_col * half, values.shape[0]
    for r in range(n_row):
        for h in range(2):
            own = mass[:, r, h].reshape(size, wcap)
            pressed = rows(own, values[...]).astype(BF16)
            part[r * size : (r + 1) * size, h * vectors : (h + 1) * vectors] = pressed


def start_pressure(values, mass):
    n_col, n_row, _, half, _ = mass.shape
    return pl.pallas_call(
        start_pressure_kernel,
        in_specs=[VMEM, VMEM],
        out_specs=VMEM,
        out_shape=jax.ShapeDtypeStruct((n_col * n_row * half, 2 * values.shape[0]), BF16),
        compiler_params=pltpu.CompilerParams(vmem_limit_bytes=LIMIT),
        name="start_pressure",
    )(values, mass)


def spread_kernel(count, slots, mass, spread, own):
    n_col, n_row, _, half, wcap = mass.shape
    size = n_col * half

    @pl.when(pl.program_id(0) == 0)
    def _():
        for h in range(2):
            for r in range(n_row):
                first = (h * n_row + r) * size
                own[first : first + size] = mass[:, r, h].reshape(size, wcap)

    columns = spread.shape[1]
    onehot = chosen(pl.program_id(0) * columns, (columns, wcap), live_slots(count, slots))
    spread[...] = rows(own[...], onehot).astype(BF16)


def spread_mass(count, slots, mass, width):
    n_col, n_row, _, half, wcap = mass.shape
    size = n_col * n_row * half
    columns = min(width, 512)
    return pl.pallas_call(
        spread_kernel,
        grid=(width // columns,),
        in_specs=[
            SMEM,
            pl.BlockSpec(slots.shape, lambda i: (0, 0)),
            pl.BlockSpec(mass.shape, lambda i: (0,) * 5),
        ],
        out_specs=pl.BlockSpec((2 * size, columns), lambda i: (0, i)),
        out_shape=pltpu.HBM((2 * size, width), BF16),
        scratch_shapes=[pltpu.VMEM((2 * size, wcap), BF16)],
        compiler_params=pltpu.CompilerParams(vmem_limit_bytes=LIMIT),
        cost_estimate=pl.CostEstimate(
            flops=4 * size * wcap * width, bytes_accessed=4 * size * width, transcendentals=0
        ),
        name="spread",
    )(count, slots, mass)


def pivot_rows(top, s):
    lanes = top[0].shape[1]
    at = lambda i, j: jnp.broadcast_to(top[i][:, s + j : s + j + 1], (1, lanes))
    a, b, c = at(0, 0), at(0, 1), at(1, 1)
    p2, q2, p3, q3 = at(2, 0), at(2, 1), at(3, 0), at(3, 1)
    d22, d23, d33 = at(2, 2), at(2, 3), at(3, 3)
    scale = 1.0 / (a * c - b * b)
    first = ((c * top[0] - b * top[1]) * scale, (a * top[1] - b * top[0]) * scale)
    y02, y03 = (c * p2 - b * q2) * scale, (c * p3 - b * q3) * scale
    y12, y13 = (a * q2 - b * p2) * scale, (a * q3 - b * p3) * scale
    a2 = d22 - p2 * y02 - q2 * y12
    b2 = d23 - p2 * y03 - q2 * y13
    c2 = d33 - p3 * y03 - q3 * y13
    scale2 = 1.0 / (a2 * c2 - b2 * b2)
    third = top[2] - p2 * first[0] - q2 * first[1]
    fourth = top[3] - p3 * first[0] - q3 * first[1]
    v2 = (c2 * third - b2 * fourth) * scale2
    v3 = (a2 * fourth - b2 * third) * scale2
    v0 = first[0] - y02 * v2 - y03 * v3
    v1 = first[1] - y12 * v2 - y13 * v3
    return first, (v0, v1, v2, v3)


def eliminate_four(work, s, j, keep):
    sub = lax.broadcasted_iota(jnp.int32, (8, 1), 0)
    first, full = pivot_rows([work[0][s + k : s + k + 1, :] for k in range(4)], j)
    out = []
    for i, group in enumerate(work):
        columns = [group[:, j + k : j + k + 1] for k in range(4)]
        half = columns[0] * full[0] + columns[1] * full[1]
        update = half + (columns[2] * full[2] + columns[3] * full[3])
        if i == 0:
            pair = columns[0] * first[0] + columns[1] * first[1]
            update = jnp.where(sub > s + 3, update, jnp.where(sub > s + 1, pair, 0.0))
        elif keep is not None:
            update = jnp.where(keep(i), update, 0.0)
        out.append(group - update)
    return out


def eliminate(matrix, beside, coef, factor_t):
    n = matrix.shape[0]
    groups = n // 8
    row_id = lax.broadcasted_iota(jnp.int32, (n, 2 * n), 0)
    lane_id = lax.broadcasted_iota(jnp.int32, (n, 2 * n), 1)
    factor_t[...] = jnp.where(row_id + n == lane_id, 1.0, 0.0)
    factor_t[:, :n] = matrix
    if beside:
        work = [factor_t[g * 8 : (g + 1) * 8, :] for g in range(groups)]
        done = 0
        for j in range(0, n, 4):
            g, s = divmod(j, 8)
            work[g:] = eliminate_four(work[g:], s, j, None)
            goal = len(beside) * (j + 4) // n
            while done < goal:
                beside[done]()
                done += 1
        reduced = jnp.concatenate(work, 0)
    else:

        def group(step, _):
            work = [factor_t[g * 8 : (g + 1) * 8, :] for g in range(groups)]
            for s in range(0, 8, 4):
                work = eliminate_four(work, s, s, lambda i: step + i < groups)
            for i in range(groups):
                target = (i - 1) % groups
                factor_t[target * 8 : (target + 1) * 8, :] = pltpu.roll(work[i], 2 * n - 8, 1)
            return 0

        lax.fori_loop(0, groups, group, 0)
        reduced = pltpu.roll(factor_t[...], n, 1)
    above = pltpu.roll(reduced, 1, 0)
    odd = lax.broadcasted_iota(jnp.int32, (n, 1), 0) % 2 == 1
    pick = lambda values, where: jnp.sum(jnp.where(where, values, 0.0), 1, keepdims=True)
    under = pick(above, lane_id == row_id) / jnp.where(odd, pick(above, lane_id + 1 == row_id), 1.0)
    reduced = reduced - jnp.where(odd, under, 0.0) * above
    diagonal = pick(reduced, lane_id == row_id)
    scale = lax.rsqrt(diagonal)
    scale = scale * (1.5 - 0.5 * diagonal * scale * scale)
    reduced = reduced * scale
    factor_t[...] = reduced
    upper = jnp.where(row_id <= lane_id, reduced, 0.0)
    coef[2] = upper.T[:n, :]
    return factor_t[:, n:]


def congruent(factor, matrix):
    return exact(factor, exact_rows(matrix, factor))


def settle(total, gram, inner, lag, both, beside, coef, factor_t):
    n = gram.shape[0] // 2
    scale = 1.0 / total
    pull = lag[:, :n]
    aa = congruent(pull, gram[:n, :n] * scale)
    cc = congruent(pull, gram[n:, n:] * scale)
    self_ = both[:, :n]
    prev = both[:, n:]
    cp = inner[:, :n]
    pp = inner[:, n:]
    coef[0] = self_
    coef[1] = prev
    t_c = self_ - exact(self_, cc) - exact_rows(prev, cp)
    t_p = prev - exact(self_, cp) - exact(prev, pp)
    t_a = aa - exact_rows(self_, self_) - exact_rows(prev, prev)
    matrix = t_a - exact_rows(t_c, self_) - exact_rows(t_p, prev)
    inverse = eliminate(0.5 * (matrix + matrix.T), beside, coef, factor_t)
    return inverse, t_c, cc


def put_weights(weights, mix, pull):
    n = mix.shape[0]
    high, low = halves(mix)
    pull_high, pull_low = halves(pull)
    for k in range(3):
        cut = slice(k * n, (k + 1) * n)
        weights[:n, 2 * k * n : (2 * k + 1) * n] = high[:, cut]
        weights[:n, (2 * k + 1) * n : (2 * k + 2) * n] = high[:, cut]
        weights[n : 2 * n, 2 * k * n : (2 * k + 1) * n] = low[:, cut]
        weights[n : 2 * n, (2 * k + 1) * n : (2 * k + 2) * n] = jnp.zeros((n, n), BF16)
    if weights.shape[0] > 2 * n:
        weights[2 * n :, :] = jnp.zeros((2 * n, 6 * n), BF16)
        weights[2 * n : 3 * n, 2 * n : 3 * n] = pull_high
        weights[2 * n : 3 * n, 3 * n : 4 * n] = pull_high
        weights[3 * n :, 2 * n : 3 * n] = pull_low


def blend(total, gram, lag, both, mix):
    n = gram.shape[0] // 2
    scale = 1.0 / total
    pull, square = lag[:, :n], lag[:, n:]
    crossed = gram[:n, n:] * scale
    prev = exact(pull, gram[n:, :n] * scale)
    mix[:, :n] = pull
    mix[:, n : 2 * n] = -exact(pull, exact(crossed, square))
    mix[:, 2 * n :] = -prev
    both[:, :n] = congruent(pull, crossed)
    both[:, n:] = prev


def factor_kernel(total, gram, inner, lag, both, lag_out, inner_out, coef, factor_t):
    n = gram.shape[0] // 2
    inverse, t_c, cc = settle(total, gram, inner, lag, both, [], coef, factor_t)
    lag_out[:, :n] = inverse
    lag_out[:, n:] = exact(inverse.T, inverse)
    inner_out[:, :n] = exact(inverse, t_c)
    inner_out[:, n:] = cc


def factor(total, gram, inner, lag, both):
    n = gram.shape[0] // 2
    sds = jax.ShapeDtypeStruct
    return pl.pallas_call(
        functools.partial(factor_kernel, total),
        in_specs=[VMEM] * 4,
        out_specs=[VMEM] * 3,
        out_shape=[sds((n, 2 * n), F32), sds((n, 2 * n), F32), sds((3, n, n), F32)],
        scratch_shapes=[pltpu.VMEM((n, 2 * n), F32)],
        compiler_params=pltpu.CompilerParams(vmem_limit_bytes=LIMIT),
        cost_estimate=pl.CostEstimate(flops=100_000_000, bytes_accessed=10_000_000, transcendentals=0),
        name="factor",
    )(gram, inner, lag, both)


def thirds(values):
    high = values.astype(BF16)
    rest = values - high.astype(F32)
    return jnp.concatenate([high, *halves(rest)], 0)


def unpack(lines, received, target, lanes, offset):
    for s in range(received.shape[0]):
        if s * lines < target.shape[0]:
            target[s * lines : (s + 1) * lines, lanes] = received[s, offset : offset + lines]


def place_columns(extended, block, edge):
    size = extended.shape[2]
    count = extended.shape[0] - 2
    for i in range(count):
        extended[i] = block[:, i * size : (i + 1) * size]
    extended[count] = edge[:, :size].astype(BF16)
    extended[count + 1] = edge[:, size:].astype(BF16)


def block_row(ids, extended, mixed, i):
    picked = jnp.concatenate([extended[ids[i, k]] for k in range(ids.shape[1])], 1)
    pair = jnp.dot(picked, mixed[i], preferred_element_type=F32)
    size = pair.shape[1] // 2
    return pair[:, :size] + pair[:, size:]


def advance_kernel(mode, total, peers, *refs):
    it = iter(refs)
    take = lambda k: [next(it) for _ in range(k)]
    ids, rates = take(2)
    if mode == "first":
        arrived, below, above = take(3)
    else:
        received, pressed, lag, edges, wet_held = take(5)
    (held,) = take(1)
    pick, place, mixed_in, spread_in = take(4)
    (state_out,) = take(1)
    if mode == "last":
        (gram_s,) = take(1)
    else:
        edges_out, wet_out, send = take(3)
    if mode != "first":
        both, gram_in = take(2)
    extended, terms, stack, mixed, spread, edge_in, sems = take(7)
    if mode != "last":
        gram_s, rest = take(2)
    if mode != "first":
        mix, weights = take(2)

    n = terms.shape[0] // 6
    width = terms.shape[1]
    size = edge_in.shape[1] // 2
    count = width // size
    glines = -(-2 * n // peers)
    hlines = -(-n // peers)
    load = pltpu.make_async_copy(held, stack, sems.at[0])
    load.start()
    load_mixed = pltpu.make_async_copy(mixed_in, mixed, sems.at[1])
    load_mixed.start()
    load_spread = []
    if mode != "last":
        for h in range(2):
            part = spread_in.at[pl.ds(h * spread.shape[1], spread.shape[1])]
            load_spread.append(pltpu.make_async_copy(part, spread.at[h], sems.at[3 + h]))
            load_spread[-1].start()

    if mode == "first":
        edge = jnp.concatenate([below[...], above[...]], 1)
        summed = jnp.sum(arrived[...].astype(F32), 0)
        wet = jnp.concatenate([summed[:, :n], summed[:, n:]], 0)
        edges_out[:n, :] = edge
        edges_out[n:, :] = jnp.zeros_like(edge)
        wet_out[:, :n] = wet
        wet_out[:, n:] = jnp.zeros_like(wet)
        load.wait()
        residual = stack[...]
        terms[4 * n :, :] = jnp.zeros((2 * n, width), BF16)
    else:
        unpack(glines, received, gram_in, slice(None), 0)
        unpack(hlines, received, edge_in.at[pl.ds(0, n)], slice(0, size), glines)
        unpack(hlines, received, edge_in.at[pl.ds(0, n)], slice(size, 2 * size), glines + hlines)
        edge_in[n:, :] = edges[...]
        blend(total, gram_in, lag, both, mix)
        pull = lag[:, :n]
        put_weights(weights, mix[...], pull)
        edge = exact(mix[...], edge_in[...])
        summed = pressed[...]
        wet = exact_rows(jnp.concatenate([summed[:, :n], summed[:, n:]], 0), pull)
        wet = wet + exact_rows(wet_held[...], mix[:, n:])
        if mode != "last":
            edges_out[:n, :] = edge
            edges_out[n:, :] = exact(pull, edges[:n, :])
            wet_out[:, :n] = wet
            wet_out[:, n:] = exact_rows(wet_held[:, :n], pull)
        load.wait()
        mixture = jnp.dot(weights[...], stack[...], preferred_element_type=F32)
        residual = mixture[:n] + mixture[n : 2 * n]
        terms[4 * n : 5 * n, :], terms[5 * n :, :] = halves(mixture[2 * n : 3 * n] + mixture[3 * n :])
    high, low = halves(residual)
    terms[2 * n : 3 * n, :] = high
    terms[3 * n : 4 * n, :] = low
    force = thirds(wet.T * rates[1])
    place_columns(extended, high, edge)
    load_mixed.wait()
    for i in range(count):
        lanes = slice(i * size, (i + 1) * size)
        added = jnp.dot(force, place[:, lanes], preferred_element_type=F32)
        applied = block_row(ids, extended, mixed, i) - (added[:n] + added[n : 2 * n] + added[2 * n :])
        terms[:n, lanes], terms[n : 2 * n, lanes] = halves(applied)
    store = pltpu.make_async_copy(terms, state_out, sems.at[2])
    store.start()

    known = 4 * n if mode == "first" else 6 * n
    products = rows(terms[: 2 * n, :], terms[:known, :])
    products = products[:n] + products[n:]
    gram_s[:n, :n] = products[:, :n] + products[:, n : 2 * n]
    gram_s[:n, n:] = products[:, 2 * n : 3 * n] + products[:, 3 * n : 4 * n]
    if mode == "first":
        gram_s[n:, :n] = jnp.zeros((n, n), F32)
    else:
        gram_s[n:, :n] = products[:, 4 * n : 5 * n] + products[:, 5 * n :]
    squares = rows(terms[2 * n : 4 * n, :], terms[2 * n : 4 * n, :])
    squares = squares[:n] + squares[n:]
    gram_s[n:, n:] = squares[:, :n] + squares[:, n:]
    if mode != "last":
        rim = jnp.dot(terms[: 2 * n, :], pick[...], preferred_element_type=F32)
        edge_in[:n, :size] = rim[:n] + rim[n:]
        wets = wet_out.shape[0] // 2
        for copy in load_spread:
            copy.wait()
        tops = rows(spread[0], terms[: 2 * n, :])
        tops = tops + pltpu.roll(tops, n, 1)
        ends = rows(spread[1], terms[: 2 * n, :])
        ends = ends + pltpu.roll(ends, n, 1)
        lane = lax.broadcasted_iota(jnp.int32, tops.shape, 1)
        send[:, :wets, :] = jnp.where(lane < n, tops, ends).astype(BF16).reshape(peers, wets, 2 * n)
        left = gram_s[...]
        offset = 0
        for _ in range(3):
            term = left.astype(BF16).astype(F32)
            left = left - term
            gram_s[...] = term
            for d in range(peers):
                if d * glines < 2 * n:
                    rest[d, offset : offset + glines] = gram_s[d * glines : (d + 1) * glines, :]
            offset += glines
        left = edge_in[:n, :size]
        for _ in range(2):
            term = left.astype(BF16).astype(F32)
            left = left - term
            edge_in[:n, :size] = term
            for d in range(peers):
                if d * hlines < n:
                    rest[d, offset : offset + hlines] = edge_in[d * hlines : (d + 1) * hlines, :size]
                else:
                    rest[d, offset : offset + hlines] = jnp.zeros((hlines, size), F32)
            offset += hlines
        if offset < rest.shape[1]:
            rest[:, offset:, :] = jnp.zeros((peers, rest.shape[1] - offset, 2 * n), F32)
        send[:, wets:, :] = rest[...].astype(BF16)
    store.wait()


def advance(mode, total, peers, ids, rates, state, fixed):
    mixed, pick, place, spread = fixed
    width, size = pick.shape
    wets = place.shape[0]
    vectors = state[3].shape[0] if mode == "first" else state[2].shape[0]
    extra = 3 * -(-2 * vectors // peers) + 2 * -(-vectors // peers)
    extra = -(-extra // 16) * 16
    sds = jax.ShapeDtypeStruct
    block = pltpu.HBM((6 * vectors, width), BF16)
    small = sds((2 * vectors, 2 * vectors), F32)
    shapes, specs = [block], [HBM]
    if mode == "last":
        shapes += [small]
        specs += [VMEM]
    else:
        shapes += [
            sds((2 * vectors, 2 * size), F32),
            sds((wets, 2 * vectors), F32),
            sds((peers, wets // 2 + extra, 2 * vectors), BF16),
        ]
        specs += [VMEM] * 3
    if mode != "first":
        shapes += [sds((vectors, 2 * vectors), F32), small]
        specs += [VMEM, VMEM]
    scratch = [
        pltpu.VMEM((width // size + 2, vectors, size), BF16),
        pltpu.VMEM((6 * vectors, width), BF16),
        pltpu.VMEM((vectors, width), F32) if mode == "first" else pltpu.VMEM((6 * vectors, width), BF16),
        pltpu.VMEM(mixed.shape, BF16),
        pltpu.VMEM((2, spread.shape[0] // 2, spread.shape[1]) if mode != "last" else (16, 128), BF16),
        pltpu.VMEM((3 * vectors, 2 * size), F32),
        pltpu.SemaphoreType.DMA((5,)),
    ]
    if mode != "last":
        scratch += [pltpu.VMEM(small.shape, F32), pltpu.VMEM((peers, extra, 2 * vectors), F32)]
    if mode != "first":
        scratch += [pltpu.VMEM((vectors, 3 * vectors), F32), pltpu.VMEM((4 * vectors, 6 * vectors), BF16)]
    return pl.pallas_call(
        functools.partial(advance_kernel, mode, total, peers),
        in_specs=[SMEM, SMEM] + [VMEM] * (len(state) - 1) + [HBM, VMEM, VMEM, HBM, HBM],
        out_specs=specs,
        out_shape=shapes,
        scratch_shapes=scratch,
        compiler_params=pltpu.CompilerParams(vmem_limit_bytes=LIMIT),
        name="advance_" + mode,
    )(ids, rates, *state, pick, place, mixed, spread)


def route_kernel(vectors, wets, received, _lag, pressed, send, rest):
    peers = received.shape[0]
    glines = -(-2 * vectors // peers)
    hlines = -(-vectors // peers)
    pressed[...] = jnp.sum(received[:, :wets, :].astype(F32), 0)
    rest[...] = received[:, wets:, :].astype(F32)
    sums = jnp.sum(rest[...], 0)
    mine = sums[:glines] + sums[glines : 2 * glines] + sums[2 * glines : 3 * glines]
    edge = 3 * glines
    nothing = jnp.zeros((hlines, 2 * vectors), F32)

    def halo(t):
        if not 0 <= t < peers:
            return nothing
        return rest[t, edge : edge + hlines] + rest[t, edge + hlines : edge + 2 * hlines]

    send[...] = jnp.zeros(send.shape, F32)
    for t in range(peers):
        send[t, :glines] = mine
        send[t, glines : glines + hlines] = halo(t - 1)
        send[t, glines + hlines : glines + 2 * hlines] = halo(t + 1)


def route(vectors, wets, received, lag):
    peers, lines, lanes = received.shape
    return pl.pallas_call(
        functools.partial(route_kernel, vectors, wets),
        in_specs=[VMEM, VMEM],
        out_specs=[VMEM] * 2,
        out_shape=[
            jax.ShapeDtypeStruct((wets, 2 * vectors), F32),
            jax.ShapeDtypeStruct((peers, 8, 2 * vectors), F32),
        ],
        scratch_shapes=[pltpu.VMEM((peers, lines - wets, lanes), F32)],
        compiler_params=pltpu.CompilerParams(vmem_limit_bytes=LIMIT),
        name="route",
    )(received, lag)


def repeat_sum_kernel(received, _lag, send):
    mine = jnp.sum(received[...], 0)
    for t in range(send.shape[0]):
        send[t] = mine


def repeat_sum(received, lag):
    return pl.pallas_call(
        repeat_sum_kernel,
        in_specs=[VMEM, VMEM],
        out_specs=VMEM,
        out_shape=jax.ShapeDtypeStruct(received.shape, F32),
        compiler_params=pltpu.CompilerParams(vmem_limit_bytes=LIMIT),
        name="repeat_sum",
    )(received, lag)


def finish_kernel(total, gram, inner, lag, state, *refs):
    *earlier, out, coefs, factor_t, mix, weights, both, stack, fresh, sem = refs
    coef = coefs.at[len(earlier)]
    n = inner.shape[0]
    load = pltpu.make_async_copy(state, stack, sem)
    load.start()
    blend(total, gram, lag, both, mix)
    for k, known in enumerate(earlier):
        coefs[k] = known[...]
    put_weights(weights, mix[...], lag[:, :n])
    load.wait()

    def next_residual():
        mixture = jnp.dot(weights[...], stack[...], preferred_element_type=F32)
        fresh[...] = mixture[:n] + mixture[n:]

    inverse, _, _ = settle(total, gram, inner, lag, both, [next_residual], coef, factor_t)
    out[...] = exact(inverse, fresh[...])


def finish(total, gram, inner, lag, state, earlier):
    vectors, width = lag.shape[0], state.shape[1]
    return pl.pallas_call(
        functools.partial(finish_kernel, total),
        in_specs=[VMEM] * 3 + [HBM] + [VMEM] * len(earlier),
        out_specs=[VMEM] * 2,
        out_shape=[
            pltpu.HBM((vectors, width), F32),
            pltpu.HBM((len(earlier) + 1, 3, vectors, vectors), F32),
        ],
        scratch_shapes=[
            pltpu.VMEM((vectors, 2 * vectors), F32),
            pltpu.VMEM((vectors, 3 * vectors), F32),
            pltpu.VMEM((2 * vectors, 6 * vectors), BF16),
            pltpu.VMEM((vectors, 2 * vectors), F32),
            pltpu.VMEM((6 * vectors, width), BF16),
            pltpu.VMEM((vectors, width), F32),
            pltpu.SemaphoreType.DMA,
        ],
        compiler_params=pltpu.CompilerParams(vmem_limit_bytes=LIMIT),
        name="finish",
    )(gram, inner, lag, state, *earlier)


def local(n_row, n_col, start_block, struct_blocks, block_ids, rim_rows, wet_slots, wet_counts, added_mass, rates):
    peers = n_row * n_col
    vectors, width = start_block.shape
    total = float(width * peers)
    wcap = wet_slots.shape[0]
    wets = added_mass.shape[0] // n_row

    def exchange(parts):
        return lax.all_to_all(parts, AXES, 0, 0, tiled=True)

    def neighbours(halo):
        up = [(i, i + 1) for i in range(peers - 1)]
        down = [(i + 1, i) for i in range(peers - 1)]
        return lax.ppermute(halo, AXES, up), lax.ppermute(halo, AXES, down)

    def summed(gram, lag):
        lines = gram.shape[0] // peers
        return exchange(repeat_sum(exchange(gram.reshape(peers, lines, -1)), lag)).reshape(gram.shape)

    blocks = by_owner(in_hbm(added_mass), n_col, wcap)
    mass = lax.all_to_all(blocks, "col", 0, 0, tiled=True)
    mass = mass.reshape(n_col, n_row, 2, wets // 2, wcap)
    slots = wet_slots[None, :]
    mixed, pick, place, halo, values = combine(
        rates, wet_counts, rim_rows[None, :], wet_slots[:wets, None], slots, start_block, struct_blocks
    )
    below, above = neighbours(halo)
    part = start_pressure(values, mass)
    spread = spread_mass(wet_counts, slots, mass, width)
    fixed = (in_hbm(mixed), pick, place, in_hbm(spread))
    arrived = exchange(part.reshape(peers, wets // 2, 2 * vectors))
    step = functools.partial(advance, total=total, peers=peers, ids=block_ids, rates=rates, fixed=fixed)
    state, edges, wet_held, send = step("first", state=(arrived, below, above, in_hbm(start_block)))
    inner = jnp.zeros((vectors, 2 * vectors), F32)
    unit = jnp.eye(vectors, dtype=F32)
    lag = jnp.concatenate([unit, unit], 1)
    coefficients = []
    for number in range(1, STEPS):
        pressed, again = route(vectors, wets // 2, exchange(send), lag)
        received = exchange(again)
        known = (received, pressed, lag, edges, wet_held, in_hbm(state))
        if number < STEPS - 1:
            state, edges, wet_held, send, both, gram = step("mid", state=known)
        else:
            state, products, both, gram = step("last", state=known)
        lag, inner, coef = factor(total, gram, inner, lag, both)
        coefficients.append(coef)
    final, coefs = finish(total, summed(products, lag), inner, lag, in_hbm(state), coefficients)
    return final, coefs


def solution(mesh):
    return jax.shard_map(
        functools.partial(local, mesh.shape["row"], mesh.shape["col"]),
        mesh=mesh,
        in_specs=(
            P(None, AXES),
            P(None, AXES, None, None, None),
            P(AXES, None),
            P(AXES),
            P(AXES),
            P(AXES),
            P("col", "row"),
            P(),
        ),
        out_specs=(P(None, AXES), P()),
        check_vma=False,
    )
```

```python
import functools

import jax
import jax.numpy as jnp
from jax import lax
from jax.experimental import pallas as pl
from jax.experimental.pallas import tpu as pltpu
from jax.sharding import PartitionSpec as P

STEPS = 6
AXES = ("row", "col")
VMEM = pl.BlockSpec(memory_space=pltpu.VMEM)
SMEM = pl.BlockSpec(memory_space=pltpu.SMEM)
HBM = pl.BlockSpec(memory_space=pltpu.HBM)
ANY = pl.BlockSpec(memory_space=pl.ANY)
F32 = jnp.float32
BF16 = jnp.bfloat16
LIMIT = 40 * 1024 * 1024


def exact(left, right):
    return lax.dot_general(
        left, right, (((1,), (0,)), ((), ())), precision=lax.Precision.HIGHEST, preferred_element_type=F32
    )


def exact_rows(left, right):
    return lax.dot_general(
        left, right, (((1,), (1,)), ((), ())), precision=lax.Precision.HIGHEST, preferred_element_type=F32
    )


def rows(left, right):
    return lax.dot_general(left, right, (((1,), (1,)), ((), ())), preferred_element_type=F32)


def in_hbm(values):
    return pltpu.with_memory_space_constraint(values, pltpu.HBM)


def halves(values):
    high = values.astype(BF16)
    return high, (values - high.astype(F32)).astype(BF16)


def by_owner_kernel(mass, out, held, sems):
    wcap = out.shape[2]
    reads, writes = [], []
    for c in range(out.shape[0]):
        reads.append(pltpu.make_async_copy(mass.at[:, pl.ds(c * wcap, wcap)], held.at[c], sems.at[0, c]))
        writes.append(pltpu.make_async_copy(held.at[c], out.at[c], sems.at[1, c]))
        reads[-1].start()
    for read, write in zip(reads, writes):
        read.wait()
        write.start()
    for write in writes:
        write.wait()


def by_owner(mass, n_col, wcap):
    shape = (n_col, mass.shape[0], wcap)
    return pl.pallas_call(
        by_owner_kernel,
        in_specs=[HBM],
        out_specs=HBM,
        out_shape=pltpu.HBM(shape, BF16),
        scratch_shapes=[pltpu.VMEM(shape, BF16), pltpu.SemaphoreType.DMA((2, n_col))],
        compiler_params=pltpu.CompilerParams(vmem_limit_bytes=LIMIT),
        name="by_owner",
    )(mass)


def combine_kernel(rates, count, rim, wet, slots, start, blocks, mixed, pick, place, halo, values):
    size = blocks.shape[-1]
    for k in range(blocks.shape[2]):
        whole = (
            blocks[0, 0, k].astype(F32)
            + rates[0] * blocks[1, 0, k].astype(F32)
            - rates[1] * blocks[2, 0, k].astype(F32)
        ).T
        mixed[0, k * size : (k + 1) * size] = whole.astype(BF16)

    @pl.when(pl.program_id(0) == 0)
    def _():
        index = lax.broadcasted_iota(jnp.int32, pick.shape, 0)
        pick[...] = jnp.where(index == rim[...], 1.0, 0.0).astype(BF16)
        index = lax.broadcasted_iota(jnp.int32, place.shape, 1)
        place[...] = jnp.where(index == wet[...], 1.0, 0.0).astype(BF16)
        high, low = halves(start[...])
        halo[...] = jnp.dot(high, pick[...], preferred_element_type=F32) + jnp.dot(
            low, pick[...], preferred_element_type=F32
        )
        live = live_slots(count, slots)
        columns = min(start.shape[1], 512)
        total = jnp.zeros(values.shape, F32)
        for first in range(0, start.shape[1], columns):
            picked = chosen(first, (columns, slots.shape[1]), live)
            total = total + jnp.dot(high[:, first : first + columns], picked, preferred_element_type=F32)
        values[...] = total.astype(BF16)


def combine(rates, count, rim, wet, slots, start, blocks):
    _, block_rows, nnz, size, _ = blocks.shape
    vectors, width = start.shape
    whole = lambda shape: pl.BlockSpec(shape, lambda i: (0,) * len(shape))
    return pl.pallas_call(
        combine_kernel,
        grid=(block_rows,),
        in_specs=[
            SMEM,
            SMEM,
            whole(rim.shape),
            whole(wet.shape),
            whole(slots.shape),
            whole(start.shape),
            pl.BlockSpec((3, 1, nnz, size, size), lambda i: (0, i, 0, 0, 0)),
        ],
        out_specs=[
            pl.BlockSpec((1, nnz * size, size), lambda i: (i, 0, 0)),
            whole((width, rim.shape[1])),
            whole((wet.shape[0], width)),
            whole((vectors, rim.shape[1])),
            whole((vectors, slots.shape[1])),
        ],
        out_shape=[
            pltpu.HBM((block_rows, nnz * size, size), BF16),
            jax.ShapeDtypeStruct((width, rim.shape[1]), BF16),
            jax.ShapeDtypeStruct((wet.shape[0], width), BF16),
            jax.ShapeDtypeStruct((vectors, rim.shape[1]), F32),
            jax.ShapeDtypeStruct((vectors, slots.shape[1]), BF16),
        ],
        compiler_params=pltpu.CompilerParams(vmem_limit_bytes=LIMIT),
        name="combine",
    )(rates, count, rim, wet, slots, start, blocks)


def live_slots(count, slots):
    slot = lax.broadcasted_iota(jnp.int32, slots.shape, 1)
    return jnp.where(slot < count[0], slots[...], -1)


def chosen(first, shape, live):
    index = lax.broadcasted_iota(jnp.int32, shape, 0) + first
    return jnp.where(index == live, 1.0, 0.0).astype(BF16)


def start_pressure_kernel(values, mass, part):
    n_col, n_row, _, half, wcap = mass.shape
    size, vectors = n_col * half, values.shape[0]
    for r in range(n_row):
        for h in range(2):
            own = mass[:, r, h].reshape(size, wcap)
            pressed = rows(own, values[...]).astype(BF16)
            part[r * size : (r + 1) * size, h * vectors : (h + 1) * vectors] = pressed


def start_pressure(values, mass):
    n_col, n_row, _, half, _ = mass.shape
    return pl.pallas_call(
        start_pressure_kernel,
        in_specs=[VMEM, VMEM],
        out_specs=VMEM,
        out_shape=jax.ShapeDtypeStruct((n_col * n_row * half, 2 * values.shape[0]), BF16),
        compiler_params=pltpu.CompilerParams(vmem_limit_bytes=LIMIT),
        name="start_pressure",
    )(values, mass)


def spread_kernel(count, slots, mass, spread, own):
    n_col, n_row, _, half, wcap = mass.shape
    size = n_col * half

    @pl.when(pl.program_id(0) == 0)
    def _():
        for h in range(2):
            for r in range(n_row):
                first = (h * n_row + r) * size
                own[first : first + size] = mass[:, r, h].reshape(size, wcap)

    columns = spread.shape[1]
    onehot = chosen(pl.program_id(0) * columns, (columns, wcap), live_slots(count, slots))
    spread[...] = rows(own[...], onehot).astype(BF16)


def spread_mass(count, slots, mass, width):
    n_col, n_row, _, half, wcap = mass.shape
    size = n_col * n_row * half
    columns = min(width, 512)
    return pl.pallas_call(
        spread_kernel,
        grid=(width // columns,),
        in_specs=[
            SMEM,
            pl.BlockSpec(slots.shape, lambda i: (0, 0)),
            pl.BlockSpec(mass.shape, lambda i: (0,) * 5),
        ],
        out_specs=pl.BlockSpec((2 * size, columns), lambda i: (0, i)),
        out_shape=pltpu.HBM((2 * size, width), BF16),
        scratch_shapes=[pltpu.VMEM((2 * size, wcap), BF16)],
        compiler_params=pltpu.CompilerParams(vmem_limit_bytes=LIMIT),
        cost_estimate=pl.CostEstimate(
            flops=4 * size * wcap * width, bytes_accessed=4 * size * width, transcendentals=0
        ),
        name="spread",
    )(count, slots, mass)


def pivot_rows(top, s):
    lanes = top[0].shape[1]
    at = lambda i, j: jnp.broadcast_to(top[i][:, s + j : s + j + 1], (1, lanes))
    a, b, c = at(0, 0), at(0, 1), at(1, 1)
    p2, q2, p3, q3 = at(2, 0), at(2, 1), at(3, 0), at(3, 1)
    d22, d23, d33 = at(2, 2), at(2, 3), at(3, 3)
    scale = 1.0 / (a * c - b * b)
    first = ((c * top[0] - b * top[1]) * scale, (a * top[1] - b * top[0]) * scale)
    y02, y03 = (c * p2 - b * q2) * scale, (c * p3 - b * q3) * scale
    y12, y13 = (a * q2 - b * p2) * scale, (a * q3 - b * p3) * scale
    a2 = d22 - p2 * y02 - q2 * y12
    b2 = d23 - p2 * y03 - q2 * y13
    c2 = d33 - p3 * y03 - q3 * y13
    scale2 = 1.0 / (a2 * c2 - b2 * b2)
    third = top[2] - p2 * first[0] - q2 * first[1]
    fourth = top[3] - p3 * first[0] - q3 * first[1]
    v2 = (c2 * third - b2 * fourth) * scale2
    v3 = (a2 * fourth - b2 * third) * scale2
    v0 = first[0] - y02 * v2 - y03 * v3
    v1 = first[1] - y12 * v2 - y13 * v3
    return first, (v0, v1, v2, v3)


def eliminate_four(work, s, j, keep):
    sub = lax.broadcasted_iota(jnp.int32, (8, 1), 0)
    first, full = pivot_rows([work[0][s + k : s + k + 1, :] for k in range(4)], j)
    out = []
    for i, group in enumerate(work):
        columns = [group[:, j + k : j + k + 1] for k in range(4)]
        half = columns[0] * full[0] + columns[1] * full[1]
        update = half + (columns[2] * full[2] + columns[3] * full[3])
        if i == 0:
            pair = columns[0] * first[0] + columns[1] * first[1]
            update = jnp.where(sub > s + 3, update, jnp.where(sub > s + 1, pair, 0.0))
        elif keep is not None:
            update = jnp.where(keep(i), update, 0.0)
        out.append(group - update)
    return out


def eliminate(matrix, beside, coef, factor_t):
    n = matrix.shape[0]
    groups = n // 8
    row_id = lax.broadcasted_iota(jnp.int32, (n, 2 * n), 0)
    lane_id = lax.broadcasted_iota(jnp.int32, (n, 2 * n), 1)
    factor_t[...] = jnp.where(row_id + n == lane_id, 1.0, 0.0)
    factor_t[:, :n] = matrix
    if beside:
        work = [factor_t[g * 8 : (g + 1) * 8, :] for g in range(groups)]
        done = 0
        for j in range(0, n, 4):
            g, s = divmod(j, 8)
            work[g:] = eliminate_four(work[g:], s, j, None)
            goal = len(beside) * (j + 4) // n
            while done < goal:
                beside[done]()
                done += 1
        reduced = jnp.concatenate(work, 0)
    else:

        def group(step, _):
            work = [factor_t[g * 8 : (g + 1) * 8, :] for g in range(groups)]
            for s in range(0, 8, 4):
                work = eliminate_four(work, s, s, lambda i: step + i < groups)
            for i in range(groups):
                target = (i - 1) % groups
                factor_t[target * 8 : (target + 1) * 8, :] = pltpu.roll(work[i], 2 * n - 8, 1)
            return 0

        lax.fori_loop(0, groups, group, 0)
        reduced = pltpu.roll(factor_t[...], n, 1)
    above = pltpu.roll(reduced, 1, 0)
    odd = lax.broadcasted_iota(jnp.int32, (n, 1), 0) % 2 == 1
    pick = lambda values, where: jnp.sum(jnp.where(where, values, 0.0), 1, keepdims=True)
    under = pick(above, lane_id == row_id) / jnp.where(odd, pick(above, lane_id + 1 == row_id), 1.0)
    reduced = reduced - jnp.where(odd, under, 0.0) * above
    diagonal = pick(reduced, lane_id == row_id)
    scale = lax.rsqrt(diagonal)
    scale = scale * (1.5 - 0.5 * diagonal * scale * scale)
    reduced = reduced * scale
    factor_t[...] = reduced
    upper = jnp.where(row_id <= lane_id, reduced, 0.0)
    coef[2] = upper.T[:n, :]
    return factor_t[:, n:]


def congruent(factor, matrix):
    return exact(factor, exact_rows(matrix, factor))


def settle(total, gram, inner, lag, both, beside, coef, factor_t):
    n = gram.shape[0] // 2
    scale = 1.0 / total
    pull = lag[:, :n]
    aa = congruent(pull, gram[:n, :n] * scale)
    cc = congruent(pull, gram[n:, n:] * scale)
    self_ = both[:, :n]
    prev = both[:, n:]
    cp = inner[:, :n]
    pp = inner[:, n:]
    coef[0] = self_
    coef[1] = prev
    t_c = self_ - exact(self_, cc) - exact_rows(prev, cp)
    t_p = prev - exact(self_, cp) - exact(prev, pp)
    t_a = aa - exact_rows(self_, self_) - exact_rows(prev, prev)
    matrix = t_a - exact_rows(t_c, self_) - exact_rows(t_p, prev)
    inverse = eliminate(0.5 * (matrix + matrix.T), beside, coef, factor_t)
    return inverse, t_c, cc


def put_weights(weights, mix, pull):
    n = mix.shape[0]
    high, low = halves(mix)
    pull_high, pull_low = halves(pull)
    for k in range(3):
        cut = slice(k * n, (k + 1) * n)
        weights[:n, 2 * k * n : (2 * k + 1) * n] = high[:, cut]
        weights[:n, (2 * k + 1) * n : (2 * k + 2) * n] = high[:, cut]
        weights[n : 2 * n, 2 * k * n : (2 * k + 1) * n] = low[:, cut]
        weights[n : 2 * n, (2 * k + 1) * n : (2 * k + 2) * n] = jnp.zeros((n, n), BF16)
    if weights.shape[0] > 2 * n:
        weights[2 * n :, :] = jnp.zeros((2 * n, 6 * n), BF16)
        weights[2 * n : 3 * n, 2 * n : 3 * n] = pull_high
        weights[2 * n : 3 * n, 3 * n : 4 * n] = pull_high
        weights[3 * n :, 2 * n : 3 * n] = pull_low


def blend(total, gram, lag, both, mix):
    n = gram.shape[0] // 2
    scale = 1.0 / total
    pull, square = lag[:, :n], lag[:, n:]
    crossed = gram[:n, n:] * scale
    prev = exact(pull, gram[n:, :n] * scale)
    mix[:, :n] = pull
    mix[:, n : 2 * n] = -exact(pull, exact(crossed, square))
    mix[:, 2 * n :] = -prev
    both[:, :n] = congruent(pull, crossed)
    both[:, n:] = prev


def factor_kernel(total, gram, inner, lag, both, lag_out, inner_out, coef, factor_t):
    n = gram.shape[0] // 2
    inverse, t_c, cc = settle(total, gram, inner, lag, both, [], coef, factor_t)
    lag_out[:, :n] = inverse
    lag_out[:, n:] = exact(inverse.T, inverse)
    inner_out[:, :n] = exact(inverse, t_c)
    inner_out[:, n:] = cc


def factor(total, gram, inner, lag, both):
    n = gram.shape[0] // 2
    sds = jax.ShapeDtypeStruct
    return pl.pallas_call(
        functools.partial(factor_kernel, total),
        in_specs=[VMEM] * 4,
        out_specs=[VMEM] * 3,
        out_shape=[sds((n, 2 * n), F32), sds((n, 2 * n), F32), sds((3, n, n), F32)],
        scratch_shapes=[pltpu.VMEM((n, 2 * n), F32)],
        compiler_params=pltpu.CompilerParams(vmem_limit_bytes=LIMIT),
        cost_estimate=pl.CostEstimate(flops=100_000_000, bytes_accessed=10_000_000, transcendentals=0),
        name="factor",
    )(gram, inner, lag, both)


def thirds(values):
    high = values.astype(BF16)
    rest = values - high.astype(F32)
    return jnp.concatenate([high, *halves(rest)], 0)


def unpack(lines, received, target, lanes, offset):
    for s in range(received.shape[0]):
        if s * lines < target.shape[0]:
            target[s * lines : (s + 1) * lines, lanes] = received[s, offset : offset + lines]


def place_columns(extended, block, edge):
    size = extended.shape[2]
    count = extended.shape[0] - 2
    for i in range(count):
        extended[i] = block[:, i * size : (i + 1) * size]
    extended[count] = edge[:, :size].astype(BF16)
    extended[count + 1] = edge[:, size:].astype(BF16)


def block_row(ids, extended, mixed, i):
    picked = jnp.concatenate([extended[ids[i, k]] for k in range(ids.shape[1])], 1)
    return jnp.dot(picked, mixed[i], preferred_element_type=F32)


def advance_kernel(mode, total, peers, *refs):
    it = iter(refs)
    take = lambda k: [next(it) for _ in range(k)]
    ids, rates = take(2)
    if mode == "first":
        arrived, below, above = take(3)
    else:
        received, pressed, lag, edges, wet_held = take(5)
    (held,) = take(1)
    pick, place, mixed_in, spread_in = take(4)
    (state_out,) = take(1)
    if mode == "last":
        (gram_s,) = take(1)
    else:
        edges_out, wet_out, send = take(3)
    if mode != "first":
        both, gram_in = take(2)
    extended, terms, stack, mixed, spread, edge_in, sems = take(7)
    if mode != "last":
        gram_s, rest = take(2)
    if mode != "first":
        mix, weights = take(2)

    n = terms.shape[0] // 6
    width = terms.shape[1]
    size = edge_in.shape[1] // 2
    count = width // size
    glines = -(-2 * n // peers)
    hlines = -(-n // peers)
    load = pltpu.make_async_copy(held, stack, sems.at[0])
    load.start()
    load_mixed = pltpu.make_async_copy(mixed_in, mixed, sems.at[1])
    load_mixed.start()
    load_spread = []
    if mode != "last":
        for h in range(2):
            part = spread_in.at[pl.ds(h * spread.shape[1], spread.shape[1])]
            load_spread.append(pltpu.make_async_copy(part, spread.at[h], sems.at[3 + h]))
            load_spread[-1].start()

    if mode == "first":
        edge = jnp.concatenate([below[...], above[...]], 1)
        summed = jnp.sum(arrived[...].astype(F32), 0)
        wet = jnp.concatenate([summed[:, :n], summed[:, n:]], 0)
        edges_out[:n, :] = edge
        edges_out[n:, :] = jnp.zeros_like(edge)
        wet_out[:, :n] = wet
        wet_out[:, n:] = jnp.zeros_like(wet)
        load.wait()
        residual = stack[...]
        terms[4 * n :, :] = jnp.zeros((2 * n, width), BF16)
    else:
        unpack(glines, received, gram_in, slice(None), 0)
        unpack(hlines, received, edge_in.at[pl.ds(0, n)], slice(0, size), glines)
        unpack(hlines, received, edge_in.at[pl.ds(0, n)], slice(size, 2 * size), glines + hlines)
        edge_in[n:, :] = edges[...]
        blend(total, gram_in, lag, both, mix)
        pull = lag[:, :n]
        put_weights(weights, mix[...], pull)
        edge = exact(mix[...], edge_in[...])
        summed = pressed[...]
        wet = exact_rows(jnp.concatenate([summed[:, :n], summed[:, n:]], 0), pull)
        wet = wet + exact_rows(wet_held[...], mix[:, n:])
        if mode != "last":
            edges_out[:n, :] = edge
            edges_out[n:, :] = exact(pull, edges[:n, :])
            wet_out[:, :n] = wet
            wet_out[:, n:] = exact_rows(wet_held[:, :n], pull)
        load.wait()
        mixture = jnp.dot(weights[...], stack[...], preferred_element_type=F32)
        residual = mixture[:n] + mixture[n : 2 * n]
        terms[4 * n : 5 * n, :], terms[5 * n :, :] = halves(mixture[2 * n : 3 * n] + mixture[3 * n :])
    high, low = halves(residual)
    terms[2 * n : 3 * n, :] = high
    terms[3 * n : 4 * n, :] = low
    force = thirds(wet.T * rates[1])
    place_columns(extended, high, edge)
    load_mixed.wait()
    for i in range(count):
        lanes = slice(i * size, (i + 1) * size)
        added = jnp.dot(force, place[:, lanes], preferred_element_type=F32)
        applied = block_row(ids, extended, mixed, i) - (added[:n] + added[n : 2 * n] + added[2 * n :])
        terms[:n, lanes], terms[n : 2 * n, lanes] = halves(applied)
    store = pltpu.make_async_copy(terms, state_out, sems.at[2])
    store.start()

    known = 4 * n if mode == "first" else 6 * n
    products = rows(terms[: 2 * n, :], terms[:known, :])
    products = products[:n] + products[n:]
    gram_s[:n, :n] = products[:, :n] + products[:, n : 2 * n]
    gram_s[:n, n:] = products[:, 2 * n : 3 * n] + products[:, 3 * n : 4 * n]
    if mode == "first":
        gram_s[n:, :n] = jnp.zeros((n, n), F32)
    else:
        gram_s[n:, :n] = products[:, 4 * n : 5 * n] + products[:, 5 * n :]
    squares = rows(terms[2 * n : 4 * n, :], terms[2 * n : 4 * n, :])
    squares = squares[:n] + squares[n:]
    gram_s[n:, n:] = squares[:, :n] + squares[:, n:]
    if mode != "last":
        rim = jnp.dot(terms[: 2 * n, :], pick[...], preferred_element_type=F32)
        edge_in[:n, :size] = rim[:n] + rim[n:]
        wets = wet_out.shape[0] // 2
        for copy in load_spread:
            copy.wait()
        tops = rows(spread[0], terms[: 2 * n, :])
        tops = tops + pltpu.roll(tops, n, 1)
        ends = rows(spread[1], terms[: 2 * n, :])
        ends = ends + pltpu.roll(ends, n, 1)
        lane = lax.broadcasted_iota(jnp.int32, tops.shape, 1)
        send[:, :wets, :] = jnp.where(lane < n, tops, ends).astype(BF16).reshape(peers, wets, 2 * n)
        left = gram_s[...]
        offset = 0
        for _ in range(3):
            term = left.astype(BF16).astype(F32)
            left = left - term
            gram_s[...] = term
            for d in range(peers):
                if d * glines < 2 * n:
                    rest[d, offset : offset + glines] = gram_s[d * glines : (d + 1) * glines, :]
            offset += glines
        left = edge_in[:n, :size]
        for _ in range(2):
            term = left.astype(BF16).astype(F32)
            left = left - term
            edge_in[:n, :size] = term
            for d in range(peers):
                if d * hlines < n:
                    rest[d, offset : offset + hlines] = edge_in[d * hlines : (d + 1) * hlines, :size]
                else:
                    rest[d, offset : offset + hlines] = jnp.zeros((hlines, size), F32)
            offset += hlines
        if offset < rest.shape[1]:
            rest[:, offset:, :] = jnp.zeros((peers, rest.shape[1] - offset, 2 * n), F32)
        send[:, wets:, :] = rest[...].astype(BF16)
    store.wait()


def advance(mode, total, peers, ids, rates, state, fixed):
    mixed, pick, place, spread = fixed
    width, size = pick.shape
    wets = place.shape[0]
    vectors = state[3].shape[0] if mode == "first" else state[2].shape[0]
    extra = 3 * -(-2 * vectors // peers) + 2 * -(-vectors // peers)
    extra = -(-extra // 16) * 16
    sds = jax.ShapeDtypeStruct
    block = pltpu.HBM((6 * vectors, width), BF16)
    small = sds((2 * vectors, 2 * vectors), F32)
    shapes, specs = [block], [HBM]
    if mode == "last":
        shapes += [small]
        specs += [VMEM]
    else:
        shapes += [
            sds((2 * vectors, 2 * size), F32),
            sds((wets, 2 * vectors), F32),
            sds((peers, wets // 2 + extra, 2 * vectors), BF16),
        ]
        specs += [VMEM] * 3
    if mode != "first":
        shapes += [sds((vectors, 2 * vectors), F32), small]
        specs += [VMEM, VMEM]
    scratch = [
        pltpu.VMEM((width // size + 2, vectors, size), BF16),
        pltpu.VMEM((6 * vectors, width), BF16),
        pltpu.VMEM((vectors, width), F32) if mode == "first" else pltpu.VMEM((6 * vectors, width), BF16),
        pltpu.VMEM(mixed.shape, BF16),
        pltpu.VMEM((2, spread.shape[0] // 2, spread.shape[1]) if mode != "last" else (16, 128), BF16),
        pltpu.VMEM((3 * vectors, 2 * size), F32),
        pltpu.SemaphoreType.DMA((5,)),
    ]
    if mode != "last":
        scratch += [pltpu.VMEM(small.shape, F32), pltpu.VMEM((peers, extra, 2 * vectors), F32)]
    if mode != "first":
        scratch += [pltpu.VMEM((vectors, 3 * vectors), F32), pltpu.VMEM((4 * vectors, 6 * vectors), BF16)]
    return pl.pallas_call(
        functools.partial(advance_kernel, mode, total, peers),
        in_specs=[SMEM, SMEM] + [VMEM] * (len(state) - 1) + [HBM, VMEM, VMEM, HBM, HBM],
        out_specs=specs,
        out_shape=shapes,
        scratch_shapes=scratch,
        compiler_params=pltpu.CompilerParams(vmem_limit_bytes=LIMIT),
        name="advance_" + mode,
    )(ids, rates, *state, pick, place, mixed, spread)


def route_kernel(vectors, wets, received, _lag, pressed, send, rest):
    peers = received.shape[0]
    glines = -(-2 * vectors // peers)
    hlines = -(-vectors // peers)
    pressed[...] = jnp.sum(received[:, :wets, :].astype(F32), 0)
    rest[...] = received[:, wets:, :].astype(F32)
    sums = jnp.sum(rest[...], 0)
    mine = sums[:glines] + sums[glines : 2 * glines] + sums[2 * glines : 3 * glines]
    edge = 3 * glines
    nothing = jnp.zeros((hlines, 2 * vectors), F32)

    def halo(t):
        if not 0 <= t < peers:
            return nothing
        return rest[t, edge : edge + hlines] + rest[t, edge + hlines : edge + 2 * hlines]

    send[...] = jnp.zeros(send.shape, F32)
    for t in range(peers):
        send[t, :glines] = mine
        send[t, glines : glines + hlines] = halo(t - 1)
        send[t, glines + hlines : glines + 2 * hlines] = halo(t + 1)


def route(vectors, wets, received, lag):
    peers, lines, lanes = received.shape
    return pl.pallas_call(
        functools.partial(route_kernel, vectors, wets),
        in_specs=[VMEM, VMEM],
        out_specs=[VMEM] * 2,
        out_shape=[
            jax.ShapeDtypeStruct((wets, 2 * vectors), F32),
            jax.ShapeDtypeStruct((peers, 8, 2 * vectors), F32),
        ],
        scratch_shapes=[pltpu.VMEM((peers, lines - wets, lanes), F32)],
        compiler_params=pltpu.CompilerParams(vmem_limit_bytes=LIMIT),
        name="route",
    )(received, lag)


def repeat_sum_kernel(received, _lag, send):
    mine = jnp.sum(received[...], 0)
    for t in range(send.shape[0]):
        send[t] = mine


def repeat_sum(received, lag):
    return pl.pallas_call(
        repeat_sum_kernel,
        in_specs=[VMEM, VMEM],
        out_specs=VMEM,
        out_shape=jax.ShapeDtypeStruct(received.shape, F32),
        compiler_params=pltpu.CompilerParams(vmem_limit_bytes=LIMIT),
        name="repeat_sum",
    )(received, lag)


def finish_kernel(total, gram, inner, lag, state, *refs):
    *earlier, out, coefs, factor_t, mix, weights, both, stack, fresh, sem = refs
    coef = coefs.at[len(earlier)]
    n = inner.shape[0]
    load = pltpu.make_async_copy(state, stack, sem)
    load.start()
    blend(total, gram, lag, both, mix)
    for k, known in enumerate(earlier):
        coefs[k] = known[...]
    put_weights(weights, mix[...], lag[:, :n])
    load.wait()

    def next_residual():
        mixture = jnp.dot(weights[...], stack[...], preferred_element_type=F32)
        fresh[...] = mixture[:n] + mixture[n:]

    inverse, _, _ = settle(total, gram, inner, lag, both, [next_residual], coef, factor_t)
    out[...] = exact(inverse, fresh[...])


def finish(total, gram, inner, lag, state, earlier):
    vectors, width = lag.shape[0], state.shape[1]
    return pl.pallas_call(
        functools.partial(finish_kernel, total),
        in_specs=[VMEM] * 3 + [HBM] + [VMEM] * len(earlier),
        out_specs=[VMEM] * 2,
        out_shape=[
            pltpu.HBM((vectors, width), F32),
            pltpu.HBM((len(earlier) + 1, 3, vectors, vectors), F32),
        ],
        scratch_shapes=[
            pltpu.VMEM((vectors, 2 * vectors), F32),
            pltpu.VMEM((vectors, 3 * vectors), F32),
            pltpu.VMEM((2 * vectors, 6 * vectors), BF16),
            pltpu.VMEM((vectors, 2 * vectors), F32),
            pltpu.VMEM((6 * vectors, width), BF16),
            pltpu.VMEM((vectors, width), F32),
            pltpu.SemaphoreType.DMA,
        ],
        compiler_params=pltpu.CompilerParams(vmem_limit_bytes=LIMIT),
        name="finish",
    )(gram, inner, lag, state, *earlier)


def local(n_row, n_col, start_block, struct_blocks, block_ids, rim_rows, wet_slots, wet_counts, added_mass, rates):
    peers = n_row * n_col
    vectors, width = start_block.shape
    total = float(width * peers)
    wcap = wet_slots.shape[0]
    wets = added_mass.shape[0] // n_row

    def exchange(parts):
        return lax.all_to_all(parts, AXES, 0, 0, tiled=True)

    def neighbours(halo):
        up = [(i, i + 1) for i in range(peers - 1)]
        down = [(i + 1, i) for i in range(peers - 1)]
        return lax.ppermute(halo, AXES, up), lax.ppermute(halo, AXES, down)

    def summed(gram, lag):
        lines = gram.shape[0] // peers
        return exchange(repeat_sum(exchange(gram.reshape(peers, lines, -1)), lag)).reshape(gram.shape)

    blocks = by_owner(in_hbm(added_mass), n_col, wcap)
    mass = lax.all_to_all(blocks, "col", 0, 0, tiled=True)
    mass = mass.reshape(n_col, n_row, 2, wets // 2, wcap)
    slots = wet_slots[None, :]
    mixed, pick, place, halo, values = combine(
        rates, wet_counts, rim_rows[None, :], wet_slots[:wets, None], slots, start_block, struct_blocks
    )
    below, above = neighbours(halo)
    part = start_pressure(values, mass)
    spread = spread_mass(wet_counts, slots, mass, width)
    fixed = (in_hbm(mixed), pick, place, in_hbm(spread))
    arrived = exchange(part.reshape(peers, wets // 2, 2 * vectors))
    step = functools.partial(advance, total=total, peers=peers, ids=block_ids, rates=rates, fixed=fixed)
    state, edges, wet_held, send = step("first", state=(arrived, below, above, in_hbm(start_block)))
    inner = jnp.zeros((vectors, 2 * vectors), F32)
    unit = jnp.eye(vectors, dtype=F32)
    lag = jnp.concatenate([unit, unit], 1)
    coefficients = []
    for number in range(1, STEPS):
        pressed, again = route(vectors, wets // 2, exchange(send), lag)
        received = exchange(again)
        known = (received, pressed, lag, edges, wet_held, in_hbm(state))
        if number < STEPS - 1:
            state, edges, wet_held, send, both, gram = step("mid", state=known)
        else:
            state, products, both, gram = step("last", state=known)
        lag, inner, coef = factor(total, gram, inner, lag, both)
        coefficients.append(coef)
    final, coefs = finish(total, summed(products, lag), inner, lag, in_hbm(state), coefficients)
    return final, coefs


def solution(mesh):
    return jax.shard_map(
        functools.partial(local, mesh.shape["row"], mesh.shape["col"]),
        mesh=mesh,
        in_specs=(
            P(None, AXES),
            P(None, AXES, None, None, None),
            P(AXES, None),
            P(AXES),
            P(AXES),
            P(AXES),
            P("col", "row"),
            P(),
        ),
        out_specs=(P(None, AXES), P()),
        check_vma=False,
    )
```

```python
import functools

import jax
import jax.numpy as jnp
from jax import lax
from jax.experimental import pallas as pl
from jax.experimental.pallas import tpu as pltpu
from jax.sharding import PartitionSpec as P

STEPS = 6
AXES = ("row", "col")
VMEM = pl.BlockSpec(memory_space=pltpu.VMEM)
SMEM = pl.BlockSpec(memory_space=pltpu.SMEM)
HBM = pl.BlockSpec(memory_space=pltpu.HBM)
ANY = pl.BlockSpec(memory_space=pl.ANY)
F32 = jnp.float32
BF16 = jnp.bfloat16
LIMIT = 40 * 1024 * 1024


def exact(left, right):
    return lax.dot_general(
        left, right, (((1,), (0,)), ((), ())), precision=lax.Precision.HIGHEST, preferred_element_type=F32
    )


def exact_rows(left, right):
    return lax.dot_general(
        left, right, (((1,), (1,)), ((), ())), precision=lax.Precision.HIGHEST, preferred_element_type=F32
    )


def rows(left, right):
    return lax.dot_general(left, right, (((1,), (1,)), ((), ())), preferred_element_type=F32)


def in_hbm(values):
    return pltpu.with_memory_space_constraint(values, pltpu.HBM)


def halves(values):
    high = values.astype(BF16)
    return high, (values - high.astype(F32)).astype(BF16)


def by_owner_kernel(mass, out, held, sems):
    wcap = out.shape[2]
    reads, writes = [], []
    for c in range(out.shape[0]):
        reads.append(pltpu.make_async_copy(mass.at[:, pl.ds(c * wcap, wcap)], held.at[c], sems.at[0, c]))
        writes.append(pltpu.make_async_copy(held.at[c], out.at[c], sems.at[1, c]))
        reads[-1].start()
    for read, write in zip(reads, writes):
        read.wait()
        write.start()
    for write in writes:
        write.wait()


def by_owner(mass, n_col, wcap):
    shape = (n_col, mass.shape[0], wcap)
    return pl.pallas_call(
        by_owner_kernel,
        in_specs=[HBM],
        out_specs=HBM,
        out_shape=pltpu.HBM(shape, BF16),
        scratch_shapes=[pltpu.VMEM(shape, BF16), pltpu.SemaphoreType.DMA((2, n_col))],
        compiler_params=pltpu.CompilerParams(vmem_limit_bytes=LIMIT),
        name="by_owner",
    )(mass)


def combine_kernel(rates, count, rim, wet, slots, start, blocks, mixed, pick, place, halo, values):
    size = blocks.shape[-1]
    for k in range(blocks.shape[2]):
        whole = (
            blocks[0, 0, k].astype(F32)
            + rates[0] * blocks[1, 0, k].astype(F32)
            - rates[1] * blocks[2, 0, k].astype(F32)
        ).T
        mixed[0, k * size : (k + 1) * size] = whole.astype(BF16)

    @pl.when(pl.program_id(0) == 0)
    def _():
        index = lax.broadcasted_iota(jnp.int32, pick.shape, 0)
        pick[...] = jnp.where(index == rim[...], 1.0, 0.0).astype(BF16)
        index = lax.broadcasted_iota(jnp.int32, place.shape, 1)
        place[...] = jnp.where(index == wet[...], 1.0, 0.0).astype(BF16)
        high, low = halves(start[...])
        halo[...] = jnp.dot(high, pick[...], preferred_element_type=F32) + jnp.dot(
            low, pick[...], preferred_element_type=F32
        )
        live = live_slots(count, slots)
        columns = min(start.shape[1], 512)
        total = jnp.zeros(values.shape, F32)
        for first in range(0, start.shape[1], columns):
            picked = chosen(first, (columns, slots.shape[1]), live)
            total = total + jnp.dot(high[:, first : first + columns], picked, preferred_element_type=F32)
        values[...] = total.astype(BF16)


def combine(rates, count, rim, wet, slots, start, blocks):
    _, block_rows, nnz, size, _ = blocks.shape
    vectors, width = start.shape
    whole = lambda shape: pl.BlockSpec(shape, lambda i: (0,) * len(shape))
    return pl.pallas_call(
        combine_kernel,
        grid=(block_rows,),
        in_specs=[
            SMEM,
            SMEM,
            whole(rim.shape),
            whole(wet.shape),
            whole(slots.shape),
            whole(start.shape),
            pl.BlockSpec((3, 1, nnz, size, size), lambda i: (0, i, 0, 0, 0)),
        ],
        out_specs=[
            pl.BlockSpec((1, nnz * size, size), lambda i: (i, 0, 0)),
            whole((width, rim.shape[1])),
            whole((wet.shape[0], width)),
            whole((vectors, rim.shape[1])),
            whole((vectors, slots.shape[1])),
        ],
        out_shape=[
            pltpu.HBM((block_rows, nnz * size, size), BF16),
            jax.ShapeDtypeStruct((width, rim.shape[1]), BF16),
            jax.ShapeDtypeStruct((wet.shape[0], width), BF16),
            jax.ShapeDtypeStruct((vectors, rim.shape[1]), F32),
            jax.ShapeDtypeStruct((vectors, slots.shape[1]), BF16),
        ],
        compiler_params=pltpu.CompilerParams(vmem_limit_bytes=LIMIT),
        name="combine",
    )(rates, count, rim, wet, slots, start, blocks)


def live_slots(count, slots):
    slot = lax.broadcasted_iota(jnp.int32, slots.shape, 1)
    return jnp.where(slot < count[0], slots[...], -1)


def chosen(first, shape, live):
    index = lax.broadcasted_iota(jnp.int32, shape, 0) + first
    return jnp.where(index == live, 1.0, 0.0).astype(BF16)


def start_pressure_kernel(values, mass, part):
    n_col, n_row, _, half, wcap = mass.shape
    size, vectors = n_col * half, values.shape[0]
    for r in range(n_row):
        for h in range(2):
            own = mass[:, r, h].reshape(size, wcap)
            pressed = rows(own, values[...]).astype(BF16)
            part[r * size : (r + 1) * size, h * vectors : (h + 1) * vectors] = pressed


def start_pressure(values, mass):
    n_col, n_row, _, half, _ = mass.shape
    return pl.pallas_call(
        start_pressure_kernel,
        in_specs=[VMEM, VMEM],
        out_specs=VMEM,
        out_shape=jax.ShapeDtypeStruct((n_col * n_row * half, 2 * values.shape[0]), BF16),
        compiler_params=pltpu.CompilerParams(vmem_limit_bytes=LIMIT),
        name="start_pressure",
    )(values, mass)


def spread_kernel(count, slots, mass, spread, own):
    n_col, n_row, _, half, wcap = mass.shape
    size = n_col * half

    @pl.when(pl.program_id(0) == 0)
    def _():
        for h in range(2):
            for r in range(n_row):
                first = (h * n_row + r) * size
                own[first : first + size] = mass[:, r, h].reshape(size, wcap)

    columns = spread.shape[1]
    onehot = chosen(pl.program_id(0) * columns, (columns, wcap), live_slots(count, slots))
    spread[...] = rows(own[...], onehot).astype(BF16)


def spread_mass(count, slots, mass, width):
    n_col, n_row, _, half, wcap = mass.shape
    size = n_col * n_row * half
    columns = min(width, 512)
    return pl.pallas_call(
        spread_kernel,
        grid=(width // columns,),
        in_specs=[
            SMEM,
            pl.BlockSpec(slots.shape, lambda i: (0, 0)),
            pl.BlockSpec(mass.shape, lambda i: (0,) * 5),
        ],
        out_specs=pl.BlockSpec((2 * size, columns), lambda i: (0, i)),
        out_shape=pltpu.HBM((2 * size, width), BF16),
        scratch_shapes=[pltpu.VMEM((2 * size, wcap), BF16)],
        compiler_params=pltpu.CompilerParams(vmem_limit_bytes=LIMIT),
        cost_estimate=pl.CostEstimate(
            flops=4 * size * wcap * width, bytes_accessed=4 * size * width, transcendentals=0
        ),
        name="spread",
    )(count, slots, mass)


def pivot_rows(top, s):
    lanes = top[0].shape[1]
    at = lambda i, j: jnp.broadcast_to(top[i][:, s + j : s + j + 1], (1, lanes))
    a, b, c = at(0, 0), at(0, 1), at(1, 1)
    p2, q2, p3, q3 = at(2, 0), at(2, 1), at(3, 0), at(3, 1)
    d22, d23, d33 = at(2, 2), at(2, 3), at(3, 3)
    scale = 1.0 / (a * c - b * b)
    first = ((c * top[0] - b * top[1]) * scale, (a * top[1] - b * top[0]) * scale)
    y02, y03 = (c * p2 - b * q2) * scale, (c * p3 - b * q3) * scale
    y12, y13 = (a * q2 - b * p2) * scale, (a * q3 - b * p3) * scale
    a2 = d22 - p2 * y02 - q2 * y12
    b2 = d23 - p2 * y03 - q2 * y13
    c2 = d33 - p3 * y03 - q3 * y13
    scale2 = 1.0 / (a2 * c2 - b2 * b2)
    third = top[2] - p2 * first[0] - q2 * first[1]
    fourth = top[3] - p3 * first[0] - q3 * first[1]
    v2 = (c2 * third - b2 * fourth) * scale2
    v3 = (a2 * fourth - b2 * third) * scale2
    v0 = first[0] - y02 * v2 - y03 * v3
    v1 = first[1] - y12 * v2 - y13 * v3
    return first, (v0, v1, v2, v3)


def eliminate_four(work, s, j, keep):
    sub = lax.broadcasted_iota(jnp.int32, (8, 1), 0)
    first, full = pivot_rows([work[0][s + k : s + k + 1, :] for k in range(4)], j)
    out = []
    for i, group in enumerate(work):
        columns = [group[:, j + k : j + k + 1] for k in range(4)]
        half = columns[0] * full[0] + columns[1] * full[1]
        update = half + (columns[2] * full[2] + columns[3] * full[3])
        if i == 0:
            pair = columns[0] * first[0] + columns[1] * first[1]
            update = jnp.where(sub > s + 3, update, jnp.where(sub > s + 1, pair, 0.0))
        elif keep is not None:
            update = jnp.where(keep(i), update, 0.0)
        out.append(group - update)
    return out


def eliminate(matrix, beside, coef, factor_t):
    n = matrix.shape[0]
    groups = n // 8
    row_id = lax.broadcasted_iota(jnp.int32, (n, 2 * n), 0)
    lane_id = lax.broadcasted_iota(jnp.int32, (n, 2 * n), 1)
    factor_t[...] = jnp.where(row_id + n == lane_id, 1.0, 0.0)
    factor_t[:, :n] = matrix
    if beside:
        work = [factor_t[g * 8 : (g + 1) * 8, :] for g in range(groups)]
        done = 0
        for j in range(0, n, 4):
            g, s = divmod(j, 8)
            work[g:] = eliminate_four(work[g:], s, j, None)
            goal = len(beside) * (j + 4) // n
            while done < goal:
                beside[done]()
                done += 1
        reduced = jnp.concatenate(work, 0)
    else:

        def group(step, _):
            work = [factor_t[g * 8 : (g + 1) * 8, :] for g in range(groups)]
            for s in range(0, 8, 4):
                work = eliminate_four(work, s, s, lambda i: step + i < groups)
            for i in range(groups):
                target = (i - 1) % groups
                factor_t[target * 8 : (target + 1) * 8, :] = pltpu.roll(work[i], 2 * n - 8, 1)
            return 0

        lax.fori_loop(0, groups, group, 0)
        reduced = pltpu.roll(factor_t[...], n, 1)
    above = pltpu.roll(reduced, 1, 0)
    odd = lax.broadcasted_iota(jnp.int32, (n, 1), 0) % 2 == 1
    pick = lambda values, where: jnp.sum(jnp.where(where, values, 0.0), 1, keepdims=True)
    under = pick(above, lane_id == row_id) / jnp.where(odd, pick(above, lane_id + 1 == row_id), 1.0)
    reduced = reduced - jnp.where(odd, under, 0.0) * above
    diagonal = pick(reduced, lane_id == row_id)
    scale = lax.rsqrt(diagonal)
    scale = scale * (1.5 - 0.5 * diagonal * scale * scale)
    reduced = reduced * scale
    factor_t[...] = reduced
    upper = jnp.where(row_id <= lane_id, reduced, 0.0)
    coef[2] = upper.T[:n, :]
    return factor_t[:, n:]


def congruent(factor, matrix):
    return exact(factor, exact_rows(matrix, factor))


def settle(total, gram, inner, lag, both, beside, coef, factor_t):
    n = gram.shape[0] // 2
    scale = 1.0 / total
    pull = lag[:, :n]
    aa = congruent(pull, gram[:n, :n] * scale)
    cc = congruent(pull, gram[n:, n:] * scale)
    self_ = both[:, :n]
    prev = both[:, n:]
    cp = inner[:, :n]
    pp = inner[:, n:]
    coef[0] = self_
    coef[1] = prev
    t_c = self_ - exact(self_, cc) - exact_rows(prev, cp)
    t_p = prev - exact(self_, cp) - exact(prev, pp)
    t_a = aa - exact_rows(self_, self_) - exact_rows(prev, prev)
    matrix = t_a - exact_rows(t_c, self_) - exact_rows(t_p, prev)
    inverse = eliminate(0.5 * (matrix + matrix.T), beside, coef, factor_t)
    return inverse, t_c, cc


def put_weights(weights, mix, pull):
    n = mix.shape[0]
    high, low = halves(mix)
    pull_high, pull_low = halves(pull)
    for k in range(3):
        cut = slice(k * n, (k + 1) * n)
        weights[:n, 2 * k * n : (2 * k + 1) * n] = high[:, cut]
        weights[:n, (2 * k + 1) * n : (2 * k + 2) * n] = high[:, cut]
        weights[n : 2 * n, 2 * k * n : (2 * k + 1) * n] = low[:, cut]
        weights[n : 2 * n, (2 * k + 1) * n : (2 * k + 2) * n] = jnp.zeros((n, n), BF16)
    if weights.shape[0] > 2 * n:
        weights[2 * n :, :] = jnp.zeros((2 * n, 6 * n), BF16)
        weights[2 * n : 3 * n, 2 * n : 3 * n] = pull_high
        weights[2 * n : 3 * n, 3 * n : 4 * n] = pull_high
        weights[3 * n :, 2 * n : 3 * n] = pull_low


def blend(total, gram, lag, both, mix):
    n = gram.shape[0] // 2
    scale = 1.0 / total
    pull, square = lag[:, :n], lag[:, n:]
    crossed = gram[:n, n:] * scale
    prev = exact(pull, gram[n:, :n] * scale)
    mix[:, :n] = pull
    mix[:, n : 2 * n] = -exact(pull, exact(crossed, square))
    mix[:, 2 * n :] = -prev
    both[:, :n] = congruent(pull, crossed)
    both[:, n:] = prev


def factor_kernel(total, gram, inner, lag, both, lag_out, inner_out, coef, factor_t):
    n = gram.shape[0] // 2
    inverse, t_c, cc = settle(total, gram, inner, lag, both, [], coef, factor_t)
    lag_out[:, :n] = inverse
    lag_out[:, n:] = exact(inverse.T, inverse)
    inner_out[:, :n] = exact(inverse, t_c)
    inner_out[:, n:] = cc


def factor(total, gram, inner, lag, both):
    n = gram.shape[0] // 2
    sds = jax.ShapeDtypeStruct
    return pl.pallas_call(
        functools.partial(factor_kernel, total),
        in_specs=[VMEM] * 4,
        out_specs=[VMEM] * 3,
        out_shape=[sds((n, 2 * n), F32), sds((n, 2 * n), F32), sds((3, n, n), F32)],
        scratch_shapes=[pltpu.VMEM((n, 2 * n), F32)],
        compiler_params=pltpu.CompilerParams(vmem_limit_bytes=LIMIT),
        cost_estimate=pl.CostEstimate(flops=100_000_000, bytes_accessed=10_000_000, transcendentals=0),
        name="factor",
    )(gram, inner, lag, both)


def thirds(values):
    high = values.astype(BF16)
    rest = values - high.astype(F32)
    return jnp.concatenate([high, *halves(rest)], 0)


def unpack(lines, received, target, lanes, offset):
    for s in range(received.shape[0]):
        if s * lines < target.shape[0]:
            target[s * lines : (s + 1) * lines, lanes] = received[s, offset : offset + lines]


def place_columns(extended, block, edge):
    size = extended.shape[2]
    count = extended.shape[0] - 2
    for i in range(count):
        extended[i] = block[:, i * size : (i + 1) * size]
    extended[count] = edge[:, :size].astype(BF16)
    extended[count + 1] = edge[:, size:].astype(BF16)


def block_row(ids, extended, mixed, i):
    picked = jnp.concatenate([extended[ids[i, k]] for k in range(ids.shape[1])], 1)
    return jnp.dot(picked, mixed[i], preferred_element_type=F32)


def advance_kernel(mode, total, peers, *refs):
    it = iter(refs)
    take = lambda k: [next(it) for _ in range(k)]
    ids, rates = take(2)
    if mode == "first":
        arrived, below, above = take(3)
    else:
        received, pressed, lag, edges, wet_held = take(5)
    (held,) = take(1)
    pick, place, mixed_in, spread_in = take(4)
    (state_out,) = take(1)
    if mode == "last":
        (gram_s,) = take(1)
    else:
        edges_out, wet_out, send = take(3)
    if mode != "first":
        both, gram_in = take(2)
    extended, terms, stack, mixed, spread, edge_in, sems = take(7)
    if mode != "last":
        gram_s, rest = take(2)
    if mode != "first":
        mix, weights = take(2)

    n = terms.shape[0] // 6
    width = terms.shape[1]
    size = edge_in.shape[1] // 2
    count = width // size
    glines = -(-2 * n // peers)
    hlines = -(-n // peers)
    load = pltpu.make_async_copy(held, stack, sems.at[0])
    load.start()
    load_mixed = pltpu.make_async_copy(mixed_in, mixed, sems.at[1])
    load_mixed.start()
    load_spread = []
    if mode != "last":
        for h in range(2):
            part = spread_in.at[pl.ds(h * spread.shape[1], spread.shape[1])]
            load_spread.append(pltpu.make_async_copy(part, spread.at[h], sems.at[3 + h]))

    if mode == "first":
        edge = jnp.concatenate([below[...], above[...]], 1)
        summed = jnp.sum(arrived[...].astype(F32), 0)
        wet = jnp.concatenate([summed[:, :n], summed[:, n:]], 0)
        edges_out[:n, :] = edge
        edges_out[n:, :] = jnp.zeros_like(edge)
        wet_out[:, :n] = wet
        wet_out[:, n:] = jnp.zeros_like(wet)
        load.wait()
        for copy in load_spread:
            copy.start()
        residual = stack[...]
        terms[4 * n :, :] = jnp.zeros((2 * n, width), BF16)
    else:
        unpack(glines, received, gram_in, slice(None), 0)
        unpack(hlines, received, edge_in.at[pl.ds(0, n)], slice(0, size), glines)
        unpack(hlines, received, edge_in.at[pl.ds(0, n)], slice(size, 2 * size), glines + hlines)
        edge_in[n:, :] = edges[...]
        blend(total, gram_in, lag, both, mix)
        pull = lag[:, :n]
        put_weights(weights, mix[...], pull)
        edge = exact(mix[...], edge_in[...])
        summed = pressed[...]
        wet = exact_rows(jnp.concatenate([summed[:, :n], summed[:, n:]], 0), pull)
        wet = wet + exact_rows(wet_held[...], mix[:, n:])
        if mode != "last":
            edges_out[:n, :] = edge
            edges_out[n:, :] = exact(pull, edges[:n, :])
            wet_out[:, :n] = wet
            wet_out[:, n:] = exact_rows(wet_held[:, :n], pull)
        load.wait()
        for copy in load_spread:
            copy.start()
        mixture = jnp.dot(weights[...], stack[...], preferred_element_type=F32)
        residual = mixture[:n] + mixture[n : 2 * n]
        terms[4 * n : 5 * n, :], terms[5 * n :, :] = halves(mixture[2 * n : 3 * n] + mixture[3 * n :])
    high, low = halves(residual)
    terms[2 * n : 3 * n, :] = high
    terms[3 * n : 4 * n, :] = low
    force = thirds(wet.T * rates[1])
    place_columns(extended, high, edge)
    load_mixed.wait()
    for i in range(count):
        lanes = slice(i * size, (i + 1) * size)
        added = jnp.dot(force, place[:, lanes], preferred_element_type=F32)
        applied = block_row(ids, extended, mixed, i) - (added[:n] + added[n : 2 * n] + added[2 * n :])
        terms[:n, lanes], terms[n : 2 * n, lanes] = halves(applied)
    store = pltpu.make_async_copy(terms, state_out, sems.at[2])
    store.start()

    known = 4 * n if mode == "first" else 6 * n
    products = rows(terms[: 2 * n, :], terms[:known, :])
    products = products[:n] + products[n:]
    gram_s[:n, :n] = products[:, :n] + products[:, n : 2 * n]
    gram_s[:n, n:] = products[:, 2 * n : 3 * n] + products[:, 3 * n : 4 * n]
    if mode == "first":
        gram_s[n:, :n] = jnp.zeros((n, n), F32)
    else:
        gram_s[n:, :n] = products[:, 4 * n : 5 * n] + products[:, 5 * n :]
    squares = rows(terms[2 * n : 4 * n, :], terms[2 * n : 4 * n, :])
    squares = squares[:n] + squares[n:]
    gram_s[n:, n:] = squares[:, :n] + squares[:, n:]
    if mode != "last":
        rim = jnp.dot(terms[: 2 * n, :], pick[...], preferred_element_type=F32)
        edge_in[:n, :size] = rim[:n] + rim[n:]
        wets = wet_out.shape[0] // 2
        for copy in load_spread:
            copy.wait()
        tops = rows(spread[0], terms[: 2 * n, :])
        tops = tops + pltpu.roll(tops, n, 1)
        ends = rows(spread[1], terms[: 2 * n, :])
        ends = ends + pltpu.roll(ends, n, 1)
        lane = lax.broadcasted_iota(jnp.int32, tops.shape, 1)
        send[:, :wets, :] = jnp.where(lane < n, tops, ends).astype(BF16).reshape(peers, wets, 2 * n)
        left = gram_s[...]
        offset = 0
        for _ in range(3):
            term = left.astype(BF16).astype(F32)
            left = left - term
            gram_s[...] = term
            for d in range(peers):
                if d * glines < 2 * n:
                    rest[d, offset : offset + glines] = gram_s[d * glines : (d + 1) * glines, :]
            offset += glines
        left = edge_in[:n, :size]
        for _ in range(2):
            term = left.astype(BF16).astype(F32)
            left = left - term
            edge_in[:n, :size] = term
            for d in range(peers):
                if d * hlines < n:
                    rest[d, offset : offset + hlines] = edge_in[d * hlines : (d + 1) * hlines, :size]
                else:
                    rest[d, offset : offset + hlines] = jnp.zeros((hlines, size), F32)
            offset += hlines
        if offset < rest.shape[1]:
            rest[:, offset:, :] = jnp.zeros((peers, rest.shape[1] - offset, 2 * n), F32)
        send[:, wets:, :] = rest[...].astype(BF16)
    store.wait()


def advance(mode, total, peers, ids, rates, state, fixed):
    mixed, pick, place, spread = fixed
    width, size = pick.shape
    wets = place.shape[0]
    vectors = state[3].shape[0] if mode == "first" else state[2].shape[0]
    extra = 3 * -(-2 * vectors // peers) + 2 * -(-vectors // peers)
    extra = -(-extra // 16) * 16
    sds = jax.ShapeDtypeStruct
    block = pltpu.HBM((6 * vectors, width), BF16)
    small = sds((2 * vectors, 2 * vectors), F32)
    shapes, specs = [block], [HBM]
    if mode == "last":
        shapes += [small]
        specs += [VMEM]
    else:
        shapes += [
            sds((2 * vectors, 2 * size), F32),
            sds((wets, 2 * vectors), F32),
            sds((peers, wets // 2 + extra, 2 * vectors), BF16),
        ]
        specs += [VMEM] * 3
    if mode != "first":
        shapes += [sds((vectors, 2 * vectors), F32), small]
        specs += [VMEM, VMEM]
    scratch = [
        pltpu.VMEM((width // size + 2, vectors, size), BF16),
        pltpu.VMEM((6 * vectors, width), BF16),
        pltpu.VMEM((vectors, width), F32) if mode == "first" else pltpu.VMEM((6 * vectors, width), BF16),
        pltpu.VMEM(mixed.shape, BF16),
        pltpu.VMEM((2, spread.shape[0] // 2, spread.shape[1]) if mode != "last" else (16, 128), BF16),
        pltpu.VMEM((3 * vectors, 2 * size), F32),
        pltpu.SemaphoreType.DMA((5,)),
    ]
    if mode != "last":
        scratch += [pltpu.VMEM(small.shape, F32), pltpu.VMEM((peers, extra, 2 * vectors), F32)]
    if mode != "first":
        scratch += [pltpu.VMEM((vectors, 3 * vectors), F32), pltpu.VMEM((4 * vectors, 6 * vectors), BF16)]
    return pl.pallas_call(
        functools.partial(advance_kernel, mode, total, peers),
        in_specs=[SMEM, SMEM] + [VMEM] * (len(state) - 1) + [HBM, VMEM, VMEM, HBM, HBM],
        out_specs=specs,
        out_shape=shapes,
        scratch_shapes=scratch,
        compiler_params=pltpu.CompilerParams(vmem_limit_bytes=LIMIT),
        name="advance_" + mode,
    )(ids, rates, *state, pick, place, mixed, spread)


def route_kernel(vectors, wets, received, _lag, pressed, send, rest):
    peers = received.shape[0]
    glines = -(-2 * vectors // peers)
    hlines = -(-vectors // peers)
    pressed[...] = jnp.sum(received[:, :wets, :].astype(F32), 0)
    rest[...] = received[:, wets:, :].astype(F32)
    sums = jnp.sum(rest[...], 0)
    mine = sums[:glines] + sums[glines : 2 * glines] + sums[2 * glines : 3 * glines]
    edge = 3 * glines
    nothing = jnp.zeros((hlines, 2 * vectors), F32)

    def halo(t):
        if not 0 <= t < peers:
            return nothing
        return rest[t, edge : edge + hlines] + rest[t, edge + hlines : edge + 2 * hlines]

    send[...] = jnp.zeros(send.shape, F32)
    for t in range(peers):
        send[t, :glines] = mine
        send[t, glines : glines + hlines] = halo(t - 1)
        send[t, glines + hlines : glines + 2 * hlines] = halo(t + 1)


def route(vectors, wets, received, lag):
    peers, lines, lanes = received.shape
    return pl.pallas_call(
        functools.partial(route_kernel, vectors, wets),
        in_specs=[VMEM, VMEM],
        out_specs=[VMEM] * 2,
        out_shape=[
            jax.ShapeDtypeStruct((wets, 2 * vectors), F32),
            jax.ShapeDtypeStruct((peers, 8, 2 * vectors), F32),
        ],
        scratch_shapes=[pltpu.VMEM((peers, lines - wets, lanes), F32)],
        compiler_params=pltpu.CompilerParams(vmem_limit_bytes=LIMIT),
        name="route",
    )(received, lag)


def repeat_sum_kernel(received, _lag, send):
    mine = jnp.sum(received[...], 0)
    for t in range(send.shape[0]):
        send[t] = mine


def repeat_sum(received, lag):
    return pl.pallas_call(
        repeat_sum_kernel,
        in_specs=[VMEM, VMEM],
        out_specs=VMEM,
        out_shape=jax.ShapeDtypeStruct(received.shape, F32),
        compiler_params=pltpu.CompilerParams(vmem_limit_bytes=LIMIT),
        name="repeat_sum",
    )(received, lag)


def finish_kernel(total, gram, inner, lag, state, *refs):
    *earlier, out, coefs, factor_t, mix, weights, both, stack, fresh, sem = refs
    coef = coefs.at[len(earlier)]
    n = inner.shape[0]
    load = pltpu.make_async_copy(state, stack, sem)
    load.start()
    blend(total, gram, lag, both, mix)
    for k, known in enumerate(earlier):
        coefs[k] = known[...]
    put_weights(weights, mix[...], lag[:, :n])
    load.wait()

    def next_residual():
        mixture = jnp.dot(weights[...], stack[...], preferred_element_type=F32)
        fresh[...] = mixture[:n] + mixture[n:]

    inverse, _, _ = settle(total, gram, inner, lag, both, [next_residual], coef, factor_t)
    out[...] = exact(inverse, fresh[...])


def finish(total, gram, inner, lag, state, earlier):
    vectors, width = lag.shape[0], state.shape[1]
    return pl.pallas_call(
        functools.partial(finish_kernel, total),
        in_specs=[VMEM] * 3 + [HBM] + [VMEM] * len(earlier),
        out_specs=[VMEM] * 2,
        out_shape=[
            pltpu.HBM((vectors, width), F32),
            pltpu.HBM((len(earlier) + 1, 3, vectors, vectors), F32),
        ],
        scratch_shapes=[
            pltpu.VMEM((vectors, 2 * vectors), F32),
            pltpu.VMEM((vectors, 3 * vectors), F32),
            pltpu.VMEM((2 * vectors, 6 * vectors), BF16),
            pltpu.VMEM((vectors, 2 * vectors), F32),
            pltpu.VMEM((6 * vectors, width), BF16),
            pltpu.VMEM((vectors, width), F32),
            pltpu.SemaphoreType.DMA,
        ],
        compiler_params=pltpu.CompilerParams(vmem_limit_bytes=LIMIT),
        name="finish",
    )(gram, inner, lag, state, *earlier)


def local(n_row, n_col, start_block, struct_blocks, block_ids, rim_rows, wet_slots, wet_counts, added_mass, rates):
    peers = n_row * n_col
    vectors, width = start_block.shape
    total = float(width * peers)
    wcap = wet_slots.shape[0]
    wets = added_mass.shape[0] // n_row

    def exchange(parts):
        return lax.all_to_all(parts, AXES, 0, 0, tiled=True)

    def neighbours(halo):
        up = [(i, i + 1) for i in range(peers - 1)]
        down = [(i + 1, i) for i in range(peers - 1)]
        return lax.ppermute(halo, AXES, up), lax.ppermute(halo, AXES, down)

    def summed(gram, lag):
        lines = gram.shape[0] // peers
        return exchange(repeat_sum(exchange(gram.reshape(peers, lines, -1)), lag)).reshape(gram.shape)

    blocks = by_owner(in_hbm(added_mass), n_col, wcap)
    mass = lax.all_to_all(blocks, "col", 0, 0, tiled=True)
    mass = mass.reshape(n_col, n_row, 2, wets // 2, wcap)
    slots = wet_slots[None, :]
    mixed, pick, place, halo, values = combine(
        rates, wet_counts, rim_rows[None, :], wet_slots[:wets, None], slots, start_block, struct_blocks
    )
    below, above = neighbours(halo)
    part = start_pressure(values, mass)
    spread = spread_mass(wet_counts, slots, mass, width)
    fixed = (in_hbm(mixed), pick, place, in_hbm(spread))
    arrived = exchange(part.reshape(peers, wets // 2, 2 * vectors))
    step = functools.partial(advance, total=total, peers=peers, ids=block_ids, rates=rates, fixed=fixed)
    state, edges, wet_held, send = step("first", state=(arrived, below, above, in_hbm(start_block)))
    inner = jnp.zeros((vectors, 2 * vectors), F32)
    unit = jnp.eye(vectors, dtype=F32)
    lag = jnp.concatenate([unit, unit], 1)
    coefficients = []
    for number in range(1, STEPS):
        pressed, again = route(vectors, wets // 2, exchange(send), lag)
        received = exchange(again)
        known = (received, pressed, lag, edges, wet_held, in_hbm(state))
        if number < STEPS - 1:
            state, edges, wet_held, send, both, gram = step("mid", state=known)
        else:
            state, products, both, gram = step("last", state=known)
        lag, inner, coef = factor(total, gram, inner, lag, both)
        coefficients.append(coef)
    final, coefs = finish(total, summed(products, lag), inner, lag, in_hbm(state), coefficients)
    return final, coefs


def solution(mesh):
    return jax.shard_map(
        functools.partial(local, mesh.shape["row"], mesh.shape["col"]),
        mesh=mesh,
        in_specs=(
            P(None, AXES),
            P(None, AXES, None, None, None),
            P(AXES, None),
            P(AXES),
            P(AXES),
            P(AXES),
            P("col", "row"),
            P(),
        ),
        out_specs=(P(None, AXES), P()),
        check_vma=False,
    )
```
